32 devices in a mesh: dp: 4 (over y, x), expert: 8 (over z, core).
Axes of the slice: x: 2, y: 2, z: 4, core: 2. Of those that a mesh axis runs over, the one named last changes fastest.
Arguments:
- hidden: bfloat16 [16384, 1024], P(('dp', 'expert')), may hold values from -6 to 6
- segment_ids: int32 [32, 512], P(('dp', 'expert')), may hold values from 0 to 3, never falling along the last dimension, each value on 1 to 256 neighbouring positions
- routes: int32 [16384, 8], P(('dp', 'expert')), may hold values from 0 to 31, all different within a row; in each aligned block of 512 rows (0 to 511, 512 to 1023, ...) at most 192 rows name the same one
- norm_attn: bfloat16 [1024], P('expert'), may hold values from 0.5 to 1.5
- w_query: bfloat16 [1024, 1024], P('expert'), may hold values from -0.1875 to 0.1875
- key_weight: bfloat16 [1024, 512], P('expert'), may hold values from -0.1875 to 0.1875
- value_weight: bfloat16 [1024, 512], P('expert'), may hold values from -0.1875 to 0.1875
- w_out: bfloat16 [1024, 1024], P('expert'), may hold values from -0.75 to 0.75
- norm_moe: bfloat16 [1024], P('expert'), may hold values from 0.5 to 1.5
- w_router: bfloat16 [1024, 32], P('expert'), may hold values from -0.09375 to 0.09375
- w_gate: bfloat16 [32, 1024, 512], P('expert'), may hold values from -0.1875 to 0.1875
- w_up: bfloat16 [32, 1024, 512], P('expert'), may hold values from -0.1875 to 0.1875
- w_down: bfloat16 [32, 512, 1024], P('expert'), may hold values from -1 to 1
- cotangent: bfloat16 [16384, 1024], P(('dp', 'expert')), may hold values from -6 to 6
Outputs:
- output: bfloat16 [16384, 1024], P(('dp', 'expert'))
- grad_input: bfloat16 [16384, 1024], P(('dp', 'expert'))
- grad_norm_attn: float32 [1024], P('expert')
- grad_query: float32 [1024, 1024], P('expert')
- grad_key: float32 [1024, 512], P('expert')
- grad_value: float32 [1024, 512], P('expert')
- grad_out: float32 [1024, 1024], P('expert')
- grad_norm_moe: float32 [1024], P('expert')
- grad_router: float32 [1024, 32], P('expert')
- grad_gate: float32 [32, 1024, 512], P('expert')
- grad_up: float32 [32, 1024, 512], P('expert')
- grad_down: float32 [32, 512, 1024], P('expert')
The draws below stay inside these ranges and needn't reach their ends.
Inputs may be any that keep to these rules, and one draw needn't show every extreme that they name: `segment_ids`: along each row the document numbers never fall; every document has 1 to half of the 512 tokens, and some has exactly that many. `routes`: each token names 8 different experts. Among the 512 tokens of one sequence no expert is named more than 192 times, and in some sequences one expert is named exactly 192 times.
All inputs are finite; a program needn't handle non-finite values.
Results may differ from the reference program's by a relative error of at most 0.022.
Values may be sent and summed in bfloat16 or wider, within the bound.
No kernel may reach another device: no remote copies, remote signals or barrier semaphores. Data moves between devices by JAX's collectives and lax.ppermute only.
A program may use at most 320 MiB of HBM per device.

```python
import math
import jax
import jax.numpy as jnp
import numpy as np
from jax import lax

MODEL_DIMENSION = 1024
QUERY_HEADS = 16
KEY_VALUE_HEADS = 8
HEAD_SIZE = 64
F = 512
EXPERTS = 32
TOP = 8
TOK_DEV = 512
SEGS = 4
CAP = 192
SEQS = 32
TOKENS = 16384


def levels(rng, dims, split, least, largest):
    loudness = 1.0
    for dim, shards_of in split:
        heights = jax.random.uniform(jax.random.fold_in(jax.random.fold_in(rng, 6), dim), (shards_of,), jnp.float32, least / len(split), largest / len(split))
        loudness = loudness * jnp.repeat(jnp.exp(heights), dims[dim] // shards_of).reshape((-1,) + (1,) * (len(dims) - 1 - dim))
    return loudness


def length_profile(number_of, total, limit, slope):
    weights = [(1 << 20) // math.isqrt(rank ** slope) + 1 for rank in range(2, number_of + 1)]
    surplus, counts = total - limit - (number_of - 1), [1] * (number_of - 1)
    while surplus > 0:
        free = [i for i in range(number_of - 1) if counts[i] < limit]
        mass, budget = sum([weights[i] for i in free]), surplus
        for i in free:
            addition = min(limit - counts[i], max(1, budget * weights[i] // mass), surplus)
            counts[i] = counts[i] + addition
            surplus = surplus - addition
    return np.array([limit] + counts)


def uneven_parts(own_key, amount, total, most, slope):
    if amount == 2:
        one = jax.random.randint(own_key, (), max(1, total - most), min(most, total - 1) + 1)
        return jnp.stack([one, total - one])
    lengths = jnp.asarray(length_profile(amount, total, most, slope), jnp.int32)
    couples = (amount - 1) // 2
    source_of, taker = lengths[1:1 + 2 * couples:2], lengths[2:2 + 2 * couples:2]
    margin = jnp.minimum(source_of - 1, most - taker)
    passed = jax.random.randint(jax.random.fold_in(own_key, 1), (couples,), 0, 1 << 20) % (margin + 1)
    lengths = lengths.at[1:1 + 2 * couples:2].set(source_of - passed).at[2:2 + 2 * couples:2].set(taker + passed)
    return lengths[jax.random.permutation(jax.random.fold_in(own_key, 2), amount)]


def routed_block(stream_key, own, number, rows, number_of, top, most, lean):
    ranking = jax.random.permutation(stream_key, number_of)
    packed, ordinary = portions_of(number_of, rows * top, most, lean, True), portions_of(number_of, rows * top, most, lean, False)
    places = jnp.arange(number_of)

    def named(sizes, turn):
        used = int((sizes > 0).sum())
        fixed = max(1, used // 4)
        passed = fixed + (places - fixed + turn * (used - fixed)) % max(1, number_of - fixed)
        return jnp.zeros((number_of,), jnp.int32).at[ranking[jnp.where(places < fixed, places, passed)]].set(jnp.asarray(sizes, jnp.int32))

    sizes = jnp.where(number % 4 == 0, named(packed, number // 4), named(ordinary, number - number // 4 - 1))
    mixed = jax.random.permutation(jax.random.fold_in(own, 3), number_of)
    giver, sink = mixed[0:number_of // 2 * 2:2], mixed[1:number_of // 2 * 2:2]
    slack = jnp.minimum(sizes[giver] - 1, most - sizes[sink]) // 2
    slack = jnp.where((giver == ranking[0]) | (sink == ranking[0]) | (sizes[sink] == 0), 0, jnp.maximum(slack, 0))
    passed = jax.random.randint(jax.random.fold_in(own, 4), (number_of // 2,), 0, 1 << 20) % (slack + 1)
    sizes = sizes.at[giver].add(-passed).at[sink].add(passed)
    members = jnp.searchsorted(jnp.cumsum(sizes), jnp.arange(rows * top), side="right").astype(jnp.int32)
    grid = members.reshape(top, rows).T
    grid = grid[jax.random.permutation(jax.random.fold_in(own, 1), rows)]
    turn = jax.random.randint(jax.random.fold_in(own, 2), (rows, 1), 0, top)
    return jnp.take_along_axis(grid, (jnp.arange(top)[None, :] + turn) % top, axis=1)


def portions_of(count, total, most, skew, full):
    loads = [(1 << 20) // math.isqrt(rank ** skew) + 1 for rank in range(1, count + 1)]
    largest = most if full else min(most, max(-(-total // count), total * loads[0] // sum(loads)))
    least = 1 if total - largest >= count - 1 else 0
    given, spare = [largest] + [least] * (count - 1), total - largest - least * (count - 1)
    while spare > 0:
        candidates = [i for i in range(1, count) if given[i] < largest] or [i for i in range(1, count) if given[i] < most]
        mass, budget = sum([loads[i] for i in candidates]), spare
        for i in candidates:
            extra = min(most - given[i], max(1, budget * loads[i] // mass), spare)
            given[i] = given[i] + extra
            spare = spare - extra
    return np.array(given)


def centred(stream_key, shape, spread, reach, cuts=(), held_as=jnp.bfloat16):
    gain = levels(stream_key, shape, cuts, -0.22, 0.18) if cuts else 1.0
    values = jax.random.normal(stream_key, shape, jnp.float32) * spread * gain
    return jnp.minimum(jnp.maximum(values, -reach), reach).astype(held_as)


def setup_inputs(seed: int = 0) -> dict:
    key_list = jax.random.split(jax.random.key(seed), 15)
    hidden = centred(key_list[0], (TOKENS, MODEL_DIMENSION), 1.0, 6.0, ((0, 32),))
    segment_ids = jax.vmap(lambda own: jnp.searchsorted(jnp.cumsum(uneven_parts(own, SEGS, TOK_DEV, TOK_DEV // 2, 2)), jnp.arange(TOK_DEV), side="right"))(jax.random.split(key_list[1], SEQS)).reshape((SEQS, TOK_DEV)).astype(jnp.int32)
    routes_keys = jax.random.split(jax.random.fold_in(key_list[2], 1), TOKENS // TOK_DEV)
    routes_turns = jax.random.permutation(jax.random.fold_in(key_list[2], 3), TOKENS // TOK_DEV)
    routes = jax.vmap(lambda own, number: routed_block(jax.random.fold_in(key_list[2], 2), own, number, TOK_DEV, EXPERTS, TOP, CAP, 2))(routes_keys, routes_turns).reshape((TOKENS, TOP))
    norm_attn = jnp.clip(1.0 + 0.1 * jax.random.normal(key_list[3], (MODEL_DIMENSION,), jnp.float32), 0.5, 1.5).astype(jnp.bfloat16)
    w_query = centred(key_list[4], (MODEL_DIMENSION, QUERY_HEADS * HEAD_SIZE), MODEL_DIMENSION ** -0.5, 0.1875, ((0, 8),))
    key_weight = centred(key_list[5], (MODEL_DIMENSION, KEY_VALUE_HEADS * HEAD_SIZE), MODEL_DIMENSION ** -0.5, 0.1875, ((0, 8),))
    value_weight = centred(key_list[6], (MODEL_DIMENSION, KEY_VALUE_HEADS * HEAD_SIZE), MODEL_DIMENSION ** -0.5, 0.1875, ((0, 8),))
    w_out = centred(key_list[7], (QUERY_HEADS * HEAD_SIZE, MODEL_DIMENSION), (QUERY_HEADS * HEAD_SIZE // 16) ** -0.5, 0.75, ((0, 8),))
    norm_moe = jnp.clip(1.0 + 0.1 * jax.random.normal(key_list[8], (MODEL_DIMENSION,), jnp.float32), 0.5, 1.5).astype(jnp.bfloat16)
    w_router = centred(key_list[9], (MODEL_DIMENSION, EXPERTS), (4 * MODEL_DIMENSION) ** -0.5, 0.09375, ((0, 8),))
    w_gate = centred(key_list[10], (EXPERTS, MODEL_DIMENSION, F), MODEL_DIMENSION ** -0.5, 0.1875, ((0, 8),))
    w_up = centred(key_list[11], (EXPERTS, MODEL_DIMENSION, F), MODEL_DIMENSION ** -0.5, 0.1875, ((0, 8),))
    w_down = centred(key_list[12], (EXPERTS, F, MODEL_DIMENSION), (F // 16) ** -0.5, 1.0, ((0, 8),))
    cotangent = centred(key_list[13], (TOKENS, MODEL_DIMENSION), 1.0, 6.0, ((0, 32),))
    return {"hidden": hidden, "segment_ids": segment_ids, "routes": routes, "norm_attn": norm_attn, "w_query": w_query, "key_weight": key_weight, "value_weight": value_weight, "w_out": w_out, "norm_moe": norm_moe, "w_router": w_router, "w_gate": w_gate, "w_up": w_up, "w_down": w_down, "cotangent": cotangent}


norm_eps = 1e-06
rope_base = 10000.0
masked_score = -1e+30
highest_precision = lax.Precision.HIGHEST

@jax.custom_vjp
def lower_precision(v):
    return lax.optimization_barrier(v.astype(jnp.bfloat16)).astype(jnp.float32)

@jax.custom_vjp
def lower_backward(v):
    return v

def low_keep(v):
    return (lower_precision(v), None)

def low_pass(kept, grad):
    return (grad,)

def back_keep(v):
    return (v, None)

def back_low(kept, grad):
    return (lower_precision(grad),)
lower_precision.defvjp(low_keep, low_pass)
lower_backward.defvjp(back_keep, back_low)

def positions_of(segment_row):
    sequence_length = segment_row.shape[0]
    row_index = jnp.arange(sequence_length, dtype=jnp.int32)
    previous = jnp.concatenate([jnp.full((1,), -1, jnp.int32), segment_row[:-1].astype(jnp.int32)])
    starts = lax.cummax(jnp.where(segment_row != previous, row_index, 0).astype(jnp.int32), axis=0)
    return (row_index - starts).astype(jnp.int32)

def rope_tables(segment_row):
    position = positions_of(segment_row).astype(jnp.float32)
    half_size = HEAD_SIZE // 2
    frequency = rope_base ** (-jnp.arange(half_size, dtype=jnp.float32) / half_size)
    angles = position[:, None] * frequency[None, :]
    cosine_table = jnp.cos(angles)
    sine_lookup = jnp.sin(angles)
    return (jnp.concatenate([cosine_table, cosine_table], -1), jnp.concatenate([sine_lookup, sine_lookup], -1))

def turn_half(vectors):
    half_size = vectors.shape[-1] // 2
    return jnp.concatenate([-vectors[..., half_size:], vectors[..., :half_size]], -1)

def apply_rotation(vectors, cosine_table, sine_lookup):
    return vectors * cosine_table[:, None, :] + turn_half(vectors) * sine_lookup[:, None, :]

def rms_scale(value_rows):
    return lax.rsqrt(lax.optimization_barrier(jnp.mean(value_rows * value_rows, axis=-1, keepdims=True)) + norm_eps)

def slot_index(route_rows):
    flat_routes = route_rows.reshape(-1).astype(jnp.int32)
    choose = (flat_routes[:, None] == jnp.arange(EXPERTS, dtype=jnp.int32)[None, :]).astype(jnp.int32)
    before = (jnp.cumsum(choose, axis=0) - choose).astype(jnp.int32)
    return (flat_routes * CAP + lax.optimization_barrier(jnp.sum(before * choose, axis=-1)).astype(jnp.int32)).astype(jnp.int32)

def sequence_layer(params, inputs, segment_row, route_rows):
    gain_attn, query_full, key_expanded, value_expanded, out_full, gain_moe, router_full, gate_full, up_full, down_full = params
    sequence_length = inputs.shape[0]
    query_groups = QUERY_HEADS // KEY_VALUE_HEADS
    cosine_table, sine_lookup = rope_tables(segment_row)
    attention_input = lower_precision(inputs * rms_scale(inputs) * gain_attn)
    query_linear = lower_backward(jnp.dot(attention_input, query_full, precision=highest_precision)).reshape(sequence_length, QUERY_HEADS, HEAD_SIZE)
    key_linear = lower_backward(jnp.dot(attention_input, key_expanded, precision=highest_precision)).reshape(sequence_length, KEY_VALUE_HEADS, HEAD_SIZE)
    value_rows = lower_precision(lower_backward(jnp.dot(attention_input, value_expanded, precision=highest_precision))).reshape(sequence_length, KEY_VALUE_HEADS, HEAD_SIZE)
    query_rows = lower_precision(apply_rotation(query_linear, cosine_table, sine_lookup)).reshape(sequence_length, KEY_VALUE_HEADS, query_groups, HEAD_SIZE)
    keys_rot = lower_precision(apply_rotation(key_linear, cosine_table, sine_lookup))
    scores = lower_backward(HEAD_SIZE ** (-0.5) * jnp.einsum('qhgd,khd->hgqk', query_rows, keys_rot, precision=highest_precision))
    row_index = jnp.arange(sequence_length, dtype=jnp.int32)
    allowed = (segment_row[:, None] == segment_row[None, :]) & (row_index[None, :] <= row_index[:, None])
    probabilities = jax.nn.softmax(jnp.where(allowed, scores, masked_score), axis=-1)
    mixed_heads = jnp.einsum('hgqk,khd->qhgd', lower_precision(probabilities), value_rows, precision=highest_precision)
    mixed_flat = lower_backward(lower_precision(mixed_heads)).reshape(sequence_length, QUERY_HEADS * HEAD_SIZE)
    residual = inputs + lower_backward(jnp.dot(mixed_flat, out_full, precision=highest_precision))
    moe_in = lower_precision(residual * rms_scale(residual) * gain_moe)
    logits = lower_backward(jnp.dot(moe_in, router_full, precision=highest_precision))
    gate_probs = jax.nn.softmax(jnp.take_along_axis(logits, route_rows.astype(jnp.int32), axis=1), axis=-1)
    flat_slot = slot_index(route_rows)
    token_rows = lower_backward(jnp.repeat(moe_in, TOP, axis=0))
    model_width = moe_in.shape[1]
    buffer = jnp.zeros((EXPERTS * CAP, model_width), moe_in.dtype).at[flat_slot].set(token_rows)
    buffer = buffer.reshape(EXPERTS, CAP, model_width)
    gate_lin = lower_backward(jnp.einsum('ecd,edf->ecf', buffer, gate_full, precision=highest_precision))
    up_lin = lower_backward(jnp.einsum('ecd,edf->ecf', buffer, up_full, precision=highest_precision))
    hidden_act = lower_precision(jax.nn.silu(gate_lin) * up_lin)
    expert_out = lower_backward(lower_precision(jnp.einsum('ecf,efd->ecd', hidden_act, down_full, precision=highest_precision)))
    combined = expert_out.reshape(EXPERTS * CAP, model_width)[flat_slot].reshape(sequence_length, TOP, model_width)
    return residual + lax.optimization_barrier(jnp.sum(gate_probs[:, :, None] * combined, axis=1))

def forward_all(inputs, params, segment_ids, routes):
    layer_step = jax.checkpoint(sequence_layer)

    def advance(carried, sequence_item):
        seq_inputs, seq_segments, seq_routes = sequence_item
        return (carried, layer_step(params, seq_inputs, seq_segments, seq_routes))
    seq_count = segment_ids.shape[0]
    model_width = inputs.shape[1]
    _, outputs = lax.scan(advance, None, (inputs.reshape(seq_count, -1, model_width), segment_ids, routes.reshape(seq_count, -1, TOP)))
    return outputs.reshape(-1, model_width)

def reference(hidden, segment_ids, routes, norm_attn, w_query, key_weight, value_weight, w_out, norm_moe, w_router, w_gate, w_up, w_down, cotangent):
    params = tuple((weight.astype(jnp.float32) for weight in (norm_attn, w_query, key_weight, value_weight, w_out, norm_moe, w_router, w_gate, w_up, w_down)))

    def whole_layer(inputs, weights):
        return forward_all(inputs, weights, segment_ids, routes)
    result, pullback = jax.vjp(whole_layer, hidden.astype(jnp.float32), params)
    grad_inputs, weight_grads = pullback(cotangent.astype(jnp.float32))
    return (result.astype(jnp.bfloat16), grad_inputs.astype(jnp.bfloat16), weight_grads[0], weight_grads[1], weight_grads[2], weight_grads[3], weight_grads[4], weight_grads[5], weight_grads[6], weight_grads[7], weight_grads[8], weight_grads[9])
```

```python
import jax
import jax.numpy as jnp
from jax import lax
from jax.sharding import PartitionSpec as P

QUERY_HEADS = 16
KEY_VALUE_HEADS = 8
HEAD_SIZE = 64
EXPERTS = 32
TOP = 8
CAP = 192


norm_eps = 1e-06
rope_base = 10000.0
masked_score = -1e30


def positions_of(segment_row):
    row_index = jnp.arange(segment_row.shape[0], dtype=jnp.int32)
    earlier = (segment_row[:, None] == segment_row[None, :]) & (
        row_index[None, :] < row_index[:, None]
    )
    return jnp.sum(earlier.astype(jnp.int32), axis=-1)


def rope_tables(segment_row):
    position = positions_of(segment_row).astype(jnp.float32)
    half_size = HEAD_SIZE // 2
    frequency = rope_base ** (-jnp.arange(half_size, dtype=jnp.float32) / half_size)
    angles = position[:, None] * frequency[None, :]
    cosine_table = jnp.cos(angles)
    sine_lookup = jnp.sin(angles)
    return (
        jnp.concatenate([cosine_table, cosine_table], -1),
        jnp.concatenate([sine_lookup, sine_lookup], -1),
    )


def turn_half(vectors):
    half_size = vectors.shape[-1] // 2
    return jnp.concatenate([-vectors[..., half_size:], vectors[..., :half_size]], -1)


def apply_rotation(vectors, cosine_table, sine_lookup):
    return vectors * cosine_table[:, None, :] + turn_half(vectors) * sine_lookup[:, None, :]


def rotation_backward(gradient, cosine_table, sine_lookup):
    return gradient * cosine_table[:, None, :] - turn_half(gradient * sine_lookup[:, None, :])


def rms_scale(value_rows):
    return lax.rsqrt(jnp.mean(value_rows * value_rows, axis=-1, keepdims=True) + norm_eps)


def rms_backward(value_rows, inverse, gain, grad_normed):
    scaled = grad_normed * gain
    grad_gain = jnp.sum(grad_normed * value_rows * inverse, axis=0)
    value_rows_gradient = inverse * scaled - value_rows * inverse**3 * jnp.mean(
        scaled * value_rows, axis=-1, keepdims=True
    )
    return (value_rows_gradient, grad_gain)


def masked_softmax(logits, member):
    kept = jnp.where(member, logits, masked_score)
    largest = jnp.max(kept, axis=-1, keepdims=True)
    exponent = jnp.where(member, jnp.exp(kept - largest), 0.0)
    return exponent / jnp.sum(exponent, axis=-1, keepdims=True)


def block_scores(query_rows, keys_rot, segment_row, first_row, block_rows, score_scale):
    sequence_length = segment_row.shape[0]
    query_index = first_row + jnp.arange(block_rows, dtype=jnp.int32)
    key_index = jnp.arange(sequence_length, dtype=jnp.int32)
    allowed = (segment_row[:, None] == segment_row[None, :]) & (
        key_index[None, :] <= query_index[:, None]
    )
    scores = (
        jnp.einsum("qhgd,khd->hgqk", query_rows, keys_rot, preferred_element_type=jnp.float32)
        * score_scale
    )
    return (query_rows, jnp.where(allowed, scores, masked_score))


def attention_forward(query_rows, keys_rot, value_rows, segment_row, score_scale):
    sequence_length = query_rows.shape[0]
    block_rows = min(512, sequence_length)
    query_block, scores = block_scores(
        query_rows, keys_rot, segment_row, 0, block_rows, score_scale
    )
    largest = jnp.max(scores, axis=-1, keepdims=True)
    exponent = jnp.exp(scores - largest)
    row_total = jnp.sum(exponent, axis=-1, keepdims=True)
    probabilities = (exponent / row_total).astype(jnp.bfloat16)
    outputs = jnp.einsum(
        "hgqk,khd->qhgd", probabilities, value_rows, preferred_element_type=jnp.float32
    ).astype(jnp.bfloat16)
    row_sums = [largest + jnp.log(row_total)]
    return (outputs, row_sums)


def attention_backward(
    query_rows, keys_rot, value_rows, segment_row, score_scale, row_sums, mixed_gradient
):
    sequence_length = query_rows.shape[0]
    block_rows = min(512, sequence_length)
    grad_queries = []
    key_rows_gradient = jnp.zeros(keys_rot.shape, jnp.float32)
    value_rows_gradient = jnp.zeros(value_rows.shape, jnp.float32)
    for number, first_row in enumerate(range(0, sequence_length, block_rows)):
        query_block, scores = block_scores(
            query_rows, keys_rot, segment_row, first_row, block_rows, score_scale
        )
        probabilities = jnp.exp(scores - row_sums[number])
        probs_low = probabilities.astype(jnp.bfloat16)
        grad_probs = jnp.einsum(
            "qhgd,khd->hgqk", mixed_gradient, value_rows, preferred_element_type=jnp.float32
        )
        row_delta = jnp.sum(probabilities * grad_probs, axis=-1, keepdims=True)
        grad_scores = (probabilities * (grad_probs - row_delta)).astype(jnp.bfloat16)
        grad_queries.append(
            jnp.einsum("hgqk,khd->qhgd", grad_scores, keys_rot, preferred_element_type=jnp.float32)
            * score_scale
        )
        key_rows_gradient = (
            jnp.einsum(
                "hgqk,qhgd->khd", grad_scores, query_block, preferred_element_type=jnp.float32
            )
            * score_scale
        )
        value_rows_gradient = jnp.einsum(
            "hgqk,qhgd->khd", probs_low, mixed_gradient, preferred_element_type=jnp.float32
        )
    return (grad_queries[0], key_rows_gradient, value_rows_gradient)


def body(
    hidden,
    segment_ids,
    routes,
    norm_attn,
    w_query,
    key_weight,
    value_weight,
    w_out,
    norm_moe,
    w_router,
    w_gate,
    w_up,
    w_down,
    cotangent,
):
    own_rows = w_query.shape[0]
    packed = jnp.concatenate(
        [
            w_query,
            key_weight,
            value_weight,
            w_out,
            w_router,
            norm_attn[:, None],
            norm_moe[:, None],
            routes.astype(jnp.bfloat16).reshape(own_rows, -1),
        ],
        axis=1,
    )
    whole_weights = lax.all_gather(packed, "expert", axis=0, tiled=True)
    columns = [
        w_query.shape[1],
        key_weight.shape[1],
        value_weight.shape[1],
        w_out.shape[1],
        w_router.shape[1],
        1,
        1,
    ]
    pieces = []
    first = 0
    for width in columns:
        pieces.append(whole_weights[:, first : first + width])
        first += width
    query_full, key_expanded, value_expanded, out_full, router_full = pieces[:5]
    gain_attn = pieces[5][:, 0].astype(jnp.float32)
    gain_moe = pieces[6][:, 0].astype(jnp.float32)
    peers = lax.axis_size("expert")
    routes_all = whole_weights[:, first:].astype(jnp.int32).reshape(peers, -1, TOP)
    cotangent_all = lax.all_gather(cotangent, "expert", axis=0, tiled=True)
    sequence_length = hidden.shape[0]
    model_width = hidden.shape[1]
    query_groups = QUERY_HEADS // KEY_VALUE_HEADS
    score_scale = HEAD_SIZE ** (-0.5)
    owned_experts = w_gate.shape[0]
    segment_row = segment_ids[0]
    cosine_table, sine_lookup = rope_tables(segment_row)
    inputs = hidden.astype(jnp.float32)
    inverse_one = rms_scale(inputs)
    attention_input = (inputs * inverse_one * gain_attn).astype(jnp.bfloat16)
    query_linear = jnp.dot(attention_input, query_full, preferred_element_type=jnp.float32).reshape(
        sequence_length, QUERY_HEADS, HEAD_SIZE
    )
    key_linear = jnp.dot(attention_input, key_expanded, preferred_element_type=jnp.float32).reshape(
        sequence_length, KEY_VALUE_HEADS, HEAD_SIZE
    )
    value_rows = (
        jnp.dot(attention_input, value_expanded, preferred_element_type=jnp.float32)
        .astype(jnp.bfloat16)
        .reshape(sequence_length, KEY_VALUE_HEADS, HEAD_SIZE)
    )
    query_rows = (
        apply_rotation(query_linear, cosine_table, sine_lookup)
        .astype(jnp.bfloat16)
        .reshape(sequence_length, KEY_VALUE_HEADS, query_groups, HEAD_SIZE)
    )
    keys_rot = apply_rotation(key_linear, cosine_table, sine_lookup).astype(jnp.bfloat16)
    mixed_heads, row_sums = attention_forward(
        query_rows, keys_rot, value_rows, segment_row, score_scale
    )
    mixed_flat = mixed_heads.reshape(sequence_length, QUERY_HEADS * HEAD_SIZE)
    residual = inputs + jnp.dot(mixed_flat, out_full, preferred_element_type=jnp.float32)
    inverse_two = rms_scale(residual)
    moe_in = (residual * inverse_two * gain_moe).astype(jnp.bfloat16)
    logits = jnp.dot(moe_in, router_full, preferred_element_type=jnp.float32)
    expert_ids = jnp.arange(EXPERTS, dtype=jnp.int32)
    member = jnp.any(routes[:, :, None] == expert_ids[None, None, :], axis=1)
    gate_probs = masked_softmax(logits, member)
    moe_all = lax.all_gather(moe_in, "expert", axis=0, tiled=True)
    logits_all = jnp.dot(moe_all, router_full, preferred_element_type=jnp.float32)
    member_all = jnp.any(routes_all[:, :, :, None] == expert_ids, axis=2)
    gate_all = masked_softmax(logits_all.reshape(member_all.shape), member_all)
    first_expert = lax.axis_index("expert") * owned_experts
    gate_own = lax.dynamic_slice_in_dim(gate_all, first_expert, owned_experts, 2)
    member_own = lax.dynamic_slice_in_dim(member_all, first_expert, owned_experts, 2)
    gate_own = jnp.swapaxes(gate_own, 1, 2)
    member_own = jnp.swapaxes(member_own, 1, 2)
    row_index = jnp.arange(sequence_length, dtype=jnp.int32)
    before = (row_index[:, None] < row_index[None, :]).astype(jnp.bfloat16)
    rank = jnp.einsum(
        "sjt,tu->sju", member_own.astype(jnp.bfloat16), before, preferred_element_type=jnp.float32
    ).astype(jnp.int32)
    rank = jnp.where(member_own, rank, -1)
    place = (rank[:, :, None, :] == jnp.arange(CAP, dtype=jnp.int32)[:, None]).astype(jnp.bfloat16)
    moe_rows = moe_all.reshape(peers, sequence_length, model_width)
    cotangent_rows = cotangent_all.reshape(peers, sequence_length, model_width)
    arrived = jnp.einsum(
        "sjct,std->sjcd", place, moe_rows, preferred_element_type=jnp.float32
    ).astype(jnp.bfloat16)
    dout_rows = jnp.einsum(
        "sjct,std->sjcd", place, cotangent_rows, preferred_element_type=jnp.float32
    ).astype(jnp.bfloat16)
    gate_slot = jnp.sum(place.astype(jnp.float32) * gate_own[:, :, None, :], axis=-1)
    gate_weights, up_weights, down_weights = (w_gate, w_up, w_down)
    gate_lin = jnp.einsum(
        "sjcd,jdf->sjcf", arrived, gate_weights, preferred_element_type=jnp.float32
    )
    up_lin = jnp.einsum("sjcd,jdf->sjcf", arrived, up_weights, preferred_element_type=jnp.float32)
    hidden_act = (jax.nn.silu(gate_lin) * up_lin).astype(jnp.bfloat16)
    expert_out = jnp.einsum(
        "sjcf,jfd->sjcd", hidden_act, down_weights, preferred_element_type=jnp.float32
    ).astype(jnp.bfloat16)
    weighted = (gate_slot[..., None] * expert_out).astype(jnp.bfloat16)
    partial_out = jnp.einsum(
        "sjct,sjcd->std", place, weighted, preferred_element_type=jnp.float32
    ).astype(jnp.bfloat16)
    moe_out = lax.psum_scatter(
        partial_out.reshape(-1, model_width), "expert", scatter_dimension=0, tiled=True
    ).astype(jnp.float32)
    result = (residual + moe_out).astype(jnp.bfloat16)
    grad_result = cotangent.astype(jnp.float32)
    slot_dot = jnp.sum(dout_rows.astype(jnp.float32) * expert_out, axis=-1)
    token_dot = jnp.sum(place.astype(jnp.float32) * slot_dot[..., None], axis=2)
    token_dot = lax.all_to_all(token_dot, "expert", split_axis=0, concat_axis=0, tiled=True)
    grad_gate_probs = token_dot.reshape(EXPERTS, sequence_length).T
    grad_chosen = gate_probs * (
        grad_gate_probs - jnp.sum(gate_probs * grad_gate_probs, axis=-1, keepdims=True)
    )
    grad_logits = grad_chosen.astype(jnp.bfloat16)
    grad_router = jnp.einsum("td,te->de", moe_in, grad_logits, preferred_element_type=jnp.float32)
    grad_moe_in = jnp.einsum(
        "te,de->td", grad_logits, router_full, preferred_element_type=jnp.float32
    )
    grad_arrived = (gate_slot[..., None] * dout_rows).astype(jnp.bfloat16)
    grad_hidden = jnp.einsum(
        "sjcd,jfd->sjcf", grad_arrived, down_weights, preferred_element_type=jnp.float32
    )
    sigmoid_gate = jax.nn.sigmoid(gate_lin)
    activation = gate_lin * sigmoid_gate
    grad_gate_lin = (
        grad_hidden * up_lin * sigmoid_gate * (1.0 + gate_lin * (1.0 - sigmoid_gate))
    ).astype(jnp.bfloat16)
    grad_up_lin = (grad_hidden * activation).astype(jnp.bfloat16)
    grad_down = jnp.einsum(
        "sjcf,sjcd->jfd", hidden_act, grad_arrived, preferred_element_type=jnp.float32
    )
    grad_gate = jnp.einsum(
        "sjcd,sjcf->jdf", arrived, grad_gate_lin, preferred_element_type=jnp.float32
    )
    grad_up = jnp.einsum("sjcd,sjcf->jdf", arrived, grad_up_lin, preferred_element_type=jnp.float32)
    grad_rows = jnp.einsum(
        "sjcf,jdf->sjcd", grad_gate_lin, gate_weights, preferred_element_type=jnp.float32
    )
    grad_rows = (
        grad_rows
        + jnp.einsum("sjcf,jdf->sjcd", grad_up_lin, up_weights, preferred_element_type=jnp.float32)
    ).astype(jnp.bfloat16)
    partial_grad = jnp.einsum(
        "sjct,sjcd->std", place, grad_rows, preferred_element_type=jnp.float32
    ).astype(jnp.bfloat16)
    moe_grad = lax.psum_scatter(
        partial_grad.reshape(-1, model_width), "expert", scatter_dimension=0, tiled=True
    ).astype(jnp.float32)
    expert_grads = (grad_gate, grad_up, grad_down)
    grad_moe_in = grad_moe_in + moe_grad
    grad_resid_norm, grad_gain_moe = rms_backward(residual, inverse_two, gain_moe, grad_moe_in)
    grad_residual = grad_result + grad_resid_norm
    grad_branch = grad_residual.astype(jnp.bfloat16)
    grad_out = jnp.einsum("ti,to->io", mixed_flat, grad_branch, preferred_element_type=jnp.float32)
    mixed_gradient = jnp.einsum(
        "to,io->ti", grad_branch, out_full, preferred_element_type=jnp.float32
    ).astype(jnp.bfloat16)
    mixed_gradient = mixed_gradient.reshape(
        sequence_length, KEY_VALUE_HEADS, query_groups, HEAD_SIZE
    )
    grad_queries, key_rows_gradient, value_rows_gradient = attention_backward(
        query_rows, keys_rot, value_rows, segment_row, score_scale, row_sums, mixed_gradient
    )
    grad_query_lin = (
        rotation_backward(
            grad_queries.reshape(sequence_length, QUERY_HEADS, HEAD_SIZE), cosine_table, sine_lookup
        )
        .astype(jnp.bfloat16)
        .reshape(sequence_length, QUERY_HEADS * HEAD_SIZE)
    )
    grad_key_lin = (
        rotation_backward(key_rows_gradient, cosine_table, sine_lookup)
        .astype(jnp.bfloat16)
        .reshape(sequence_length, KEY_VALUE_HEADS * HEAD_SIZE)
    )
    value_linear_gradient = value_rows_gradient.astype(jnp.bfloat16).reshape(
        sequence_length, KEY_VALUE_HEADS * HEAD_SIZE
    )
    grad_query = jnp.einsum(
        "td,tq->dq", attention_input, grad_query_lin, preferred_element_type=jnp.float32
    )
    grad_key = jnp.einsum(
        "td,tq->dq", attention_input, grad_key_lin, preferred_element_type=jnp.float32
    )
    grad_value = jnp.einsum(
        "td,tq->dq", attention_input, value_linear_gradient, preferred_element_type=jnp.float32
    )
    grad_attn_in = jnp.einsum(
        "tq,dq->td", grad_query_lin, query_full, preferred_element_type=jnp.float32
    )
    grad_attn_in = grad_attn_in + jnp.einsum(
        "tq,dq->td", grad_key_lin, key_expanded, preferred_element_type=jnp.float32
    )
    grad_attn_in = grad_attn_in + jnp.einsum(
        "tq,dq->td", value_linear_gradient, value_expanded, preferred_element_type=jnp.float32
    )
    grad_input_norm, grad_gain_attn = rms_backward(inputs, inverse_one, gain_attn, grad_attn_in)
    grad_input = (grad_residual + grad_input_norm).astype(jnp.bfloat16)
    small = jnp.concatenate(
        [grad_query, grad_key, grad_value, grad_out, grad_router]
        + [grad_gain_attn[:, None], grad_gain_moe[:, None]],
        axis=1,
    ).astype(jnp.bfloat16)
    small = lax.psum_scatter(small, "expert", scatter_dimension=0, tiled=True)
    small = lax.psum(small, "dp").astype(jnp.float32)
    shares = []
    first = 0
    for width in columns:
        shares.append(small[:, first : first + width])
        first += width
    big = [lax.psum(g.astype(jnp.bfloat16), "dp").astype(jnp.float32) for g in expert_grads]
    return (
        result,
        grad_input,
        shares[5][:, 0],
        shares[0],
        shares[1],
        shares[2],
        shares[3],
        shares[6][:, 0],
        shares[4],
        big[0],
        big[1],
        big[2],
    )


def solution(mesh):
    in_specs = (
        P(("dp", "expert"), None),
        P(("dp", "expert"), None),
        P(("dp", "expert"), None),
        P("expert"),
        P("expert", None),
        P("expert", None),
        P("expert", None),
        P("expert", None),
        P("expert"),
        P("expert", None),
        P("expert", None, None),
        P("expert", None, None),
        P("expert", None, None),
        P(("dp", "expert"), None),
    )
    out_specs = (
        P(("dp", "expert"), None),
        P(("dp", "expert"), None),
        P("expert"),
        P("expert", None),
        P("expert", None),
        P("expert", None),
        P("expert", None),
        P("expert"),
        P("expert", None),
        P("expert", None, None),
        P("expert", None, None),
        P("expert", None, None),
    )
    return jax.shard_map(body, mesh=mesh, in_specs=in_specs, out_specs=out_specs, check_vma=False)
```

```python
import functools

import jax
import jax.numpy as jnp
from jax import lax
from jax.experimental import pallas as pl
from jax.experimental.pallas import tpu as pltpu
from jax.sharding import PartitionSpec as P

EXPERTS = 32
TOP = 8
CAP = 192
HALF = 32
ROWS = 256
MISC = 16
F32 = jnp.float32
BF = jnp.bfloat16
COST = pl.CostEstimate(flops=1 << 20, bytes_accessed=1 << 20, transcendentals=0)
norm_eps = 1e-06
rope_base = 10000.0


def dot(a,b,ca=1,cb=0):
    return lax.dot_general(a,b,(((ca,),(cb,)),((),())),preferred_element_type=F32)

def step_kernel(aliased, *refs):
    (first_ref, x0_ref, x1_ref, d0_ref, d1_ref, r_ref, m_ref, rank_ref, key_ref,
     wg_ref, wu_ref, wd_ref) = refs[:12]
    (g0_ref, g1_ref, o0_ref, o1_ref, dot_ref, xs_ref, ge_ref, hs_ref, dgs_ref, dus_ref,
     t_s, gate_s, rg_s, ro_s) = refs[12 + aliased:]
    owned = gate_s.shape[0]
    E = m_ref.shape[1]
    T = x0_ref.shape[0]
    e = pl.program_id(0)
    x_refs = (x0_ref, x1_ref)
    d_refs = (d0_ref, d1_ref)

    @pl.when(e == 0)
    def _():
        for q in range(2):
            t_s[...] = dot(x_refs[q][...], r_ref[...]).T
            mem = m_ref[q] > 0.5
            kept = jnp.where(mem, t_s[:E, :], -1e30)
            ex = jnp.where(mem, jnp.exp(kept - jnp.max(kept, axis=0, keepdims=True)), 0.0)
            t_s[:E, :] = ex / jnp.sum(ex, axis=0, keepdims=True)
            for j in range(owned):
                gate_s[j, q] = t_s[pl.ds(first_ref[0] + j, 1), :]

    slot = lax.broadcasted_iota(jnp.int32, (CAP, T), 0)
    gs = []
    hits = []
    ds = []
    for q in range(2):
        rows = slice(q * CAP, (q + 1) * CAP)
        hit = slot == rank_ref[0, q]
        S = jnp.where(hit, 1.0, 0.0).astype(BF)
        xs_ref[0, rows, :] = dot(S, x_refs[q][...]).astype(BF)
        d = dot(S, d_refs[q][...])
        g = jnp.sum(jnp.where(hit, gate_s[e, q], 0.0), axis=1, keepdims=True)
        ge_ref[0, rows, :] = (g * d).astype(BF)
        gs.append(g)
        hits.append(hit)
        ds.append(d.astype(BF))
    x = xs_ref[0]
    gl = dot(x, wg_ref[0])
    ul = dot(x, wu_ref[0])
    sg = jax.nn.sigmoid(gl)
    act = gl * sg
    h = (act * ul).astype(BF)
    hs_ref[0] = h
    eo = dot(h, wd_ref[0]).astype(BF)
    for q in range(2):
        part = eo[q * CAP : (q + 1) * CAP].astype(F32)
        ro_s[q, pl.ds(pl.multiple_of(e * CAP, CAP), CAP), :] = (gs[q] * part).astype(BF)
        sd = jnp.sum(part * ds[q].astype(F32), axis=1, keepdims=True)
        dot_ref[0, q] = jnp.sum(jnp.where(hits[q], sd, 0.0), axis=0, keepdims=True)
    dh = dot(ge_ref[0], wd_ref[0], 1, 1)
    dgl = (dh * ul * sg * (1.0 + gl * (1.0 - sg))).astype(BF)
    dul = (dh * act).astype(BF)
    dgs_ref[0] = dgl
    dus_ref[0] = dul
    dr = (dot(dgl, wg_ref[0], 1, 1) + dot(dul, wu_ref[0], 1, 1)).astype(BF)
    for q in range(2):
        rg_s[q, pl.ds(pl.multiple_of(e * CAP, CAP), CAP), :] = dr[q * CAP : (q + 1) * CAP]

    @pl.when(e == owned - 1)
    def _():
        lane = lax.broadcasted_iota(jnp.int32, (T, owned * CAP), 1)
        for q, g_ref, o_ref in ((0, g0_ref, o0_ref), (1, g1_ref, o1_ref)):
            keys = key_ref[q]
            hit = lane == keys[:, 0:1]
            for j in range(1, owned):
                hit = hit | (lane == keys[:, j : j + 1])
            S = jnp.where(hit, 1.0, 0.0).astype(BF)
            g_ref[...] = dot(S, rg_s[q]).astype(BF)
            o_ref[...] = dot(S, ro_s[q]).astype(BF)


def expert_step(k, first, x, d, router, member, rank, keys, wg, wu, wd, kept):
    owned, peers, _, T = rank.shape
    D, F = wg.shape[1:]
    E = member.shape[1]
    M = 2 * CAP
    rows = peers * CAP
    full = lambda e, f: (0, 0)
    shapes = [
        jax.ShapeDtypeStruct((owned, rows, D), BF),
        jax.ShapeDtypeStruct((owned, rows, D), BF),
    ] + [jax.ShapeDtypeStruct((owned, rows, F), BF)] * 3
    token = jax.ShapeDtypeStruct((T, D), BF)
    aliased = 0 if kept is None else len(shapes)
    return pl.pallas_call(
        functools.partial(step_kernel, aliased),
        grid_spec=pltpu.PrefetchScalarGridSpec(
            num_scalar_prefetch=1,
            grid=(owned,),
            in_specs=[pl.BlockSpec((T, D), full)] * 4
            + [
                pl.BlockSpec((D, 128), lambda e, f: (0, D // 128)),
                pl.BlockSpec((2, E, T), lambda e, f: (k, 0, 0)),
                pl.BlockSpec((1, 2, 1, T), lambda e, f: (e, k, 0, 0)),
                pl.BlockSpec((2, T, owned), lambda e, f: (k, 0, 0)),
                pl.BlockSpec((1, D, F), lambda e, f: (e, 0, 0)),
                pl.BlockSpec((1, D, F), lambda e, f: (e, 0, 0)),
                pl.BlockSpec((1, F, D), lambda e, f: (e, 0, 0)),
            ]
            + [pl.BlockSpec(memory_space=pl.ANY)] * aliased,
            out_specs=[pl.BlockSpec((T, D), full)] * 4
            + [pl.BlockSpec((1, 2, 1, T), lambda e, f: (e, 0, 0, 0))]
            + [pl.BlockSpec((1, M, s.shape[2]), lambda e, f: (e, k, 0)) for s in shapes],
            scratch_shapes=[
                pltpu.VMEM((128, T), F32),
                pltpu.VMEM((owned, 2, 1, T), F32),
                pltpu.VMEM((2, owned * CAP, D), BF),
                pltpu.VMEM((2, owned * CAP, D), BF),
            ],
        ),
        out_shape=[token] * 4 + [jax.ShapeDtypeStruct((owned, 2, 1, T), F32)] + shapes,
        input_output_aliases={12 + i: 5 + i for i in range(aliased)},
        compiler_params=pltpu.CompilerParams(vmem_limit_bytes=60 << 20),
        cost_estimate=COST,
        name="expert_step",
    )(first, *x, *d, router, member, rank, keys, wg, wu, wd, *(kept or ()))


def weight_kernel(parts, bit_ref, xs_ref, ge_ref, hs_ref, dgs_ref, dus_ref, send_ref, keep_ref, *acc):
    at = pl.program_id(1)
    half = xs_ref.shape[2] // 2
    for n, o_ref in enumerate((send_ref, keep_ref)):
        bit = 1 - bit_ref[0] if n == 0 else bit_ref[0]
        off = pl.multiple_of(bit * half, half)
        x = xs_ref[0, :, pl.ds(off, half)]
        totals = (
            dot(x, dgs_ref[0], 0, 0),
            dot(x, dus_ref[0], 0, 0),
            dot(hs_ref[0], ge_ref[0, :, pl.ds(off, half)], 0, 0),
        )
        for i, total in enumerate(totals):
            if parts > 1:
                s = acc[0].at[3 * n + i]
                total = jnp.where(at == 0, 0.0, s[...]) + total
                s[...] = total
            o_ref[0, i] = total.astype(BF)


def weight_grads(bit, first, count, kept):
    rows, D = kept[0].shape[1:]
    F = kept[2].shape[2]
    half = D // 2
    assert half == F
    block = min(rows, 8 * CAP)
    parts = rows // block
    out = jax.ShapeDtypeStruct((count, 3, half, F), BF)
    return pl.pallas_call(
        functools.partial(weight_kernel, parts),
        grid_spec=pltpu.PrefetchScalarGridSpec(
            num_scalar_prefetch=1,
            grid=(count, parts),
            in_specs=[
                pl.BlockSpec((1, block, s.shape[2]), lambda e, i, b: (first + e, i, 0)) for s in kept
            ],
            out_specs=[pl.BlockSpec((1, 3, half, F), lambda e, i, b: (e, 0, 0, 0))] * 2,
            scratch_shapes=[pltpu.VMEM((6, half, F), F32)] if parts > 1 else [],
        ),
        out_shape=[out, out],
        compiler_params=pltpu.CompilerParams(vmem_limit_bytes=60 << 20),
        cost_estimate=COST,
        name="weight_grads",
    )(bit, *kept)


def halve_kernel(bit_ref, keep_ref, got_ref, send_ref, kept_ref):
    half = send_ref.shape[2]
    for n, o_ref in enumerate((send_ref, kept_ref)):
        bit = 1 - bit_ref[0] if n == 0 else bit_ref[0]
        rows = pl.ds(pl.multiple_of(bit * half, half), half)
        for i in range(keep_ref.shape[1]):
            o_ref[0, i] = (
                keep_ref[0, i, rows, :].astype(F32) + got_ref[0, i, rows, :].astype(F32)
            ).astype(BF)


def halve(bit, keep, got):
    count, mats, rows, F = keep.shape
    full = pl.BlockSpec((1, mats, rows, F), lambda e, b: (e, 0, 0, 0))
    part = pl.BlockSpec((1, mats, rows // 2, F), lambda e, b: (e, 0, 0, 0))
    out = jax.ShapeDtypeStruct((count, mats, rows // 2, F), BF)
    return pl.pallas_call(
        halve_kernel,
        grid_spec=pltpu.PrefetchScalarGridSpec(
            num_scalar_prefetch=1, grid=(count,), in_specs=[full, full], out_specs=[part, part]
        ),
        out_shape=[out, out],
        cost_estimate=COST,
        name="halve",
    )(bit, keep, got)


def place_kernel(bits_ref, q_ref, *refs):
    for i, o_ref in enumerate(refs[-3:]):
        o_ref[0] = q_ref[0, i].astype(F32)


def place_quarter(first, owned, bits, quarter, held):
    count, _, rows, F = quarter.shape
    D = 4 * rows
    shapes = [(owned, D, F), (owned, D, F), (owned, F, D)]
    tall = pl.BlockSpec((1, rows, F), lambda e, b: (first + e, 2 * b[0] + b[1], 0))
    wide = pl.BlockSpec((1, rows, F), lambda e, b: (first + e, b[1], b[0]))
    aliased = 0 if held is None else 3
    return pl.pallas_call(
        place_kernel,
        grid_spec=pltpu.PrefetchScalarGridSpec(
            num_scalar_prefetch=1,
            grid=(count,),
            in_specs=[pl.BlockSpec((1, 3, rows, F), lambda e, b: (e, 0, 0, 0))]
            + [pl.BlockSpec(memory_space=pl.ANY)] * aliased,
            out_specs=[tall, tall, wide],
        ),
        out_shape=[jax.ShapeDtypeStruct(s, F32) for s in shapes],
        input_output_aliases={2 + i: i for i in range(aliased)},
        cost_estimate=COST,
        name="place_quarter",
    )(bits, quarter, *(held or ()))


def assemble_kernel(place,p_ref,*refs):
    ins=refs[:-2]; o_ref,sem=refs[-2:]
    copies=[]
    for n,r in enumerate(ins):
        chips,sub,_=r.shape
        for k in range(chips):
            row=pl.multiple_of(p_ref[n*chips+k]*sub,sub)
            copies.append(pltpu.make_async_copy(r.at[k],o_ref.at[pl.ds(row,sub),:],sem.at[n*chips+k]))
    for c in copies: c.start()
    for c in copies: c.wait()

def assemble(places,pieces):
    n=len(pieces); chips,sub,W=pieces[0].shape
    return pl.pallas_call(functools.partial(assemble_kernel,None),
        grid_spec=pltpu.PrefetchScalarGridSpec(num_scalar_prefetch=1,grid=(1,),
          in_specs=[pl.BlockSpec(memory_space=pl.ANY)]*n,
          out_specs=pl.BlockSpec((n*chips*sub,W),lambda i,p:(0,0)),
          scratch_shapes=[pltpu.SemaphoreType.DMA((n*chips,))]),
        out_shape=jax.ShapeDtypeStruct((n*chips*sub,W),BF),cost_estimate=COST,
        compiler_params=pltpu.CompilerParams(vmem_limit_bytes=40<<20),
        name="assemble")(places,*pieces)

def ring_steps(v):
    n=lax.axis_size("expert")
    ring=[(i,(i+2)%n) for i in range(n)]
    blocks=[v]
    for _ in range(n//2-1):
        blocks.append(lax.ppermute(blocks[-1],"expert",ring))
    return blocks

def swap_pair(v):
    return lax.ppermute(v,"expert",[(i,i^1) for i in range(lax.axis_size("expert"))])

def swap_dp(v,r):
    return lax.ppermute(v,"dp",[(i,i^r) for i in range(lax.axis_size("dp"))])

def shift_chips(v,k):
    n=lax.axis_size("expert")
    return lax.ppermute(v,"expert",[(i,(i+2*k)%n) for i in range(n)])

def ring_gather(v):
    blocks=[]
    for b in ring_steps(v):
        blocks+=[b,swap_pair(b)]
    return blocks

def send_back(v,k,b):
    n=lax.axis_size("expert")
    return lax.ppermute(v,"expert",[(i,((i//2-k)%(n//2))*2+((i%2)^b)) for i in range(n)]) if k or b else v

def all_shifts(v):
    return [v]+[shift_chips(v,k) for k in range(1,lax.axis_size("expert")//2)]

def share_kernel(rows_ref, *refs):
    o_ref = refs[-1]
    for r, piece in enumerate(refs[:-1]):
        sub = piece.shape[0]
        row = pl.multiple_of(rows_ref[r], sub)
        o_ref[pl.ds(row, sub), :] = piece[...].astype(F32)


def place_share(rows, pieces):
    sub, W = pieces[0].shape
    n = len(pieces)
    return pl.pallas_call(
        share_kernel,
        grid_spec=pltpu.PrefetchScalarGridSpec(
            num_scalar_prefetch=1,
            grid=(1,),
            in_specs=[pl.BlockSpec((sub, W), lambda i, r: (0, 0))] * n,
            out_specs=pl.BlockSpec((n * sub, W), lambda i, r: (0, 0)),
        ),
        out_shape=jax.ShapeDtypeStruct((n * sub, W), F32),
        cost_estimate=COST,
        name="place_share",
    )(rows, *pieces)


def own_slice(pack):
    dp=lax.axis_size("dp")
    sub=pack.shape[0]//dp
    return lax.dynamic_slice_in_dim(pack,lax.axis_index("dp")*sub,sub,0)

def tie(*values):
    return lax.optimization_barrier(values)

def rotate(v):
    lane=lax.broadcasted_iota(jnp.int32,v.shape,1)
    width=v.shape[1]
    return jnp.where(lane%(2*HALF)<HALF,pltpu.roll(v,width-HALF,1),pltpu.roll(v,HALF,1))

def spread(v):
    lane=lax.broadcasted_iota(jnp.int32,v.shape,1)
    low=lane<2*HALF
    other=pltpu.roll(v,2*HALF,1)
    zero=jnp.zeros_like(v)
    return [jnp.where(low,v,zero).astype(BF),jnp.where(low,zero,other).astype(BF),
            jnp.where(low,other,zero).astype(BF),jnp.where(low,zero,v).astype(BF)]

def gain_row(misc_ref,which):
    return misc_ref[...].astype(F32).T[which:which+1,:]

def attend_kernel(gain_at,h_ref,misc_ref,wq_ref,wk_ref,wv_ref,cos_ref,sin_ref,segc_ref,segr_ref,
                  q_ref,k_ref,v_ref,mix_ref,lse_ref,x_s,bias_s):
    T=h_ref.shape[0]
    @pl.when(pl.program_id(0)==0)
    def _():
        inputs=h_ref[...].astype(F32)
        inv=lax.rsqrt(jnp.mean(inputs*inputs,axis=-1,keepdims=True)+norm_eps)
        x_s[...]=(inputs*inv*gain_row(misc_ref,gain_at)).astype(BF)
        r=lax.broadcasted_iota(jnp.int32,(T,T),0); c=lax.broadcasted_iota(jnp.int32,(T,T),1)
        bias_s[...]=jnp.where((segc_ref[...]==segr_ref[...])&(c<=r),0.0,-1e30)
    x=x_s[...]
    cos=cos_ref[...]; sin=sin_ref[...]
    ql=dot(x,wq_ref[...])
    qs=[]
    for c in range(2):
        part=ql[:,128*c:128*c+128]
        part=part*cos+rotate(part)*sin
        q_ref[:,128*c:128*c+128]=part.astype(BF)
        qs.append((part.astype(BF).astype(F32)*0.125).astype(BF))
    kl=dot(x,wk_ref[...])
    kl=(kl*cos+rotate(kl)*sin).astype(BF)
    k_ref[...]=kl
    vl=dot(x,wv_ref[...]).astype(BF)
    v_ref[...]=vl
    kp=spread(kl.astype(F32)); vp=spread(vl.astype(F32))
    lane=lax.broadcasted_iota(jnp.int32,(ROWS,128),1)
    for b in range(T//ROWS):
        rows=slice(b*ROWS,(b+1)*ROWS); nk=(b+1)*ROWS
        lse=jnp.zeros((ROWS,128),F32)
        for c in range(2):
            o=None
            for half in range(2):
                i=2*c+half
                s=dot(qs[c][rows],kp[i][:nk],1,1)+bias_s[rows,:nk]
                m=jnp.max(s,axis=1,keepdims=True)
                e=jnp.exp(s-m)
                l=jnp.sum(e,axis=1,keepdims=True)
                p=(e*(1.0/l)).astype(BF)
                part=dot(p,vp[i][:nk])
                o=part if o is None else o+part
                lse=jnp.where(lane==i,m+jnp.log(l),lse)
            mix_ref[rows,128*c:128*c+128]=o.astype(BF)
        lse_ref[0,:,rows]=lse.T[:8,:]

def attend(gain_at,h,w,cos,sin,segc,segr,kv_heads):
    T,D=h.shape
    steps=kv_heads//2
    full=lambda g:(0,0)
    qb=D//256; kb=D//128; vb=kb+kv_heads//2; mb=vb+kv_heads//2
    return pl.pallas_call(functools.partial(attend_kernel,gain_at),grid=(steps,),
        in_specs=[pl.BlockSpec((T,D),full),pl.BlockSpec((D,128),lambda g:(0,mb)),
                  pl.BlockSpec((D,256),lambda g:(0,g)),pl.BlockSpec((D,128),lambda g:(0,kb+g)),pl.BlockSpec((D,128),lambda g:(0,vb+g)),
                  pl.BlockSpec((T,128),full),pl.BlockSpec((T,128),full),pl.BlockSpec((T,1),full),pl.BlockSpec((1,T),full)],
        out_specs=[pl.BlockSpec((T,256),lambda g:(0,g)),pl.BlockSpec((T,128),lambda g:(0,g)),pl.BlockSpec((T,128),lambda g:(0,g)),
                   pl.BlockSpec((T,256),lambda g:(0,g)),pl.BlockSpec((1,8,T),lambda g:(g,0,0))],
        out_shape=[jax.ShapeDtypeStruct((T,D),BF),jax.ShapeDtypeStruct((T,64*kv_heads),BF),jax.ShapeDtypeStruct((T,64*kv_heads),BF),
                   jax.ShapeDtypeStruct((T,D),BF),jax.ShapeDtypeStruct((steps,8,T),F32)],
        scratch_shapes=[pltpu.VMEM((T,D),BF),pltpu.VMEM((T,T),F32)],
        cost_estimate=COST,
        name="attend")(h,w,w,w,w,cos,sin,segc,segr)


def project_kernel(gain_at,m_ref,w_ref,h_ref,misc_ref,res_ref,moe_ref):
    res=h_ref[...].astype(F32)+dot(m_ref[...],w_ref[...])
    res_ref[...]=res
    inv=lax.rsqrt(jnp.mean(res*res,axis=-1,keepdims=True)+norm_eps)
    moe_ref[...]=(res*inv*gain_row(misc_ref,gain_at)).astype(BF)

def project(gain_at,mixed,w2,h,w1):
    T,D=h.shape
    R=256
    return pl.pallas_call(functools.partial(project_kernel,gain_at),grid=(T//R,),
        in_specs=[pl.BlockSpec((R,D),lambda i:(i,0)),pl.BlockSpec((D,D),lambda i:(0,0)),pl.BlockSpec((R,D),lambda i:(i,0)),
                  pl.BlockSpec((D,128),lambda i:(0,MISC))],
        out_specs=[pl.BlockSpec((R,D),lambda i:(i,0)),pl.BlockSpec((R,D),lambda i:(i,0))],
        out_shape=[jax.ShapeDtypeStruct((T,D),F32),jax.ShapeDtypeStruct((T,D),BF)],
        cost_estimate=COST,
        name="project")(mixed,w2,h,w1)

def branch_kernel(gain_at,mg_ref,res_ref,moe_ref,mix_ref,cot_ref,wo_ref,r_ref,misc_ref,mem_ref,td_ref,
                  dres_ref,dmix_ref,out_ref,t_s):
    T,D=res_ref.shape
    E=mem_ref.shape[0]
    t_s[...]=dot(moe_ref[...],r_ref[...]).T
    mem=mem_ref[...]>0.5
    kept=jnp.where(mem,t_s[:E,:],-1e30)
    e=jnp.where(mem,jnp.exp(kept-jnp.max(kept,axis=0,keepdims=True)),0.0)
    g=e/jnp.sum(e,axis=0,keepdims=True)
    td=td_ref[...]
    t_s[...]=jnp.zeros_like(t_s)
    t_s[:E,:]=g*(td-jnp.sum(g*td,axis=0,keepdims=True))
    gl=t_s[...].T.astype(BF)
    dmoe=dot(gl,r_ref[...],1,1)+mg_ref[...].astype(F32)
    res=res_ref[...]
    inv=lax.rsqrt(jnp.mean(res*res,axis=-1,keepdims=True)+norm_eps)
    gain=gain_row(misc_ref,gain_at)
    scaled=dmoe*gain
    grad_gain=jnp.sum(dmoe*res*inv,axis=0,keepdims=True)
    dres=cot_ref[...].astype(F32)+inv*scaled-res*(inv*inv*inv*jnp.mean(scaled*res,axis=-1,keepdims=True))
    dres_ref[...]=dres
    br=dres.astype(BF)
    dmix_ref[...]=dot(br,wo_ref[...],1,1).astype(BF)
    out_ref[:,:D]=dot(mix_ref[...],br,0,0).astype(BF)
    lane=lax.broadcasted_iota(jnp.int32,(D,128),1)
    column=jnp.broadcast_to(grad_gain,(128,D)).T
    out_ref[:,D:]=jnp.where(lane==E,column,dot(moe_ref[...],gl,0,0)).astype(BF)

def branch(gain_at,mg,res,moe_in,mixed,cot,w2,w1,mem_t,td):
    T,D=res.shape
    E=mem_t.shape[0]
    full=lambda i:(0,0)
    return pl.pallas_call(functools.partial(branch_kernel,gain_at),grid=(1,),
        in_specs=[pl.BlockSpec((T,D),full)]*5+[pl.BlockSpec((D,D),full),pl.BlockSpec((D,128),lambda i:(0,D//128)),
                  pl.BlockSpec((D,128),lambda i:(0,MISC)),pl.BlockSpec((E,T),full),pl.BlockSpec((E,T),full)],
        out_specs=[pl.BlockSpec((T,D),full),pl.BlockSpec((T,D),full),pl.BlockSpec((D,D+128),full)],
        out_shape=[jax.ShapeDtypeStruct((T,D),F32),jax.ShapeDtypeStruct((T,D),BF),jax.ShapeDtypeStruct((D,D+128),BF)],
        scratch_shapes=[pltpu.VMEM((128,T),F32)],
        compiler_params=pltpu.CompilerParams(vmem_limit_bytes=60<<20),
        cost_estimate=COST,
        name="branch")(mg,res,moe_in,mixed,cot,w2,w2,w1,mem_t,td)

def fold(v):
    return v+pltpu.roll(v,2*HALF,1)

def attend_back_kernel(gain_at,h_ref,misc_ref,wq_ref,wk_ref,wv_ref,cos_ref,sin_ref,segc_ref,segr_ref,
                       q_ref,k_ref,v_ref,dm_ref,lse_ref,dres_ref,og_ref,
                       out_ref,gin_ref,x_s,bias_s,da_s):
    T,D=h_ref.shape
    step=pl.program_id(0)
    @pl.when(step==0)
    def _():
        inputs=h_ref[...].astype(F32)
        inv=lax.rsqrt(jnp.mean(inputs*inputs,axis=-1,keepdims=True)+norm_eps)
        x_s[...]=(inputs*inv*gain_row(misc_ref,gain_at)).astype(BF)
        r=lax.broadcasted_iota(jnp.int32,(T,T),0); c=lax.broadcasted_iota(jnp.int32,(T,T),1)
        bias_s[...]=jnp.where((segc_ref[...]==segr_ref[...])&(r<=c),0.0,-1e30)
        wide=og_ref.shape[1]
        out_ref[:,out_ref.shape[1]-128-wide:out_ref.shape[1]-128]=og_ref[...]
    cos=cos_ref[...]; sin=sin_ref[...]
    kp=spread(k_ref[...].astype(F32)); vp=spread(v_ref[...].astype(F32))
    low=lax.broadcasted_iota(jnp.int32,(T,128),1)<2*HALF
    dq_all=[];dk_all=[];dv_all=[]
    for c in range(2):
        cols=slice(128*c,128*c+128)
        qs=(q_ref[:,cols].astype(F32)*0.125).astype(BF)
        dm=dm_ref[:,cols]
        dks=[];dvs=[];dq=[None]*(T//ROWS)
        for half in range(2):
            i=2*c+half
            dk=None;dv=None
            for b in reversed(range(T//ROWS)):
                rows=slice(b*ROWS,(b+1)*ROWS); nk=(b+1)*ROWS
                s=dot(kp[i][:nk],qs[rows],1,1)+bias_s[:nk,rows]
                p=jnp.exp(s-lse_ref[0,i:i+1,rows])
                dp=dot(vp[i][:nk],dm[rows],1,1)
                delta=jnp.sum(p*dp,axis=0,keepdims=True)
                ds=(p*(dp-delta)).astype(BF)
                part=dot(ds,kp[i][:nk],0,0)
                dq[b]=part if dq[b] is None else dq[b]+part
                pk=dot(ds,qs[rows]); pv=dot(p.astype(BF),dm[rows])
                if dk is None:
                    dk,dv=pk,pv
                else:
                    dk=jnp.concatenate([dk[:nk]+pk,dk[nk:]],axis=0)
                    dv=jnp.concatenate([dv[:nk]+pv,dv[nk:]],axis=0)
            dks.append(dk);dvs.append(dv)
        dql=jnp.concatenate(dq,axis=0)*0.125
        dq_all.append((dql*cos-rotate(dql)*sin).astype(BF))
        dk_all.append(fold(jnp.where(low,dks[0],dks[1])))
        dv_all.append(fold(jnp.where(low,dvs[0],dvs[1])))
    dkl=jnp.where(low,dk_all[0],dk_all[1])
    dkl=(dkl*cos-rotate(dkl)*sin).astype(BF)
    dvl=jnp.where(low,dv_all[0],dv_all[1]).astype(BF)
    dql=jnp.concatenate(dq_all,axis=1)
    x=x_s[...]
    base=pl.multiple_of(step*512,512)
    out_ref[:,pl.ds(base,256)]=dot(x,dql,0,0).astype(BF)
    out_ref[:,pl.ds(base+256,128)]=dot(x,dkl,0,0).astype(BF)
    out_ref[:,pl.ds(base+384,128)]=dot(x,dvl,0,0).astype(BF)
    da=dot(dql,wq_ref[...],1,1)+dot(dkl,wk_ref[...],1,1)+dot(dvl,wv_ref[...],1,1)
    @pl.when(step==0)
    def _():
        da_s[...]=da
    @pl.when(step>0)
    def _():
        da_s[...]+=da
    @pl.when(step==pl.num_programs(0)-1)
    def _():
        inputs=h_ref[...].astype(F32)
        inv=lax.rsqrt(jnp.mean(inputs*inputs,axis=-1,keepdims=True)+norm_eps)
        dattn=da_s[...]
        scaled=dattn*gain_row(misc_ref,gain_at)
        grad_gain=jnp.sum(dattn*inputs*inv,axis=0,keepdims=True)
        gin_ref[...]=(dres_ref[...]+inv*scaled-inputs*(inv*inv*inv*jnp.mean(scaled*inputs,axis=-1,keepdims=True))).astype(BF)
        out_ref[:,out_ref.shape[1]-128:]=jnp.broadcast_to(grad_gain,(128,D)).T.astype(BF)

def attend_back(gain_at,h,w,cos,sin,segc,segr,q,k,v,dmix,lse,dres,og):
    T,D=h.shape
    kvw=k.shape[1]
    steps=lse.shape[0]
    full=lambda g:(0,0)
    kb=D//128; vb=kb+kvw//128
    wide=og.shape[1]
    width=D+2*kvw+wide+128
    return pl.pallas_call(functools.partial(attend_back_kernel,gain_at),grid=(steps,),
        in_specs=[pl.BlockSpec((T,D),full),pl.BlockSpec((D,128),lambda g:(0,MISC)),
                  pl.BlockSpec((D,256),lambda g:(0,g)),pl.BlockSpec((D,128),lambda g:(0,kb+g)),pl.BlockSpec((D,128),lambda g:(0,vb+g)),
                  pl.BlockSpec((T,128),full),pl.BlockSpec((T,128),full),pl.BlockSpec((T,1),full),pl.BlockSpec((1,T),full),
                  pl.BlockSpec((T,256),lambda g:(0,g)),pl.BlockSpec((T,128),lambda g:(0,g)),pl.BlockSpec((T,128),lambda g:(0,g)),
                  pl.BlockSpec((T,256),lambda g:(0,g)),pl.BlockSpec((1,8,T),lambda g:(g,0,0)),pl.BlockSpec((T,D),full),pl.BlockSpec((D,wide),full)],
        out_specs=[pl.BlockSpec((D,width),full),pl.BlockSpec((T,D),full)],
        out_shape=[jax.ShapeDtypeStruct((D,width),BF),jax.ShapeDtypeStruct((T,D),BF)],
        scratch_shapes=[pltpu.VMEM((T,D),BF),pltpu.VMEM((T,T),F32),pltpu.VMEM((T,D),F32)],
        compiler_params=pltpu.CompilerParams(vmem_limit_bytes=60<<20),
        cost_estimate=COST,
        name="attend_back")(h,w,w,w,w,cos,sin,segc,segr,q,k,v,dmix,lse,dres,og)

def rope_tables(segment_row):
    index = jnp.arange(segment_row.shape[0], dtype=jnp.int32)
    earlier = (segment_row[:, None] == segment_row[None, :]) & (index[None, :] < index[:, None])
    position = jnp.sum(earlier.astype(jnp.int32), axis=-1).astype(F32)
    frequency = rope_base ** (-jnp.arange(HALF, dtype=F32) / HALF)
    angles = position[:, None] * frequency[None, :]
    cosine = jnp.cos(angles)
    sine = jnp.sin(angles)
    return (
        jnp.concatenate([cosine] * 4, axis=1),
        jnp.concatenate([-sine, sine, -sine, sine], axis=1),
    )


def pad_columns(values):
    return jnp.pad(values, ((0, 0), (0, -values.shape[1] % 128)))


def body(
    hidden,
    segment_ids,
    routes,
    norm_attn,
    w_query,
    key_weight,
    value_weight,
    w_out,
    norm_moe,
    w_router,
    w_gate,
    w_up,
    w_down,
    cotangent,
):
    tokens, width = hidden.shape
    own_rows = w_query.shape[0]
    owned = w_gate.shape[0]
    peers = lax.axis_size("expert")
    me = lax.axis_index("expert")
    chips = peers // 2
    chip_order = (me // 2 - jnp.arange(chips, dtype=jnp.int32)) % chips
    core_order = (me % 2) ^ jnp.arange(2, dtype=jnp.int32)
    order = (chip_order[:, None] * 2 + core_order[None, :]).reshape(-1)
    dp_count = lax.axis_size("dp")
    dp_order = lax.axis_index("dp") ^ jnp.arange(dp_count, dtype=jnp.int32)
    places = (
        (chip_order[None, None, :] * 2 + core_order[None, :, None]) * dp_count
        + dp_order[:, None, None]
    ).reshape(-1)
    first_pack = pad_columns(
        jnp.concatenate(
            [
                w_query,
                key_weight,
                value_weight,
                norm_attn[:, None],
                norm_moe[:, None],
            ],
            axis=1,
        )
    )
    second_pack = pad_columns(jnp.concatenate([w_out, w_router], axis=1))
    cotangent_steps = [cotangent]
    routes_shifts = all_shifts(routes.astype(BF).reshape(-1, 128))
    shifts_one = all_shifts(own_slice(first_pack))
    shifts_one, routes_shifts, second_slice, cotangent_steps = tie(
        shifts_one, routes_shifts, own_slice(second_pack), cotangent_steps
    )
    shifts_two = all_shifts(second_slice)
    stack_one = jnp.stack(shifts_one)
    slices_one = [stack_one] + [swap_dp(stack_one, r) for r in range(1, dp_count)]
    cotangent_steps.append(shift_chips(cotangent_steps[0], 1))
    routes_all = []
    for s in routes_shifts:
        routes_all += [s, swap_pair(s)]
    routes_all = jnp.stack(routes_all).astype(jnp.int32).reshape(peers, tokens, TOP)
    expert_ids = jnp.arange(EXPERTS, dtype=jnp.int32)
    member_all = jnp.any(routes_all[:, None, :, :] == expert_ids[:, None, None], axis=3)
    first_expert = me * owned
    member_own = lax.dynamic_slice_in_dim(member_all, first_expert, owned, 1)
    index = jnp.arange(tokens, dtype=jnp.int32)
    before = (index[:, None] < index[None, :]).astype(BF)
    rank = jnp.einsum(
        "sjt,tu->sju", member_own.astype(BF), before, preferred_element_type=F32
    ).astype(jnp.int32)
    rank = jnp.where(member_own, rank, -1)
    first_slot = jnp.arange(owned, dtype=jnp.int32)[:, None] * CAP
    keys = jnp.swapaxes(jnp.where(member_own, rank + first_slot, -1), 1, 2)
    rank_rows = jnp.swapaxes(rank, 0, 1)[:, :, None, :]
    member_all = member_all.astype(F32)
    member_line = jnp.any(routes[None, :, :] == expert_ids[:, None, None], axis=2).astype(F32)
    segment_row = segment_ids[0]
    cosine, sine = rope_tables(segment_row)
    segment_column = segment_row[:, None]
    segment_line = segment_row[None, :]
    from_chip = (me // 2 + jnp.arange(chips, dtype=jnp.int32)) % chips
    from_order = (from_chip[:, None] * 2 + core_order[None, :]).reshape(-1)
    from_order = jnp.argsort(from_order)
    tables = [rank_rows, keys, member_all, member_line, cosine, sine, from_order]
    tables, slices_one, shifts_two = tie(tables, slices_one, shifts_two)
    rank_rows, keys, member_all, member_line, cosine, sine, from_order = tables
    pieces_one = []
    for s in slices_one:
        pieces_one += [s, swap_pair(s)]
    pieces_one, shifts_two, cotangent_steps = tie(pieces_one, shifts_two, cotangent_steps)
    for k in range(2, min(chips, 3)):
        cotangent_steps.append(shift_chips(cotangent_steps[k - 1], 1))
    stack_two = jnp.stack(shifts_two)
    slices_two = [stack_two] + [swap_dp(stack_two, r) for r in range(1, dp_count)]
    attn_weights = assemble(places, pieces_one)
    attn_weights, slices_two, cotangent_steps = tie(attn_weights, slices_two, cotangent_steps)
    pieces_two = []
    for s in slices_two:
        pieces_two += [s, swap_pair(s)]
    for k in range(3, chips):
        cotangent_steps.append(shift_chips(cotangent_steps[k - 1], 1))
    cotangent_pairs = [swap_pair(c) for c in cotangent_steps[: chips - 1]]
    kv_heads = key_weight.shape[1] // (2 * HALF)
    query, key, value, mixed, lse = attend(
        0, hidden, attn_weights, cosine, sine, segment_column, segment_line, kv_heads
    )
    mixed, pieces_two, cotangent_steps, cotangent_pairs = tie(
        mixed, pieces_two, cotangent_steps, cotangent_pairs
    )
    out_weights = assemble(places, pieces_two)
    residual, moe_in = project(1, mixed, out_weights, hidden, attn_weights)
    cotangent_pairs.append(swap_pair(cotangent_steps[-1]))
    x = [moe_in, swap_pair(moe_in)]
    x, moe_in = tie(x, moe_in)
    kept = None
    dots = []
    grad_parts = []
    out_parts = []
    hop = None
    for k in range(chips):
        following = shift_chips(x[0], 1) if k + 1 < chips else None
        if k == 3:
            hop = shift_chips(grad_parts[1], 1)
        outs = list(
            expert_step(
                k,
                first_expert[None],
                x,
                (cotangent_steps[k], cotangent_pairs[k]),
                out_weights,
                member_all,
                rank_rows,
                keys,
                w_gate,
                w_up,
                w_down,
                kept,
            )
        )
        kept = outs[5:]
        outs = outs[:5]
        outs, kept, following, hop, dots, grad_parts, out_parts = tie(
            outs, kept, following, hop, dots, grad_parts, out_parts
        )
        if following is not None:
            x = [following, swap_pair(following)]
        grad_part = (outs[0].astype(F32) + swap_pair(outs[1]).astype(F32)).astype(BF)
        out_parts = out_parts + [(outs[2], outs[3])]
        dots = dots + [outs[4]]
        if k + 1 < chips:
            x, grad_part = tie(x, grad_part)
        grad_parts = grad_parts + [grad_part]
    dp_me = lax.axis_index("dp")
    low = dp_me % 2
    high = dp_me // 2
    count = (owned + 1) // 2
    plans = [(0, count, 1, 2, low, high)]
    if owned > count:
        plans.append((count, owned - count, 2, 1, high, low))
    returned = [send_back(dots[k][:, b, 0], k, b) for k in range(chips) for b in range(2)]
    total = grad_parts[1]
    first_hop = 2
    if hop is not None:
        total, kept = tie((grad_parts[2].astype(F32) + hop.astype(F32)).astype(BF), kept)
        first_hop = 3
    halves = []
    gots = []
    for number, k in enumerate(range(first_hop, chips + 1)):
        moved = shift_chips(total, 1)
        if number < len(plans):
            first_of, many, one, two, bit_one, bit_two = plans[number]
            send, keep = weight_grads(bit_one[None], first_of, many, kept)
            halves.append((first_of, one, two, bit_one, bit_two, keep))
            moved, send, kept = tie(moved, send, kept)
            gots.append(swap_dp(send, one))
        if k < chips:
            total = (grad_parts[k].astype(F32) + moved.astype(F32)).astype(BF)
            total, kept = tie(total, kept)
    moe_grad = (grad_parts[0].astype(F32) + moved.astype(F32)).astype(BF)
    moe_grad, returned, out_parts = tie(moe_grad, returned, out_parts)
    out_parts = [(a.astype(F32) + swap_pair(b).astype(F32)).astype(BF) for a, b in out_parts]
    token_dot = jnp.stack(returned)[from_order].reshape(EXPERTS, tokens)
    grad_residual, mixed_gradient, out_grads = branch(
        1, moe_grad, residual, moe_in, mixed, cotangent, out_weights, attn_weights, member_line, token_dot
    )
    mixed_gradient, out_parts = tie(mixed_gradient, out_parts)
    out_sum = shift_chips(out_parts[1], 1)
    attn_grads, grad_input = attend_back(
        0,
        hidden,
        attn_weights,
        cosine,
        sine,
        segment_column,
        segment_line,
        query,
        key,
        value,
        mixed_gradient,
        lse,
        grad_residual,
        out_grads,
    )
    attn_grads, out_sum, gots = tie(attn_grads, out_sum, gots)

    def block_for(k, b):
        number = chip_order[k] * 2 + core_order[b]
        return lax.dynamic_slice_in_dim(attn_grads, number * own_rows, own_rows, 0)

    seconds = []
    keeps = []
    for (first_of, one, two, bit_one, bit_two, keep), got in zip(halves, gots):
        send, keep = halve(bit_two[None], keep, got)
        seconds.append(send)
        keeps.append(keep)
    parts = [(block_for(k, 0), swap_pair(block_for(k, 1))) for k in range(chips)]
    out_sum = (out_parts[2].astype(F32) + out_sum.astype(F32)).astype(BF)
    seconds, keeps, parts, out_sum = tie(seconds, keeps, parts, out_sum)
    parts = [(a.astype(F32) + b.astype(F32)).astype(BF) for a, b in parts]
    gots = [swap_dp(send, h[2]) for h, send in zip(halves, seconds)]
    running = shift_chips(parts[1], 1)
    gots, running = tie(gots, running)
    mine = [(k.astype(F32) + g.astype(F32)).astype(BF) for k, g in zip(keeps, gots)]
    running = (parts[2].astype(F32) + running.astype(F32)).astype(BF)
    mine, running, out_sum = tie(mine, running, out_sum)
    others = [swap_dp(m, h[2]) for h, m in zip(halves, mine)]
    running = shift_chips(running, 1)
    others, running, mine = tie(others, running, mine)
    thirds = [swap_dp(m, h[1]) for h, m in zip(halves, mine)]
    out_sum = shift_chips(out_sum, 1)
    for k in [*range(3, chips), 0]:
        running = (parts[k].astype(F32) + running.astype(F32)).astype(BF)
        if k:
            running = shift_chips(running, 1)
    part, thirds, others, mine, out_sum = tie(running, thirds, others, mine, out_sum)
    for o in out_parts[3:]:
        out_sum = shift_chips((o.astype(F32) + out_sum.astype(F32)).astype(BF), 1)
    result = (residual + out_parts[0].astype(F32) + out_sum.astype(F32)).astype(BF)
    sub = own_rows // dp_count

    def rows_of(r):
        return (dp_me ^ r) * sub

    fourths = [swap_dp(o, h[1]) for h, o in zip(halves, others)]
    sent = [lax.dynamic_slice_in_dim(part, rows_of(r), sub, 0) for r in range(dp_count)]
    received = [sent[0]] + [swap_dp(sent[r], r) for r in range(1, dp_count)]
    held = None
    for (first_of, one, two, bit_one, bit_two, _), m, other, third in zip(
        halves, mine, others, thirds
    ):
        held = place_quarter(first_of, owned, jnp.stack([bit_one, bit_two]), m, held)
        held = place_quarter(first_of, owned, jnp.stack([bit_one, 1 - bit_two]), other, held)
        held = place_quarter(first_of, owned, jnp.stack([1 - bit_one, bit_two]), third, held)
    held, received = tie(held, received)
    total = received[0].astype(F32)
    for piece in received[1:]:
        total = total + piece.astype(F32)
    total = total.astype(BF)
    pieces = [swap_dp(total, r) if r else total for r in range(dp_count)]
    for (first_of, one, two, bit_one, bit_two, _), fourth in zip(halves, fourths):
        held = place_quarter(first_of, owned, jnp.stack([1 - bit_one, 1 - bit_two]), fourth, held)
    big = held
    share = place_share(jnp.stack([rows_of(r) for r in range(dp_count)]), pieces)
    groups = share[:, : 2 * width].reshape(own_rows, -1, 512)
    out_share = share[:, 2 * width :]
    return (
        result,
        grad_input,
        share[:, -128],
        groups[:, :, :256].reshape(own_rows, -1),
        groups[:, :, 256:384].reshape(own_rows, -1),
        groups[:, :, 384:].reshape(own_rows, -1),
        out_share[:, :width],
        out_share[:, width + EXPERTS],
        out_share[:, width : width + EXPERTS],
        big[0],
        big[1],
        big[2],
    )


def solution(mesh):
    in_specs = (
        P(("dp", "expert"), None),
        P(("dp", "expert"), None),
        P(("dp", "expert"), None),
        P("expert"),
        P("expert", None),
        P("expert", None),
        P("expert", None),
        P("expert", None),
        P("expert"),
        P("expert", None),
        P("expert", None, None),
        P("expert", None, None),
        P("expert", None, None),
        P(("dp", "expert"), None),
    )
    out_specs = (
        P(("dp", "expert"), None),
        P(("dp", "expert"), None),
        P("expert"),
        P("expert", None),
        P("expert", None),
        P("expert", None),
        P("expert", None),
        P("expert"),
        P("expert", None),
        P("expert", None, None),
        P("expert", None, None),
        P("expert", None, None),
    )
    return jax.shard_map(body, mesh=mesh, in_specs=in_specs, out_specs=out_specs, check_vma=False)
```

```python
import functools

import jax
import jax.numpy as jnp
from jax import lax
from jax.experimental import pallas as pl
from jax.experimental.pallas import tpu as pltpu
from jax.sharding import PartitionSpec as P

EXPERTS = 32
TOP = 8
CAP = 192
HALF = 32
ROWS = 256
MISC = 16
F32 = jnp.float32
BF = jnp.bfloat16
COST = pl.CostEstimate(flops=1 << 20, bytes_accessed=1 << 20, transcendentals=0)
norm_eps = 1e-06
rope_base = 10000.0


def dot(a,b,ca=1,cb=0):
    return lax.dot_general(a,b,(((ca,),(cb,)),((),())),preferred_element_type=F32)

def step_kernel(aliased, *refs):
    (first_ref, x0_ref, x1_ref, d0_ref, d1_ref, r_ref, m_ref, rank_ref, key_ref,
     wg_ref, wu_ref, wd_ref) = refs[:12]
    (g0_ref, g1_ref, o0_ref, o1_ref, xs_ref, ge_ref, hs_ref, dgs_ref, dus_ref,
     t_s, gate_s, rg_s, ro_s, dot_s) = refs[12 + aliased:]
    owned = gate_s.shape[0]
    E = m_ref.shape[1]
    T = x0_ref.shape[0]
    e = pl.program_id(0)
    x_refs = (x0_ref, x1_ref)
    d_refs = (d0_ref, d1_ref)

    @pl.when(e == 0)
    def _():
        for q in range(2):
            t_s[...] = dot(x_refs[q][...], r_ref[...]).T
            mem = m_ref[q] > 0.5
            kept = jnp.where(mem, t_s[:E, :], -1e30)
            ex = jnp.where(mem, jnp.exp(kept - jnp.max(kept, axis=0, keepdims=True)), 0.0)
            t_s[:E, :] = ex / jnp.sum(ex, axis=0, keepdims=True)
            for j in range(owned):
                gate_s[j, q] = t_s[pl.ds(first_ref[0] + j, 1), :]

    slot = lax.broadcasted_iota(jnp.int32, (CAP, T), 0)
    gs = []
    hits = []
    ds = []
    for q in range(2):
        rows = slice(q * CAP, (q + 1) * CAP)
        hit = slot == rank_ref[0, q]
        S = jnp.where(hit, 1.0, 0.0).astype(BF)
        xs_ref[0, rows, :] = dot(S, x_refs[q][...]).astype(BF)
        d = dot(S, d_refs[q][...])
        g = jnp.sum(jnp.where(hit, gate_s[e, q], 0.0), axis=1, keepdims=True)
        ge_ref[0, rows, :] = (g * d).astype(BF)
        gs.append(g)
        hits.append(hit)
        ds.append(d.astype(BF))
    x = xs_ref[0]
    gl = dot(x, wg_ref[0])
    ul = dot(x, wu_ref[0])
    sg = jax.nn.sigmoid(gl)
    act = gl * sg
    h = (act * ul).astype(BF)
    hs_ref[0] = h
    eo = dot(h, wd_ref[0]).astype(BF)
    for q in range(2):
        part = eo[q * CAP : (q + 1) * CAP].astype(F32)
        ro_s[q, pl.ds(pl.multiple_of(e * CAP, CAP), CAP), :] = (gs[q] * part).astype(BF)
        sd = jnp.sum(part * ds[q].astype(F32), axis=1, keepdims=True)
        dot_s[e, q] = jnp.sum(jnp.where(hits[q], sd, 0.0), axis=0, keepdims=True)
    dh = dot(ge_ref[0], wd_ref[0], 1, 1)
    dgl = (dh * ul * sg * (1.0 + gl * (1.0 - sg))).astype(BF)
    dul = (dh * act).astype(BF)
    dgs_ref[0] = dgl
    dus_ref[0] = dul
    dr = (dot(dgl, wg_ref[0], 1, 1) + dot(dul, wu_ref[0], 1, 1)).astype(BF)
    for q in range(2):
        rg_s[q, pl.ds(pl.multiple_of(e * CAP, CAP), CAP), :] = dr[q * CAP : (q + 1) * CAP]

    @pl.when(e == owned - 1)
    def _():
        lane = lax.broadcasted_iota(jnp.int32, (T, owned * CAP), 1)
        for q, g_ref, o_ref in ((0, g0_ref, o0_ref), (1, g1_ref, o1_ref)):
            keys = key_ref[q]
            hit = lane == keys[:, 0:1]
            for j in range(1, owned):
                hit = hit | (lane == keys[:, j : j + 1])
            S = jnp.where(hit, 1.0, 0.0).astype(BF)
            g_ref[:T, :] = dot(S, rg_s[q]).astype(BF)
            half = E // 2
            row = lax.broadcasted_iota(jnp.int32, (half, 2 * T), 0)
            column = lax.broadcasted_iota(jnp.int32, (half, 2 * T), 1)
            dots = jnp.zeros((half, 2 * T), F32)
            for j in range(owned):
                number = first_ref[0] + j
                here = (row == number % half) & (column // T == number // half)
                twice = jnp.concatenate([dot_s[j, q], dot_s[j, q]], axis=1)
                dots = jnp.where(here, twice, dots)
            high = dots.astype(BF)
            g_ref[T : T + half, :] = high
            g_ref[T + half :, :] = (dots - high.astype(F32)).astype(BF)
            o_ref[...] = dot(S, ro_s[q]).astype(BF)


def expert_step(k, first, x, d, router, member, rank, keys, wg, wu, wd, kept):
    owned, peers, _, T = rank.shape
    D, F = wg.shape[1:]
    E = member.shape[1]
    M = 2 * CAP
    rows = peers * CAP
    full = lambda e, f: (0, 0)
    shapes = [
        jax.ShapeDtypeStruct((owned, rows, D), BF),
        jax.ShapeDtypeStruct((owned, rows, D), BF),
    ] + [jax.ShapeDtypeStruct((owned, rows, F), BF)] * 3
    token = jax.ShapeDtypeStruct((T, D), BF)
    longer = jax.ShapeDtypeStruct((T + E, D), BF)
    assert 2 * T == D
    aliased = 0 if kept is None else len(shapes)
    return pl.pallas_call(
        functools.partial(step_kernel, aliased),
        grid_spec=pltpu.PrefetchScalarGridSpec(
            num_scalar_prefetch=1,
            grid=(owned,),
            in_specs=[pl.BlockSpec((T, D), full)] * 4
            + [
                pl.BlockSpec((D, 128), lambda e, f: (0, D // 128)),
                pl.BlockSpec((2, E, T), lambda e, f: (k, 0, 0)),
                pl.BlockSpec((1, 2, 1, T), lambda e, f: (e, k, 0, 0)),
                pl.BlockSpec((2, T, owned), lambda e, f: (k, 0, 0)),
                pl.BlockSpec((1, D, F), lambda e, f: (e, 0, 0)),
                pl.BlockSpec((1, D, F), lambda e, f: (e, 0, 0)),
                pl.BlockSpec((1, F, D), lambda e, f: (e, 0, 0)),
            ]
            + [pl.BlockSpec(memory_space=pl.ANY)] * aliased,
            out_specs=[pl.BlockSpec((T + E, D), full)] * 2
            + [pl.BlockSpec((T, D), full)] * 2
            + [pl.BlockSpec((1, M, s.shape[2]), lambda e, f: (e, k, 0)) for s in shapes],
            scratch_shapes=[
                pltpu.VMEM((128, T), F32),
                pltpu.VMEM((owned, 2, 1, T), F32),
                pltpu.VMEM((2, owned * CAP, D), BF),
                pltpu.VMEM((2, owned * CAP, D), BF),
                pltpu.VMEM((owned, 2, 1, T), F32),
            ],
        ),
        out_shape=[longer] * 2 + [token] * 2 + shapes,
        input_output_aliases={12 + i: 4 + i for i in range(aliased)},
        compiler_params=pltpu.CompilerParams(vmem_limit_bytes=60 << 20),
        cost_estimate=COST,
        name="expert_step",
    )(first, *x, *d, router, member, rank, keys, wg, wu, wd, *(kept or ()))


def weight_kernel(parts, bit_ref, xs_ref, ge_ref, hs_ref, dgs_ref, dus_ref, send_ref, keep_ref, *acc):
    at = pl.program_id(1)
    half = xs_ref.shape[2] // 2
    for n, o_ref in enumerate((send_ref, keep_ref)):
        bit = 1 - bit_ref[0] if n == 0 else bit_ref[0]
        off = pl.multiple_of(bit * half, half)
        x = xs_ref[0, :, pl.ds(off, half)]
        totals = (
            dot(x, dgs_ref[0], 0, 0),
            dot(x, dus_ref[0], 0, 0),
            dot(hs_ref[0], ge_ref[0, :, pl.ds(off, half)], 0, 0),
        )
        for i, total in enumerate(totals):
            if parts > 1:
                s = acc[0].at[3 * n + i]
                total = jnp.where(at == 0, 0.0, s[...]) + total
                s[...] = total
            o_ref[0, i] = total.astype(BF)


def weight_grads(bit, first, count, kept):
    rows, D = kept[0].shape[1:]
    F = kept[2].shape[2]
    half = D // 2
    assert half == F
    block = min(rows, 8 * CAP)
    parts = rows // block
    out = jax.ShapeDtypeStruct((count, 3, half, F), BF)
    return pl.pallas_call(
        functools.partial(weight_kernel, parts),
        grid_spec=pltpu.PrefetchScalarGridSpec(
            num_scalar_prefetch=1,
            grid=(count, parts),
            in_specs=[
                pl.BlockSpec((1, block, s.shape[2]), lambda e, i, b: (first + e, i, 0)) for s in kept
            ],
            out_specs=[pl.BlockSpec((1, 3, half, F), lambda e, i, b: (e, 0, 0, 0))] * 2,
            scratch_shapes=[pltpu.VMEM((6, half, F), F32)] if parts > 1 else [],
        ),
        out_shape=[out, out],
        compiler_params=pltpu.CompilerParams(vmem_limit_bytes=60 << 20),
        cost_estimate=COST,
        name="weight_grads",
    )(bit, *kept)


def halve_kernel(bit_ref, keep_ref, got_ref, send_ref, kept_ref):
    half = send_ref.shape[2]
    for n, o_ref in enumerate((send_ref, kept_ref)):
        bit = 1 - bit_ref[0] if n == 0 else bit_ref[0]
        rows = pl.ds(pl.multiple_of(bit * half, half), half)
        for i in range(keep_ref.shape[1]):
            o_ref[0, i] = (
                keep_ref[0, i, rows, :].astype(F32) + got_ref[0, i, rows, :].astype(F32)
            ).astype(BF)


def halve(bit, keep, got):
    count, mats, rows, F = keep.shape
    full = pl.BlockSpec((1, mats, rows, F), lambda e, b: (e, 0, 0, 0))
    part = pl.BlockSpec((1, mats, rows // 2, F), lambda e, b: (e, 0, 0, 0))
    out = jax.ShapeDtypeStruct((count, mats, rows // 2, F), BF)
    return pl.pallas_call(
        halve_kernel,
        grid_spec=pltpu.PrefetchScalarGridSpec(
            num_scalar_prefetch=1, grid=(count,), in_specs=[full, full], out_specs=[part, part]
        ),
        out_shape=[out, out],
        cost_estimate=COST,
        name="halve",
    )(bit, keep, got)


def place_kernel(counts, bits_ref, *refs):
    ins, (gg_ref, gu_ref, gd_ref) = refs[:-3], refs[-3:]
    e = pl.program_id(0)
    begin = 0
    for n, many in enumerate(counts):

        @pl.when((e >= begin) & (e < begin + many))
        def _(n=n):
            for i in range(4):
                q_ref = ins[4 * n + i]
                rows, half = q_ref.shape[2:]
                one = bits_ref[2 * n] if i < 2 else 1 - bits_ref[2 * n]
                two = bits_ref[2 * n + 1] if i % 2 == 0 else 1 - bits_ref[2 * n + 1]
                at = pl.ds(pl.multiple_of((2 * one + two) * rows, rows), rows)
                gg_ref[0, at, :] = q_ref[0, 0].astype(F32)
                gu_ref[0, at, :] = q_ref[0, 1].astype(F32)
                at = pl.ds(pl.multiple_of(two * rows, rows), rows)
                columns = pl.ds(pl.multiple_of(one * half, half), half)
                gd_ref[0, at, columns] = q_ref[0, 2].astype(F32)

        begin += many


def place_all(bits, quarters):
    counts = [q[0].shape[0] for q in quarters]
    owned = sum(counts)
    _, _, rows, F = quarters[0][0].shape
    D = 4 * rows
    specs = []
    begin = 0
    for many in counts:
        block = lambda e, b, begin=begin, many=many: (jnp.clip(e - begin, 0, many - 1), 0, 0, 0)
        specs += [pl.BlockSpec((1, 3, rows, F), block)] * 4
        begin += many
    shapes = [(D, F), (D, F), (F, D)]
    return pl.pallas_call(
        functools.partial(place_kernel, counts),
        grid_spec=pltpu.PrefetchScalarGridSpec(
            num_scalar_prefetch=1,
            grid=(owned,),
            in_specs=specs,
            out_specs=[pl.BlockSpec((1,) + s, lambda e, b: (e, 0, 0)) for s in shapes],
        ),
        out_shape=[jax.ShapeDtypeStruct((owned,) + s, F32) for s in shapes],
        compiler_params=pltpu.CompilerParams(vmem_limit_bytes=60 << 20),
        cost_estimate=COST,
        name="place_all",
    )(bits, *[q for group in quarters for q in group])


def assemble_kernel(place,p_ref,*refs):
    ins=refs[:-2]; o_ref,sem=refs[-2:]
    copies=[]
    for n,r in enumerate(ins):
        chips,sub,_=r.shape
        for k in range(chips):
            row=pl.multiple_of(p_ref[n*chips+k]*sub,sub)
            copies.append(pltpu.make_async_copy(r.at[k],o_ref.at[pl.ds(row,sub),:],sem.at[n*chips+k]))
    for c in copies: c.start()
    for c in copies: c.wait()

def assemble(places,pieces):
    n=len(pieces); chips,sub,W=pieces[0].shape
    return pl.pallas_call(functools.partial(assemble_kernel,None),
        grid_spec=pltpu.PrefetchScalarGridSpec(num_scalar_prefetch=1,grid=(1,),
          in_specs=[pl.BlockSpec(memory_space=pl.ANY)]*n,
          out_specs=pl.BlockSpec((n*chips*sub,W),lambda i,p:(0,0)),
          scratch_shapes=[pltpu.SemaphoreType.DMA((n*chips,))]),
        out_shape=jax.ShapeDtypeStruct((n*chips*sub,W),BF),cost_estimate=COST,
        compiler_params=pltpu.CompilerParams(vmem_limit_bytes=40<<20),
        name="assemble")(places,*pieces)

def ring_steps(v):
    n=lax.axis_size("expert")
    ring=[(i,(i+2)%n) for i in range(n)]
    blocks=[v]
    for _ in range(n//2-1):
        blocks.append(lax.ppermute(blocks[-1],"expert",ring))
    return blocks

def swap_pair(v):
    return lax.ppermute(v,"expert",[(i,i^1) for i in range(lax.axis_size("expert"))])

def swap_dp(v,r):
    return lax.ppermute(v,"dp",[(i,i^r) for i in range(lax.axis_size("dp"))])

def shift_chips(v,k):
    n=lax.axis_size("expert")
    return lax.ppermute(v,"expert",[(i,(i+2*k)%n) for i in range(n)])

def ring_gather(v):
    blocks=[]
    for b in ring_steps(v):
        blocks+=[b,swap_pair(b)]
    return blocks

def all_shifts(v):
    return [v]+[shift_chips(v,k) for k in range(1,lax.axis_size("expert")//2)]

def share_kernel(count, rows_ref, *refs):
    q_ref, k_ref, v_ref, o_ref, r_ref, m_ref, a_ref, s_ref, g_ref = refs[count:]
    D = q_ref.shape[1]
    groups = D // 256
    for r, piece in enumerate(refs[:count]):
        sub = piece.shape[0]
        rows = pl.ds(pl.multiple_of(rows_ref[r], sub), sub)
        for g in range(groups):
            at = 512 * g
            q_ref[rows, 256 * g : 256 * g + 256] = piece[:, at : at + 256].astype(F32)
            k_ref[rows, 128 * g : 128 * g + 128] = piece[:, at + 256 : at + 384].astype(F32)
            v_ref[rows, 128 * g : 128 * g + 128] = piece[:, at + 384 : at + 512].astype(F32)
        at = 512 * groups
        o_ref[rows, :] = piece[:, at : at + D].astype(F32)
        s_ref[rows, :] = piece[:, at + D : at + D + 128].astype(F32)
        g_ref[rows, :] = piece[:, at + D + 128 : at + D + 256].astype(F32)
    E = r_ref.shape[1]
    r_ref[...] = s_ref[:, :E]
    m_ref[...] = s_ref[...].T[E : E + 1, :]
    a_ref[...] = g_ref[...].T[:1, :]


def place_share(rows, pieces, D, kv):
    sub, W = pieces[0].shape
    n = len(pieces)
    assert W == 2 * D + 2 * kv + 256 and D // 256 == kv // 128
    shapes = [(n * sub, w) for w in (D, kv, kv, D, EXPERTS)] + [(1, n * sub)] * 2
    return pl.pallas_call(
        functools.partial(share_kernel, n),
        grid_spec=pltpu.PrefetchScalarGridSpec(
            num_scalar_prefetch=1,
            grid=(1,),
            in_specs=[pl.BlockSpec((sub, W), lambda i, r: (0, 0))] * n,
            out_specs=[pl.BlockSpec(s, lambda i, r: (0, 0)) for s in shapes],
            scratch_shapes=[pltpu.VMEM((n * sub, 128), F32)] * 2,
        ),
        out_shape=[jax.ShapeDtypeStruct(s, F32) for s in shapes],
        cost_estimate=COST,
        name="place_share",
    )(rows, *pieces)


def own_slice(pack):
    dp=lax.axis_size("dp")
    sub=pack.shape[0]//dp
    return lax.dynamic_slice_in_dim(pack,lax.axis_index("dp")*sub,sub,0)

def tie(*values):
    return lax.optimization_barrier(values)

def rotate(v):
    lane=lax.broadcasted_iota(jnp.int32,v.shape,1)
    width=v.shape[1]
    return jnp.where(lane%(2*HALF)<HALF,pltpu.roll(v,width-HALF,1),pltpu.roll(v,HALF,1))

def spread(v):
    lane=lax.broadcasted_iota(jnp.int32,v.shape,1)
    low=lane<2*HALF
    other=pltpu.roll(v,2*HALF,1)
    zero=jnp.zeros_like(v)
    return [jnp.where(low,v,zero).astype(BF),jnp.where(low,zero,other).astype(BF),
            jnp.where(low,other,zero).astype(BF),jnp.where(low,zero,v).astype(BF)]

def gain_row(misc_ref,which):
    return misc_ref[...].astype(F32).T[which:which+1,:]

def attend_kernel(gain_at,h_ref,misc_ref,wq_ref,wk_ref,wv_ref,cos_ref,sin_ref,segc_ref,segr_ref,
                  q_ref,k_ref,v_ref,mix_ref,lse_ref,x_s,bias_s):
    T=h_ref.shape[0]
    @pl.when(pl.program_id(0)==0)
    def _():
        inputs=h_ref[...].astype(F32)
        inv=lax.rsqrt(jnp.mean(inputs*inputs,axis=-1,keepdims=True)+norm_eps)
        x_s[...]=(inputs*inv*gain_row(misc_ref,gain_at)).astype(BF)
        r=lax.broadcasted_iota(jnp.int32,(T,T),0); c=lax.broadcasted_iota(jnp.int32,(T,T),1)
        bias_s[...]=jnp.where((segc_ref[...]==segr_ref[...])&(c<=r),0.0,-1e30)
    x=x_s[...]
    cos=cos_ref[...]; sin=sin_ref[...]
    ql=dot(x,wq_ref[...])
    qs=[]
    for c in range(2):
        part=ql[:,128*c:128*c+128]
        part=part*cos+rotate(part)*sin
        q_ref[:,128*c:128*c+128]=part.astype(BF)
        qs.append((part.astype(BF).astype(F32)*0.125).astype(BF))
    kl=dot(x,wk_ref[...])
    kl=(kl*cos+rotate(kl)*sin).astype(BF)
    k_ref[...]=kl
    vl=dot(x,wv_ref[...]).astype(BF)
    v_ref[...]=vl
    kp=spread(kl.astype(F32)); vp=spread(vl.astype(F32))
    lane=lax.broadcasted_iota(jnp.int32,(ROWS,128),1)
    for b in range(T//ROWS):
        rows=slice(b*ROWS,(b+1)*ROWS); nk=(b+1)*ROWS
        lse=jnp.zeros((ROWS,128),F32)
        for c in range(2):
            o=None
            for half in range(2):
                i=2*c+half
                s=dot(qs[c][rows],kp[i][:nk],1,1)+bias_s[rows,:nk]
                m=jnp.max(s,axis=1,keepdims=True)
                e=jnp.exp(s-m)
                l=jnp.sum(e,axis=1,keepdims=True)
                p=(e*(1.0/l)).astype(BF)
                part=dot(p,vp[i][:nk])
                o=part if o is None else o+part
                lse=jnp.where(lane==i,m+jnp.log(l),lse)
            mix_ref[rows,128*c:128*c+128]=o.astype(BF)
        lse_ref[0,:,rows]=lse.T[:8,:]

def attend(gain_at,h,w,cos,sin,segc,segr,kv_heads):
    T,D=h.shape
    steps=kv_heads//2
    full=lambda g:(0,0)
    qb=D//256; kb=D//128; vb=kb+kv_heads//2; mb=vb+kv_heads//2
    return pl.pallas_call(functools.partial(attend_kernel,gain_at),grid=(steps,),
        in_specs=[pl.BlockSpec((T,D),full),pl.BlockSpec((D,128),lambda g:(0,mb)),
                  pl.BlockSpec((D,256),lambda g:(0,g)),pl.BlockSpec((D,128),lambda g:(0,kb+g)),pl.BlockSpec((D,128),lambda g:(0,vb+g)),
                  pl.BlockSpec((T,128),full),pl.BlockSpec((T,128),full),pl.BlockSpec((T,1),full),pl.BlockSpec((1,T),full)],
        out_specs=[pl.BlockSpec((T,256),lambda g:(0,g)),pl.BlockSpec((T,128),lambda g:(0,g)),pl.BlockSpec((T,128),lambda g:(0,g)),
                   pl.BlockSpec((T,256),lambda g:(0,g)),pl.BlockSpec((1,8,T),lambda g:(g,0,0))],
        out_shape=[jax.ShapeDtypeStruct((T,D),BF),jax.ShapeDtypeStruct((T,64*kv_heads),BF),jax.ShapeDtypeStruct((T,64*kv_heads),BF),
                   jax.ShapeDtypeStruct((T,D),BF),jax.ShapeDtypeStruct((steps,8,T),F32)],
        scratch_shapes=[pltpu.VMEM((T,D),BF),pltpu.VMEM((T,T),F32)],
        cost_estimate=COST,
        name="attend")(h,w,w,w,w,cos,sin,segc,segr)


def project_kernel(gain_at,m_ref,w_ref,h_ref,misc_ref,res_ref,moe_ref):
    res=h_ref[...].astype(F32)+dot(m_ref[...],w_ref[...])
    res_ref[...]=res
    inv=lax.rsqrt(jnp.mean(res*res,axis=-1,keepdims=True)+norm_eps)
    moe_ref[...]=(res*inv*gain_row(misc_ref,gain_at)).astype(BF)

def project(gain_at,mixed,w2,h,w1):
    T,D=h.shape
    R=256
    return pl.pallas_call(functools.partial(project_kernel,gain_at),grid=(T//R,),
        in_specs=[pl.BlockSpec((R,D),lambda i:(i,0)),pl.BlockSpec((D,D),lambda i:(0,0)),pl.BlockSpec((R,D),lambda i:(i,0)),
                  pl.BlockSpec((D,128),lambda i:(0,MISC))],
        out_specs=[pl.BlockSpec((R,D),lambda i:(i,0)),pl.BlockSpec((R,D),lambda i:(i,0))],
        out_shape=[jax.ShapeDtypeStruct((T,D),F32),jax.ShapeDtypeStruct((T,D),BF)],
        cost_estimate=COST,
        name="project")(mixed,w2,h,w1)

def branch_kernel(gain_at,mg_ref,res_ref,moe_ref,mix_ref,cot_ref,wo_ref,r_ref,misc_ref,mem_ref,
                  dres_ref,dmix_ref,out_ref,t_s):
    T,D=res_ref.shape
    E=mem_ref.shape[0]
    t_s[...]=dot(moe_ref[...],r_ref[...]).T
    mem=mem_ref[...]>0.5
    kept=jnp.where(mem,t_s[:E,:],-1e30)
    e=jnp.where(mem,jnp.exp(kept-jnp.max(kept,axis=0,keepdims=True)),0.0)
    g=e/jnp.sum(e,axis=0,keepdims=True)
    half=E//2
    sums=mg_ref[T:T+half,:].astype(F32)+mg_ref[T+half:,:].astype(F32)
    td=jnp.concatenate([sums[:,:T],sums[:,T:]],axis=0)
    t_s[...]=jnp.zeros_like(t_s)
    t_s[:E,:]=g*(td-jnp.sum(g*td,axis=0,keepdims=True))
    gl=t_s[...].T.astype(BF)
    dmoe=dot(gl,r_ref[...],1,1)+mg_ref[:T,:].astype(F32)
    res=res_ref[...]
    inv=lax.rsqrt(jnp.mean(res*res,axis=-1,keepdims=True)+norm_eps)
    gain=gain_row(misc_ref,gain_at)
    scaled=dmoe*gain
    grad_gain=jnp.sum(dmoe*res*inv,axis=0,keepdims=True)
    dres=cot_ref[...].astype(F32)+inv*scaled-res*(inv*inv*inv*jnp.mean(scaled*res,axis=-1,keepdims=True))
    dres_ref[...]=dres
    br=dres.astype(BF)
    dmix_ref[...]=dot(br,wo_ref[...],1,1).astype(BF)
    out_ref[:,:D]=dot(mix_ref[...],br,0,0).astype(BF)
    lane=lax.broadcasted_iota(jnp.int32,(D,128),1)
    column=jnp.broadcast_to(grad_gain,(128,D)).T
    out_ref[:,D:]=jnp.where(lane==E,column,dot(moe_ref[...],gl,0,0)).astype(BF)

def branch(gain_at,mg,res,moe_in,mixed,cot,w2,w1,mem_t):
    T,D=res.shape
    E=mem_t.shape[0]
    full=lambda i:(0,0)
    return pl.pallas_call(functools.partial(branch_kernel,gain_at),grid=(1,),
        in_specs=[pl.BlockSpec((T+E,D),full)]+[pl.BlockSpec((T,D),full)]*4+[pl.BlockSpec((D,D),full),pl.BlockSpec((D,128),lambda i:(0,D//128)),
                  pl.BlockSpec((D,128),lambda i:(0,MISC)),pl.BlockSpec((E,T),full)],
        out_specs=[pl.BlockSpec((T,D),full),pl.BlockSpec((T,D),full),pl.BlockSpec((D,D+128),full)],
        out_shape=[jax.ShapeDtypeStruct((T,D),F32),jax.ShapeDtypeStruct((T,D),BF),jax.ShapeDtypeStruct((D,D+128),BF)],
        scratch_shapes=[pltpu.VMEM((128,T),F32)],
        compiler_params=pltpu.CompilerParams(vmem_limit_bytes=60<<20),
        cost_estimate=COST,
        name="branch")(mg,res,moe_in,mixed,cot,w2,w2,w1,mem_t)

def fold(v):
    return v+pltpu.roll(v,2*HALF,1)

def attend_back_kernel(gain_at,h_ref,misc_ref,wq_ref,wk_ref,wv_ref,cos_ref,sin_ref,segc_ref,segr_ref,
                       q_ref,k_ref,v_ref,dm_ref,lse_ref,dres_ref,og_ref,
                       out_ref,gin_ref,x_s,bias_s,da_s):
    T,D=h_ref.shape
    step=pl.program_id(0)
    @pl.when(step==0)
    def _():
        inputs=h_ref[...].astype(F32)
        inv=lax.rsqrt(jnp.mean(inputs*inputs,axis=-1,keepdims=True)+norm_eps)
        x_s[...]=(inputs*inv*gain_row(misc_ref,gain_at)).astype(BF)
        r=lax.broadcasted_iota(jnp.int32,(T,T),0); c=lax.broadcasted_iota(jnp.int32,(T,T),1)
        bias_s[...]=jnp.where((segc_ref[...]==segr_ref[...])&(r<=c),0.0,-1e30)
        wide=og_ref.shape[1]
        out_ref[:,out_ref.shape[1]-128-wide:out_ref.shape[1]-128]=og_ref[...]
    cos=cos_ref[...]; sin=sin_ref[...]
    kp=spread(k_ref[...].astype(F32)); vp=spread(v_ref[...].astype(F32))
    low=lax.broadcasted_iota(jnp.int32,(T,128),1)<2*HALF
    dq_all=[];dk_all=[];dv_all=[]
    for c in range(2):
        cols=slice(128*c,128*c+128)
        qs=(q_ref[:,cols].astype(F32)*0.125).astype(BF)
        dm=dm_ref[:,cols]
        dks=[];dvs=[];dq=[None]*(T//ROWS)
        for half in range(2):
            i=2*c+half
            dk=None;dv=None
            for b in reversed(range(T//ROWS)):
                rows=slice(b*ROWS,(b+1)*ROWS); nk=(b+1)*ROWS
                s=dot(kp[i][:nk],qs[rows],1,1)+bias_s[:nk,rows]
                p=jnp.exp(s-lse_ref[0,i:i+1,rows])
                dp=dot(vp[i][:nk],dm[rows],1,1)
                delta=jnp.sum(p*dp,axis=0,keepdims=True)
                ds=(p*(dp-delta)).astype(BF)
                part=dot(ds,kp[i][:nk],0,0)
                dq[b]=part if dq[b] is None else dq[b]+part
                pk=dot(ds,qs[rows]); pv=dot(p.astype(BF),dm[rows])
                if dk is None:
                    dk,dv=pk,pv
                else:
                    dk=jnp.concatenate([dk[:nk]+pk,dk[nk:]],axis=0)
                    dv=jnp.concatenate([dv[:nk]+pv,dv[nk:]],axis=0)
            dks.append(dk);dvs.append(dv)
        dql=jnp.concatenate(dq,axis=0)*0.125
        dq_all.append((dql*cos-rotate(dql)*sin).astype(BF))
        dk_all.append(fold(jnp.where(low,dks[0],dks[1])))
        dv_all.append(fold(jnp.where(low,dvs[0],dvs[1])))
    dkl=jnp.where(low,dk_all[0],dk_all[1])
    dkl=(dkl*cos-rotate(dkl)*sin).astype(BF)
    dvl=jnp.where(low,dv_all[0],dv_all[1]).astype(BF)
    dql=jnp.concatenate(dq_all,axis=1)
    x=x_s[...]
    base=pl.multiple_of(step*512,512)
    out_ref[:,pl.ds(base,256)]=dot(x,dql,0,0).astype(BF)
    out_ref[:,pl.ds(base+256,128)]=dot(x,dkl,0,0).astype(BF)
    out_ref[:,pl.ds(base+384,128)]=dot(x,dvl,0,0).astype(BF)
    da=dot(dql,wq_ref[...],1,1)+dot(dkl,wk_ref[...],1,1)+dot(dvl,wv_ref[...],1,1)
    @pl.when(step==0)
    def _():
        da_s[...]=da
    @pl.when(step>0)
    def _():
        da_s[...]+=da
    @pl.when(step==pl.num_programs(0)-1)
    def _():
        inputs=h_ref[...].astype(F32)
        inv=lax.rsqrt(jnp.mean(inputs*inputs,axis=-1,keepdims=True)+norm_eps)
        dattn=da_s[...]
        scaled=dattn*gain_row(misc_ref,gain_at)
        grad_gain=jnp.sum(dattn*inputs*inv,axis=0,keepdims=True)
        gin_ref[...]=(dres_ref[...]+inv*scaled-inputs*(inv*inv*inv*jnp.mean(scaled*inputs,axis=-1,keepdims=True))).astype(BF)
        out_ref[:,out_ref.shape[1]-128:]=jnp.broadcast_to(grad_gain,(128,D)).T.astype(BF)

def attend_back(gain_at,h,w,cos,sin,segc,segr,q,k,v,dmix,lse,dres,og):
    T,D=h.shape
    kvw=k.shape[1]
    steps=lse.shape[0]
    full=lambda g:(0,0)
    kb=D//128; vb=kb+kvw//128
    wide=og.shape[1]
    width=D+2*kvw+wide+128
    return pl.pallas_call(functools.partial(attend_back_kernel,gain_at),grid=(steps,),
        in_specs=[pl.BlockSpec((T,D),full),pl.BlockSpec((D,128),lambda g:(0,MISC)),
                  pl.BlockSpec((D,256),lambda g:(0,g)),pl.BlockSpec((D,128),lambda g:(0,kb+g)),pl.BlockSpec((D,128),lambda g:(0,vb+g)),
                  pl.BlockSpec((T,128),full),pl.BlockSpec((T,128),full),pl.BlockSpec((T,1),full),pl.BlockSpec((1,T),full),
                  pl.BlockSpec((T,256),lambda g:(0,g)),pl.BlockSpec((T,128),lambda g:(0,g)),pl.BlockSpec((T,128),lambda g:(0,g)),
                  pl.BlockSpec((T,256),lambda g:(0,g)),pl.BlockSpec((1,8,T),lambda g:(g,0,0)),pl.BlockSpec((T,D),full),pl.BlockSpec((D,wide),full)],
        out_specs=[pl.BlockSpec((D,width),full),pl.BlockSpec((T,D),full)],
        out_shape=[jax.ShapeDtypeStruct((D,width),BF),jax.ShapeDtypeStruct((T,D),BF)],
        scratch_shapes=[pltpu.VMEM((T,D),BF),pltpu.VMEM((T,T),F32),pltpu.VMEM((T,D),F32)],
        compiler_params=pltpu.CompilerParams(vmem_limit_bytes=60<<20),
        cost_estimate=COST,
        name="attend_back")(h,w,w,w,w,cos,sin,segc,segr,q,k,v,dmix,lse,dres,og)

def rope_tables(segment_row):
    index = jnp.arange(segment_row.shape[0], dtype=jnp.int32)
    earlier = (segment_row[:, None] == segment_row[None, :]) & (index[None, :] < index[:, None])
    position = jnp.sum(earlier.astype(jnp.int32), axis=-1).astype(F32)
    frequency = rope_base ** (-jnp.arange(HALF, dtype=F32) / HALF)
    angles = position[:, None] * frequency[None, :]
    cosine = jnp.cos(angles)
    sine = jnp.sin(angles)
    return (
        jnp.concatenate([cosine] * 4, axis=1),
        jnp.concatenate([-sine, sine, -sine, sine], axis=1),
    )


def pad_columns(values):
    return jnp.pad(values, ((0, 0), (0, -values.shape[1] % 128)))


def body(
    hidden,
    segment_ids,
    routes,
    norm_attn,
    w_query,
    key_weight,
    value_weight,
    w_out,
    norm_moe,
    w_router,
    w_gate,
    w_up,
    w_down,
    cotangent,
):
    tokens, width = hidden.shape
    own_rows = w_query.shape[0]
    owned = w_gate.shape[0]
    peers = lax.axis_size("expert")
    me = lax.axis_index("expert")
    chips = peers // 2
    chip_order = (me // 2 - jnp.arange(chips, dtype=jnp.int32)) % chips
    core_order = (me % 2) ^ jnp.arange(2, dtype=jnp.int32)
    order = (chip_order[:, None] * 2 + core_order[None, :]).reshape(-1)
    dp_count = lax.axis_size("dp")
    dp_order = lax.axis_index("dp") ^ jnp.arange(dp_count, dtype=jnp.int32)
    places = (
        (chip_order[None, None, :] * 2 + core_order[None, :, None]) * dp_count
        + dp_order[:, None, None]
    ).reshape(-1)
    first_pack = pad_columns(
        jnp.concatenate(
            [
                w_query,
                key_weight,
                value_weight,
                norm_attn[:, None],
                norm_moe[:, None],
            ],
            axis=1,
        )
    )
    second_pack = pad_columns(jnp.concatenate([w_out, w_router], axis=1))
    cotangent_steps = [cotangent]
    routes_shifts = all_shifts(routes.astype(BF).reshape(-1, 128))
    both_shifts = all_shifts(own_slice(jnp.concatenate([first_pack, second_pack], axis=1)))
    both_shifts, routes_shifts, cotangent_steps = tie(both_shifts, routes_shifts, cotangent_steps)
    stacks = jnp.stack(both_shifts)
    first_width = first_pack.shape[1]
    stack_one = stacks[:, :, :first_width]
    stack_two = stacks[:, :, first_width:]
    slices_one = [stack_one] + [swap_dp(stack_one, r) for r in range(1, dp_count)]
    cotangent_steps.append(shift_chips(cotangent_steps[0], 1))
    routes_all = []
    for s in routes_shifts:
        routes_all += [s, swap_pair(s)]
    routes_all = jnp.stack(routes_all).astype(jnp.int32).reshape(peers, tokens, TOP)
    expert_ids = jnp.arange(EXPERTS, dtype=jnp.int32)
    member_all = jnp.any(routes_all[:, None, :, :] == expert_ids[:, None, None], axis=3)
    first_expert = me * owned
    member_own = lax.dynamic_slice_in_dim(member_all, first_expert, owned, 1)
    index = jnp.arange(tokens, dtype=jnp.int32)
    before = (index[:, None] < index[None, :]).astype(BF)
    rank = jnp.einsum(
        "sjt,tu->sju", member_own.astype(BF), before, preferred_element_type=F32
    ).astype(jnp.int32)
    rank = jnp.where(member_own, rank, -1)
    first_slot = jnp.arange(owned, dtype=jnp.int32)[:, None] * CAP
    keys = jnp.swapaxes(jnp.where(member_own, rank + first_slot, -1), 1, 2)
    rank_rows = jnp.swapaxes(rank, 0, 1)[:, :, None, :]
    member_all = member_all.astype(F32)
    member_line = jnp.any(routes[None, :, :] == expert_ids[:, None, None], axis=2).astype(F32)
    segment_row = segment_ids[0]
    cosine, sine = rope_tables(segment_row)
    segment_column = segment_row[:, None]
    segment_line = segment_row[None, :]
    tables = [rank_rows, keys, member_all, member_line, cosine, sine]
    tables, slices_one, stack_two = tie(tables, slices_one, stack_two)
    rank_rows, keys, member_all, member_line, cosine, sine = tables
    pieces_one = []
    for s in slices_one:
        pieces_one += [s, swap_pair(s)]
    pieces_one, stack_two, cotangent_steps = tie(pieces_one, stack_two, cotangent_steps)
    for k in range(2, chips - 1):
        cotangent_steps.append(shift_chips(cotangent_steps[k - 1], 1))
    if chips > 2:
        cotangent_steps.append(shift_chips(cotangent_steps[0], chips - 1))
    attn_weights = assemble(places, pieces_one)
    attn_weights, stack_two = tie(attn_weights, stack_two)
    slices_two = [stack_two] + [swap_dp(stack_two, r) for r in range(1, dp_count)]
    kv_heads = key_weight.shape[1] // (2 * HALF)
    query, key, value, mixed, lse = attend(
        0, hidden, attn_weights, cosine, sine, segment_column, segment_line, kv_heads
    )
    mixed, slices_two, cotangent_steps = tie(mixed, slices_two, cotangent_steps)
    pieces_two = []
    for s in slices_two:
        pieces_two += [s, swap_pair(s)]
    d = [cotangent_steps[0], swap_pair(cotangent_steps[0])]
    mixed, pieces_two, d = tie(mixed, pieces_two, d)
    out_weights = assemble(places, pieces_two)
    residual, moe_in = project(1, mixed, out_weights, hidden, attn_weights)
    x = [moe_in, swap_pair(moe_in)]
    x, moe_in = tie(x, moe_in)
    kept = None
    grad_parts = []
    out_parts = []
    hop = None
    for k in range(chips):
        following = shift_chips(x[0], 1) if k + 1 < chips else None
        if k == 3:
            hop = shift_chips(grad_parts[1], 1)
        outs = list(
            expert_step(
                k,
                first_expert[None],
                x,
                d,
                out_weights,
                member_all,
                rank_rows,
                keys,
                w_gate,
                w_up,
                w_down,
                kept,
            )
        )
        kept = outs[4:]
        outs = outs[:4]
        outs, kept, following, hop, grad_parts, out_parts = tie(
            outs, kept, following, hop, grad_parts, out_parts
        )
        if following is not None:
            x = [following, swap_pair(following)]
            d = [cotangent_steps[k + 1], swap_pair(cotangent_steps[k + 1])]
        grad_part = (outs[0].astype(F32) + swap_pair(outs[1]).astype(F32)).astype(BF)
        out_parts = out_parts + [(outs[2], outs[3])]
        if k + 1 < chips:
            x, d, grad_part = tie(x, d, grad_part)
        grad_parts = grad_parts + [grad_part]
    dp_me = lax.axis_index("dp")
    low = dp_me % 2
    high = dp_me // 2
    count = (owned + 1) // 2
    plans = [(0, count, 1, 2, low, high)]
    if owned > count:
        plans.append((count, owned - count, 2, 1, high, low))
    total = grad_parts[1]
    first_hop = 2
    if hop is not None:
        total, kept = tie((grad_parts[2].astype(F32) + hop.astype(F32)).astype(BF), kept)
        first_hop = 3
    moved = shift_chips(total, 1)
    halves = []
    sends = []
    for first_of, many, one, two, bit_one, bit_two in plans:
        send, keep = weight_grads(bit_one[None], first_of, many, kept)
        halves.append((first_of, one, two, bit_one, bit_two, keep))
        sends.append(send)
    moved, sends = tie(moved, sends)
    gots = [swap_dp(send, h[1]) for h, send in zip(halves, sends)]
    for k in range(first_hop, chips):
        moved = shift_chips((grad_parts[k].astype(F32) + moved.astype(F32)).astype(BF), 1)
    moe_grad = (grad_parts[0].astype(F32) + moved.astype(F32)).astype(BF)
    out_sum = (out_parts[1][0].astype(F32) + swap_pair(out_parts[1][1]).astype(F32)).astype(BF)
    moe_grad, out_sum = tie(moe_grad, out_sum)
    grad_residual, mixed_gradient, out_grads = branch(
        1, moe_grad, residual, moe_in, mixed, cotangent, out_weights, attn_weights, member_line
    )
    out_sum = shift_chips(out_sum, 1)
    attn_grads, grad_input = attend_back(
        0,
        hidden,
        attn_weights,
        cosine,
        sine,
        segment_column,
        segment_line,
        query,
        key,
        value,
        mixed_gradient,
        lse,
        grad_residual,
        out_grads,
    )
    attn_grads, out_sum, gots, out_parts = tie(attn_grads, out_sum, gots, out_parts)

    def block_for(k, b):
        number = chip_order[k] * 2 + core_order[b]
        return lax.dynamic_slice_in_dim(attn_grads, number * own_rows, own_rows, 0)

    seconds = []
    keeps = []
    for (first_of, one, two, bit_one, bit_two, keep), got in zip(halves, gots):
        send, keep = halve(bit_two[None], keep, got)
        seconds.append(send)
        keeps.append(keep)
    parts = [(block_for(k, 0), swap_pair(block_for(k, 1))) for k in range(chips)]
    seconds, keeps, parts, out_parts = tie(seconds, keeps, parts, out_parts)
    parts = [(a.astype(F32) + b.astype(F32)).astype(BF) for a, b in parts]
    gots = [swap_dp(send, h[2]) for h, send in zip(halves, seconds)]
    running = shift_chips(parts[1], 1)
    out_parts = [(a.astype(F32) + swap_pair(b).astype(F32)).astype(BF) for a, b in out_parts]
    gots, running, out_parts = tie(gots, running, out_parts)
    mine = [(k.astype(F32) + g.astype(F32)).astype(BF) for k, g in zip(keeps, gots)]
    running = (parts[2].astype(F32) + running.astype(F32)).astype(BF)
    mine, running, out_sum = tie(mine, running, out_sum)
    others = [swap_dp(m, h[2]) for h, m in zip(halves, mine)]
    running = shift_chips(running, 1)
    others, running, mine = tie(others, running, mine)
    thirds = [swap_dp(m, h[1]) for h, m in zip(halves, mine)]
    for k in [*range(3, chips), 0]:
        running = (parts[k].astype(F32) + running.astype(F32)).astype(BF)
        if k:
            running = shift_chips(running, 1)
    part, others, mine, out_sum = tie(running, others, mine, out_sum)
    sub = own_rows // dp_count

    def rows_of(r):
        return (dp_me ^ r) * sub

    sent = [lax.dynamic_slice_in_dim(part, rows_of(r), sub, 0) for r in range(dp_count)]
    received = [sent[0]] + [swap_dp(sent[r], r) for r in range(1, dp_count)]
    if chips > 2:
        out_sum = shift_chips((out_parts[2].astype(F32) + out_sum.astype(F32)).astype(BF), 1)
    received, thirds, others = tie(received, thirds, others)
    fourths = [swap_dp(o, h[1]) for h, o in zip(halves, others)]
    total = received[0].astype(F32)
    for piece in received[1:]:
        total = total + piece.astype(F32)
    total = total.astype(BF)
    pieces = [swap_dp(total, r) if r else total for r in range(dp_count)]
    for o in out_parts[3:]:
        out_sum = shift_chips((o.astype(F32) + out_sum.astype(F32)).astype(BF), 1)
    big = place_all(
        jnp.stack([b for h in halves for b in h[3:5]]),
        list(zip(mine, others, thirds, fourths)),
    )
    big, pieces, out_sum = tie(big, pieces, out_sum)
    result = (residual + out_parts[0].astype(F32) + out_sum.astype(F32)).astype(BF)
    share = place_share(
        jnp.stack([rows_of(r) for r in range(dp_count)]), pieces, width, key_weight.shape[1]
    )
    return (
        result,
        grad_input,
        share[6][0],
        share[0],
        share[1],
        share[2],
        share[3],
        share[5][0],
        share[4],
        big[0],
        big[1],
        big[2],
    )


def solution(mesh):
    in_specs = (
        P(("dp", "expert"), None),
        P(("dp", "expert"), None),
        P(("dp", "expert"), None),
        P("expert"),
        P("expert", None),
        P("expert", None),
        P("expert", None),
        P("expert", None),
        P("expert"),
        P("expert", None),
        P("expert", None, None),
        P("expert", None, None),
        P("expert", None, None),
        P(("dp", "expert"), None),
    )
    out_specs = (
        P(("dp", "expert"), None),
        P(("dp", "expert"), None),
        P("expert"),
        P("expert", None),
        P("expert", None),
        P("expert", None),
        P("expert", None),
        P("expert"),
        P("expert", None),
        P("expert", None, None),
        P("expert", None, None),
        P("expert", None, None),
    )
    return jax.shard_map(body, mesh=mesh, in_specs=in_specs, out_specs=out_specs, check_vma=False)
```

```python
import functools

import jax
import jax.numpy as jnp
from jax import lax
from jax.experimental import pallas as pl
from jax.experimental.pallas import tpu as pltpu
from jax.sharding import PartitionSpec as P

EXPERTS = 32
TOP = 8
CAP = 192
HALF = 32
ROWS = 256
MISC = 16
F32 = jnp.float32
BF = jnp.bfloat16
COST = pl.CostEstimate(flops=1 << 20, bytes_accessed=1 << 20, transcendentals=0)
norm_eps = 1e-06
rope_base = 10000.0


def dot(a,b,ca=1,cb=0):
    return lax.dot_general(a,b,(((ca,),(cb,)),((),())),preferred_element_type=F32)

def step_kernel(aliased, *refs):
    (first_ref, x0_ref, x1_ref, d0_ref, d1_ref, r_ref, m_ref, rank_ref, key_ref,
     wg_ref, wu_ref, wd_ref) = refs[:12]
    (g0_ref, g1_ref, o0_ref, o1_ref, xs_ref, ge_ref, hs_ref, dgs_ref, dus_ref,
     t_s, gate_s, rg_s, ro_s, dot_s) = refs[12 + aliased:]
    owned = gate_s.shape[0]
    E = m_ref.shape[1]
    T = x0_ref.shape[0]
    e = pl.program_id(0)
    x_refs = (x0_ref, x1_ref)
    d_refs = (d0_ref, d1_ref)

    @pl.when(e == 0)
    def _():
        for q in range(2):
            t_s[...] = dot(x_refs[q][...], r_ref[...]).T
            mem = m_ref[q] > 0.5
            kept = jnp.where(mem, t_s[:E, :], -1e30)
            ex = jnp.where(mem, jnp.exp(kept - jnp.max(kept, axis=0, keepdims=True)), 0.0)
            t_s[:E, :] = ex / jnp.sum(ex, axis=0, keepdims=True)
            for j in range(owned):
                gate_s[j, q] = t_s[pl.ds(first_ref[0] + j, 1), :]

    slot = lax.broadcasted_iota(jnp.int32, (CAP, T), 0)
    gs = []
    hits = []
    ds = []
    for q in range(2):
        rows = slice(q * CAP, (q + 1) * CAP)
        hit = slot == rank_ref[0, q]
        S = jnp.where(hit, 1.0, 0.0).astype(BF)
        xs_ref[0, rows, :] = dot(S, x_refs[q][...]).astype(BF)
        d = dot(S, d_refs[q][...])
        g = jnp.sum(jnp.where(hit, gate_s[e, q], 0.0), axis=1, keepdims=True)
        ge_ref[0, rows, :] = (g * d).astype(BF)
        gs.append(g)
        hits.append(hit)
        ds.append(d.astype(BF))
    x = xs_ref[0]
    gl = dot(x, wg_ref[0])
    ul = dot(x, wu_ref[0])
    sg = jax.nn.sigmoid(gl)
    act = gl * sg
    h = (act * ul).astype(BF)
    hs_ref[0] = h
    eo = dot(h, wd_ref[0]).astype(BF)
    for q in range(2):
        part = eo[q * CAP : (q + 1) * CAP].astype(F32)
        ro_s[q, pl.ds(pl.multiple_of(e * CAP, CAP), CAP), :] = (gs[q] * part).astype(BF)
        sd = jnp.sum(part * ds[q].astype(F32), axis=1, keepdims=True)
        dot_s[e, q] = jnp.sum(jnp.where(hits[q], sd, 0.0), axis=0, keepdims=True)
    dh = dot(ge_ref[0], wd_ref[0], 1, 1)
    dgl = (dh * ul * sg * (1.0 + gl * (1.0 - sg))).astype(BF)
    dul = (dh * act).astype(BF)
    dgs_ref[0] = dgl
    dus_ref[0] = dul
    dr = (dot(dgl, wg_ref[0], 1, 1) + dot(dul, wu_ref[0], 1, 1)).astype(BF)
    for q in range(2):
        rg_s[q, pl.ds(pl.multiple_of(e * CAP, CAP), CAP), :] = dr[q * CAP : (q + 1) * CAP]

    @pl.when(e == owned - 1)
    def _():
        lane = lax.broadcasted_iota(jnp.int32, (T, owned * CAP), 1)
        for q, g_ref, o_ref in ((0, g0_ref, o0_ref), (1, g1_ref, o1_ref)):
            keys = key_ref[q]
            hit = lane == keys[:, 0:1]
            for j in range(1, owned):
                hit = hit | (lane == keys[:, j : j + 1])
            S = jnp.where(hit, 1.0, 0.0).astype(BF)
            g_ref[:T, :] = dot(S, rg_s[q]).astype(BF)
            half = E // 2
            row = lax.broadcasted_iota(jnp.int32, (half, 2 * T), 0)
            column = lax.broadcasted_iota(jnp.int32, (half, 2 * T), 1)
            dots = jnp.zeros((half, 2 * T), F32)
            for j in range(owned):
                number = first_ref[0] + j
                here = (row == number % half) & (column // T == number // half)
                twice = jnp.concatenate([dot_s[j, q], dot_s[j, q]], axis=1)
                dots = jnp.where(here, twice, dots)
            high = dots.astype(BF)
            g_ref[T : T + half, :] = high
            g_ref[T + half :, :] = (dots - high.astype(F32)).astype(BF)
            o_ref[...] = dot(S, ro_s[q]).astype(BF)


def expert_step(k, first, x, d, router, member, rank, keys, wg, wu, wd, kept):
    owned, peers, _, T = rank.shape
    D, F = wg.shape[1:]
    E = member.shape[1]
    M = 2 * CAP
    rows = peers * CAP
    full = lambda e, f: (0, 0)
    shapes = [
        jax.ShapeDtypeStruct((owned, rows, D), BF),
        jax.ShapeDtypeStruct((owned, rows, D), BF),
    ] + [jax.ShapeDtypeStruct((owned, rows, F), BF)] * 3
    token = jax.ShapeDtypeStruct((T, D), BF)
    longer = jax.ShapeDtypeStruct((T + E, D), BF)
    assert 2 * T == D
    aliased = 0 if kept is None else len(shapes)
    return pl.pallas_call(
        functools.partial(step_kernel, aliased),
        grid_spec=pltpu.PrefetchScalarGridSpec(
            num_scalar_prefetch=1,
            grid=(owned,),
            in_specs=[pl.BlockSpec((T, D), full)] * 4
            + [
                pl.BlockSpec((D, 128), lambda e, f: (0, D // 128)),
                pl.BlockSpec((2, E, T), lambda e, f: (k, 0, 0)),
                pl.BlockSpec((1, 2, 1, T), lambda e, f: (e, k, 0, 0)),
                pl.BlockSpec((2, T, owned), lambda e, f: (k, 0, 0)),
                pl.BlockSpec((1, D, F), lambda e, f: (e, 0, 0)),
                pl.BlockSpec((1, D, F), lambda e, f: (e, 0, 0)),
                pl.BlockSpec((1, F, D), lambda e, f: (e, 0, 0)),
            ]
            + [pl.BlockSpec(memory_space=pl.ANY)] * aliased,
            out_specs=[pl.BlockSpec((T + E, D), full)] * 2
            + [pl.BlockSpec((T, D), full)] * 2
            + [pl.BlockSpec((1, M, s.shape[2]), lambda e, f: (e, k, 0)) for s in shapes],
            scratch_shapes=[
                pltpu.VMEM((128, T), F32),
                pltpu.VMEM((owned, 2, 1, T), F32),
                pltpu.VMEM((2, owned * CAP, D), BF),
                pltpu.VMEM((2, owned * CAP, D), BF),
                pltpu.VMEM((owned, 2, 1, T), F32),
            ],
        ),
        out_shape=[longer] * 2 + [token] * 2 + shapes,
        input_output_aliases={12 + i: 4 + i for i in range(aliased)},
        compiler_params=pltpu.CompilerParams(vmem_limit_bytes=60 << 20),
        cost_estimate=COST,
        name="expert_step",
    )(first, *x, *d, router, member, rank, keys, wg, wu, wd, *(kept or ()))


def weight_kernel(parts, bit_ref, xs_ref, ge_ref, hs_ref, dgs_ref, dus_ref, send_ref, keep_ref, *acc):
    at = pl.program_id(1)
    half = xs_ref.shape[2] // 2
    for n, o_ref in enumerate((send_ref, keep_ref)):
        bit = 1 - bit_ref[0] if n == 0 else bit_ref[0]
        off = pl.multiple_of(bit * half, half)
        x = xs_ref[0, :, pl.ds(off, half)]
        totals = (
            dot(x, dgs_ref[0], 0, 0),
            dot(x, dus_ref[0], 0, 0),
            dot(hs_ref[0], ge_ref[0, :, pl.ds(off, half)], 0, 0),
        )
        for i, total in enumerate(totals):
            if parts > 1:
                s = acc[0].at[3 * n + i]
                total = jnp.where(at == 0, 0.0, s[...]) + total
                s[...] = total
            o_ref[0, i] = total.astype(BF)


def weight_grads(bit, first, count, kept):
    rows, D = kept[0].shape[1:]
    F = kept[2].shape[2]
    half = D // 2
    assert half == F
    block = min(rows, 8 * CAP)
    parts = rows // block
    out = jax.ShapeDtypeStruct((count, 3, half, F), BF)
    return pl.pallas_call(
        functools.partial(weight_kernel, parts),
        grid_spec=pltpu.PrefetchScalarGridSpec(
            num_scalar_prefetch=1,
            grid=(count, parts),
            in_specs=[
                pl.BlockSpec((1, block, s.shape[2]), lambda e, i, b: (first + e, i, 0)) for s in kept
            ],
            out_specs=[pl.BlockSpec((1, 3, half, F), lambda e, i, b: (e, 0, 0, 0))] * 2,
            scratch_shapes=[pltpu.VMEM((6, half, F), F32)] if parts > 1 else [],
        ),
        out_shape=[out, out],
        compiler_params=pltpu.CompilerParams(vmem_limit_bytes=60 << 20),
        cost_estimate=COST,
        name="weight_grads",
    )(bit, *kept)


def halve_kernel(bit_ref, keep_ref, got_ref, send_ref, kept_ref):
    half = send_ref.shape[2]
    for n, o_ref in enumerate((send_ref, kept_ref)):
        bit = 1 - bit_ref[0] if n == 0 else bit_ref[0]
        rows = pl.ds(pl.multiple_of(bit * half, half), half)
        for i in range(keep_ref.shape[1]):
            o_ref[0, i] = (
                keep_ref[0, i, rows, :].astype(F32) + got_ref[0, i, rows, :].astype(F32)
            ).astype(BF)


def halve(bit, keep, got):
    count, mats, rows, F = keep.shape
    full = pl.BlockSpec((1, mats, rows, F), lambda e, b: (e, 0, 0, 0))
    part = pl.BlockSpec((1, mats, rows // 2, F), lambda e, b: (e, 0, 0, 0))
    out = jax.ShapeDtypeStruct((count, mats, rows // 2, F), BF)
    return pl.pallas_call(
        halve_kernel,
        grid_spec=pltpu.PrefetchScalarGridSpec(
            num_scalar_prefetch=1, grid=(count,), in_specs=[full, full], out_specs=[part, part]
        ),
        out_shape=[out, out],
        cost_estimate=COST,
        name="halve",
    )(bit, keep, got)


def place_early_kernel(counts, bits_ref, *refs):
    ins, (gg_ref, gu_ref, gd_ref) = refs[:-3], refs[-3:]
    e = pl.program_id(0)
    begin = 0
    for n, many in enumerate(counts):

        @pl.when((e >= begin) & (e < begin + many))
        def _(n=n):
            for i in range(3):
                q_ref = ins[3 * n + i]
                rows, half = q_ref.shape[2:]
                one = bits_ref[e, 0] if i < 2 else 1 - bits_ref[e, 0]
                two = bits_ref[e, 1] if i % 2 == 0 else 1 - bits_ref[e, 1]
                at = pl.ds(pl.multiple_of((2 * one + two) * rows, rows), rows)
                gg_ref[0, at, :] = q_ref[0, 0].astype(F32)
                gu_ref[0, at, :] = q_ref[0, 1].astype(F32)
                at = pl.ds(pl.multiple_of(two * rows, rows), rows)
                columns = pl.ds(pl.multiple_of(one * half, half), half)
                gd_ref[0, at, columns] = q_ref[0, 2].astype(F32)

        begin += many


def place_late_kernel(counts, bits_ref, *refs):
    n = len(counts)
    ins, outs = refs[:n], refs[n + 3 :]
    e = pl.program_id(0)
    begin = 0
    for q_ref, many in zip(ins, counts):

        @pl.when((e >= begin) & (e < begin + many))
        def _(q_ref=q_ref):
            for i, o_ref in enumerate(outs):
                o_ref[0] = q_ref[0, i].astype(F32)

        begin += many


def place(bits, quarters, held=None):
    counts = [q[0].shape[0] for q in quarters]
    owned = sum(counts)
    _, _, rows, F = quarters[0][0].shape
    D = 4 * rows
    specs = []
    begin = 0
    for many, group in zip(counts, quarters):
        block = lambda e, b, begin=begin, many=many: (jnp.clip(e - begin, 0, many - 1), 0, 0, 0)
        specs += [pl.BlockSpec((1, 3, rows, F), block)] * len(group)
        begin += many
    shapes = [(D, F), (D, F), (F, D)]
    if held is None:
        kernel = place_early_kernel
        outs = [pl.BlockSpec((1,) + s, lambda e, b: (e, 0, 0)) for s in shapes]
        aliases = {}
    else:
        kernel = place_late_kernel
        tall = pl.BlockSpec((1, rows, F), lambda e, b: (e, 3 - 2 * b[e, 0] - b[e, 1], 0))
        wide = pl.BlockSpec((1, rows, F), lambda e, b: (e, 1 - b[e, 1], 1 - b[e, 0]))
        outs = [tall, tall, wide]
        aliases = {1 + len(specs) + i: i for i in range(3)}
        specs = specs + [pl.BlockSpec(memory_space=pl.ANY)] * 3
    return pl.pallas_call(
        functools.partial(kernel, counts),
        grid_spec=pltpu.PrefetchScalarGridSpec(
            num_scalar_prefetch=1, grid=(owned,), in_specs=specs, out_specs=outs
        ),
        out_shape=[jax.ShapeDtypeStruct((owned,) + s, F32) for s in shapes],
        input_output_aliases=aliases,
        compiler_params=pltpu.CompilerParams(vmem_limit_bytes=60 << 20),
        cost_estimate=COST,
        name="place_early" if held is None else "place_late",
    )(bits, *[q for group in quarters for q in group], *(held or ()))


def assemble_kernel(place,p_ref,*refs):
    ins=refs[:-2]; o_ref,sem=refs[-2:]
    copies=[]
    for n,r in enumerate(ins):
        chips,sub,_=r.shape
        for k in range(chips):
            row=pl.multiple_of(p_ref[n*chips+k]*sub,sub)
            copies.append(pltpu.make_async_copy(r.at[k],o_ref.at[pl.ds(row,sub),:],sem.at[n*chips+k]))
    for c in copies: c.start()
    for c in copies: c.wait()

def assemble(places,pieces):
    n=len(pieces); chips,sub,W=pieces[0].shape
    return pl.pallas_call(functools.partial(assemble_kernel,None),
        grid_spec=pltpu.PrefetchScalarGridSpec(num_scalar_prefetch=1,grid=(1,),
          in_specs=[pl.BlockSpec(memory_space=pl.ANY)]*n,
          out_specs=pl.BlockSpec((n*chips*sub,W),lambda i,p:(0,0)),
          scratch_shapes=[pltpu.SemaphoreType.DMA((n*chips,))]),
        out_shape=jax.ShapeDtypeStruct((n*chips*sub,W),BF),cost_estimate=COST,
        compiler_params=pltpu.CompilerParams(vmem_limit_bytes=40<<20),
        name="assemble")(places,*pieces)

def ring_steps(v):
    n=lax.axis_size("expert")
    ring=[(i,(i+2)%n) for i in range(n)]
    blocks=[v]
    for _ in range(n//2-1):
        blocks.append(lax.ppermute(blocks[-1],"expert",ring))
    return blocks

def swap_pair(v):
    return lax.ppermute(v,"expert",[(i,i^1) for i in range(lax.axis_size("expert"))])

def swap_dp(v,r):
    return lax.ppermute(v,"dp",[(i,i^r) for i in range(lax.axis_size("dp"))])

def shift_chips(v,k):
    n=lax.axis_size("expert")
    return lax.ppermute(v,"expert",[(i,(i+2*k)%n) for i in range(n)])

def ring_gather(v):
    blocks=[]
    for b in ring_steps(v):
        blocks+=[b,swap_pair(b)]
    return blocks

def all_shifts(v):
    return [v]+[shift_chips(v,k) for k in range(1,lax.axis_size("expert")//2)]

def share_kernel(count, rows_ref, *refs):
    q_ref, k_ref, v_ref, o_ref, r_ref, m_ref, a_ref, s_ref, g_ref = refs[count:]
    D = q_ref.shape[1]
    groups = D // 256
    for r, piece in enumerate(refs[:count]):
        sub = piece.shape[0]
        rows = pl.ds(pl.multiple_of(rows_ref[r], sub), sub)
        for g in range(groups):
            at = 512 * g
            q_ref[rows, 256 * g : 256 * g + 256] = piece[:, at : at + 256].astype(F32)
            k_ref[rows, 128 * g : 128 * g + 128] = piece[:, at + 256 : at + 384].astype(F32)
            v_ref[rows, 128 * g : 128 * g + 128] = piece[:, at + 384 : at + 512].astype(F32)
        at = 512 * groups
        o_ref[rows, :] = piece[:, at : at + D].astype(F32)
        s_ref[rows, :] = piece[:, at + D : at + D + 128].astype(F32)
        g_ref[rows, :] = piece[:, at + D + 128 : at + D + 256].astype(F32)
    E = r_ref.shape[1]
    r_ref[...] = s_ref[:, :E]
    m_ref[...] = s_ref[...].T[E : E + 1, :]
    a_ref[...] = g_ref[...].T[:1, :]


def place_share(rows, pieces, D, kv):
    sub, W = pieces[0].shape
    n = len(pieces)
    assert W == 2 * D + 2 * kv + 256 and D // 256 == kv // 128
    shapes = [(n * sub, w) for w in (D, kv, kv, D, EXPERTS)] + [(1, n * sub)] * 2
    return pl.pallas_call(
        functools.partial(share_kernel, n),
        grid_spec=pltpu.PrefetchScalarGridSpec(
            num_scalar_prefetch=1,
            grid=(1,),
            in_specs=[pl.BlockSpec((sub, W), lambda i, r: (0, 0))] * n,
            out_specs=[pl.BlockSpec(s, lambda i, r: (0, 0)) for s in shapes],
            scratch_shapes=[pltpu.VMEM((n * sub, 128), F32)] * 2,
        ),
        out_shape=[jax.ShapeDtypeStruct(s, F32) for s in shapes],
        cost_estimate=COST,
        name="place_share",
    )(rows, *pieces)


def own_slice(pack):
    dp=lax.axis_size("dp")
    sub=pack.shape[0]//dp
    return lax.dynamic_slice_in_dim(pack,lax.axis_index("dp")*sub,sub,0)

def tie(*values):
    return lax.optimization_barrier(values)

def rotate(v):
    lane=lax.broadcasted_iota(jnp.int32,v.shape,1)
    width=v.shape[1]
    return jnp.where(lane%(2*HALF)<HALF,pltpu.roll(v,width-HALF,1),pltpu.roll(v,HALF,1))

def spread(v):
    lane=lax.broadcasted_iota(jnp.int32,v.shape,1)
    low=lane<2*HALF
    other=pltpu.roll(v,2*HALF,1)
    zero=jnp.zeros_like(v)
    return [jnp.where(low,v,zero).astype(BF),jnp.where(low,zero,other).astype(BF),
            jnp.where(low,other,zero).astype(BF),jnp.where(low,zero,v).astype(BF)]

def gain_row(misc_ref,which):
    return misc_ref[...].astype(F32).T[which:which+1,:]

def attend_kernel(gain_at,h_ref,misc_ref,wq_ref,wk_ref,wv_ref,cos_ref,sin_ref,segc_ref,segr_ref,
                  q_ref,k_ref,v_ref,mix_ref,lse_ref,x_s,bias_s):
    T=h_ref.shape[0]
    @pl.when(pl.program_id(0)==0)
    def _():
        inputs=h_ref[...].astype(F32)
        inv=lax.rsqrt(jnp.mean(inputs*inputs,axis=-1,keepdims=True)+norm_eps)
        x_s[...]=(inputs*inv*gain_row(misc_ref,gain_at)).astype(BF)
        r=lax.broadcasted_iota(jnp.int32,(T,T),0); c=lax.broadcasted_iota(jnp.int32,(T,T),1)
        bias_s[...]=jnp.where((segc_ref[...]==segr_ref[...])&(c<=r),0.0,-1e30)
    x=x_s[...]
    cos=cos_ref[...]; sin=sin_ref[...]
    ql=dot(x,wq_ref[...])
    qs=[]
    for c in range(2):
        part=ql[:,128*c:128*c+128]
        part=part*cos+rotate(part)*sin
        q_ref[:,128*c:128*c+128]=part.astype(BF)
        qs.append((part.astype(BF).astype(F32)*0.125).astype(BF))
    kl=dot(x,wk_ref[...])
    kl=(kl*cos+rotate(kl)*sin).astype(BF)
    k_ref[...]=kl
    vl=dot(x,wv_ref[...]).astype(BF)
    v_ref[...]=vl
    kp=spread(kl.astype(F32)); vp=spread(vl.astype(F32))
    lane=lax.broadcasted_iota(jnp.int32,(ROWS,128),1)
    for b in range(T//ROWS):
        rows=slice(b*ROWS,(b+1)*ROWS); nk=(b+1)*ROWS
        lse=jnp.zeros((ROWS,128),F32)
        for c in range(2):
            o=None
            for half in range(2):
                i=2*c+half
                s=dot(qs[c][rows],kp[i][:nk],1,1)+bias_s[rows,:nk]
                m=jnp.max(s,axis=1,keepdims=True)
                e=jnp.exp(s-m)
                l=jnp.sum(e,axis=1,keepdims=True)
                p=(e*(1.0/l)).astype(BF)
                part=dot(p,vp[i][:nk])
                o=part if o is None else o+part
                lse=jnp.where(lane==i,m+jnp.log(l),lse)
            mix_ref[rows,128*c:128*c+128]=o.astype(BF)
        lse_ref[0,:,rows]=lse.T[:8,:]

def attend(gain_at,h,w,cos,sin,segc,segr,kv_heads):
    T,D=h.shape
    steps=kv_heads//2
    full=lambda g:(0,0)
    qb=D//256; kb=D//128; vb=kb+kv_heads//2; mb=vb+kv_heads//2
    return pl.pallas_call(functools.partial(attend_kernel,gain_at),grid=(steps,),
        in_specs=[pl.BlockSpec((T,D),full),pl.BlockSpec((D,128),lambda g:(0,mb)),
                  pl.BlockSpec((D,256),lambda g:(0,g)),pl.BlockSpec((D,128),lambda g:(0,kb+g)),pl.BlockSpec((D,128),lambda g:(0,vb+g)),
                  pl.BlockSpec((T,128),full),pl.BlockSpec((T,128),full),pl.BlockSpec((T,1),full),pl.BlockSpec((1,T),full)],
        out_specs=[pl.BlockSpec((T,256),lambda g:(0,g)),pl.BlockSpec((T,128),lambda g:(0,g)),pl.BlockSpec((T,128),lambda g:(0,g)),
                   pl.BlockSpec((T,256),lambda g:(0,g)),pl.BlockSpec((1,8,T),lambda g:(g,0,0))],
        out_shape=[jax.ShapeDtypeStruct((T,D),BF),jax.ShapeDtypeStruct((T,64*kv_heads),BF),jax.ShapeDtypeStruct((T,64*kv_heads),BF),
                   jax.ShapeDtypeStruct((T,D),BF),jax.ShapeDtypeStruct((steps,8,T),F32)],
        scratch_shapes=[pltpu.VMEM((T,D),BF),pltpu.VMEM((T,T),F32)],
        cost_estimate=COST,
        name="attend")(h,w,w,w,w,cos,sin,segc,segr)


def project_kernel(gain_at,m_ref,w_ref,h_ref,misc_ref,res_ref,moe_ref):
    res=h_ref[...].astype(F32)+dot(m_ref[...],w_ref[...])
    res_ref[...]=res
    inv=lax.rsqrt(jnp.mean(res*res,axis=-1,keepdims=True)+norm_eps)
    moe_ref[...]=(res*inv*gain_row(misc_ref,gain_at)).astype(BF)

def project(gain_at,mixed,w2,h,w1):
    T,D=h.shape
    R=256
    return pl.pallas_call(functools.partial(project_kernel,gain_at),grid=(T//R,),
        in_specs=[pl.BlockSpec((R,D),lambda i:(i,0)),pl.BlockSpec((D,D),lambda i:(0,0)),pl.BlockSpec((R,D),lambda i:(i,0)),
                  pl.BlockSpec((D,128),lambda i:(0,MISC))],
        out_specs=[pl.BlockSpec((R,D),lambda i:(i,0)),pl.BlockSpec((R,D),lambda i:(i,0))],
        out_shape=[jax.ShapeDtypeStruct((T,D),F32),jax.ShapeDtypeStruct((T,D),BF)],
        cost_estimate=COST,
        name="project")(mixed,w2,h,w1)

def branch_kernel(gain_at,mg_ref,res_ref,moe_ref,mix_ref,cot_ref,wo_ref,r_ref,misc_ref,mem_ref,
                  dres_ref,dmix_ref,out_ref,t_s):
    T,D=res_ref.shape
    E=mem_ref.shape[0]
    t_s[...]=dot(moe_ref[...],r_ref[...]).T
    mem=mem_ref[...]>0.5
    kept=jnp.where(mem,t_s[:E,:],-1e30)
    e=jnp.where(mem,jnp.exp(kept-jnp.max(kept,axis=0,keepdims=True)),0.0)
    g=e/jnp.sum(e,axis=0,keepdims=True)
    half=E//2
    sums=mg_ref[T:T+half,:].astype(F32)+mg_ref[T+half:,:].astype(F32)
    td=jnp.concatenate([sums[:,:T],sums[:,T:]],axis=0)
    t_s[...]=jnp.zeros_like(t_s)
    t_s[:E,:]=g*(td-jnp.sum(g*td,axis=0,keepdims=True))
    gl=t_s[...].T.astype(BF)
    dmoe=dot(gl,r_ref[...],1,1)+mg_ref[:T,:].astype(F32)
    res=res_ref[...]
    inv=lax.rsqrt(jnp.mean(res*res,axis=-1,keepdims=True)+norm_eps)
    gain=gain_row(misc_ref,gain_at)
    scaled=dmoe*gain
    grad_gain=jnp.sum(dmoe*res*inv,axis=0,keepdims=True)
    dres=cot_ref[...].astype(F32)+inv*scaled-res*(inv*inv*inv*jnp.mean(scaled*res,axis=-1,keepdims=True))
    dres_ref[...]=dres
    br=dres.astype(BF)
    dmix_ref[...]=dot(br,wo_ref[...],1,1).astype(BF)
    out_ref[:,:D]=dot(mix_ref[...],br,0,0).astype(BF)
    lane=lax.broadcasted_iota(jnp.int32,(D,128),1)
    column=jnp.broadcast_to(grad_gain,(128,D)).T
    out_ref[:,D:]=jnp.where(lane==E,column,dot(moe_ref[...],gl,0,0)).astype(BF)

def branch(gain_at,mg,res,moe_in,mixed,cot,w2,w1,mem_t):
    T,D=res.shape
    E=mem_t.shape[0]
    full=lambda i:(0,0)
    return pl.pallas_call(functools.partial(branch_kernel,gain_at),grid=(1,),
        in_specs=[pl.BlockSpec((T+E,D),full)]+[pl.BlockSpec((T,D),full)]*4+[pl.BlockSpec((D,D),full),pl.BlockSpec((D,128),lambda i:(0,D//128)),
                  pl.BlockSpec((D,128),lambda i:(0,MISC)),pl.BlockSpec((E,T),full)],
        out_specs=[pl.BlockSpec((T,D),full),pl.BlockSpec((T,D),full),pl.BlockSpec((D,D+128),full)],
        out_shape=[jax.ShapeDtypeStruct((T,D),F32),jax.ShapeDtypeStruct((T,D),BF),jax.ShapeDtypeStruct((D,D+128),BF)],
        scratch_shapes=[pltpu.VMEM((128,T),F32)],
        compiler_params=pltpu.CompilerParams(vmem_limit_bytes=60<<20),
        cost_estimate=COST,
        name="branch")(mg,res,moe_in,mixed,cot,w2,w2,w1,mem_t)

def fold(v):
    return v+pltpu.roll(v,2*HALF,1)

def attend_back_kernel(gain_at,pos_ref,h_ref,misc_ref,wq_ref,wk_ref,wv_ref,cos_ref,sin_ref,segc_ref,segr_ref,
                       q_ref,k_ref,v_ref,dm_ref,lse_ref,dres_ref,og_ref,
                       own_ref,other_ref,gin_ref,x_s,bias_s,da_s,out_s,sem):
    T,D=h_ref.shape
    step=pl.program_id(0)
    def put(column,value):
        out_s[:,pl.ds(column,value.shape[1])]=value
    @pl.when(step==0)
    def _():
        inputs=h_ref[...].astype(F32)
        inv=lax.rsqrt(jnp.mean(inputs*inputs,axis=-1,keepdims=True)+norm_eps)
        x_s[...]=(inputs*inv*gain_row(misc_ref,gain_at)).astype(BF)
        r=lax.broadcasted_iota(jnp.int32,(T,T),0); c=lax.broadcasted_iota(jnp.int32,(T,T),1)
        bias_s[...]=jnp.where((segc_ref[...]==segr_ref[...])&(r<=c),0.0,-1e30)
        wide=og_ref.shape[1]
        put(out_s.shape[1]-128-wide,og_ref[...])
    cos=cos_ref[...]; sin=sin_ref[...]
    kp=spread(k_ref[...].astype(F32)); vp=spread(v_ref[...].astype(F32))
    low=lax.broadcasted_iota(jnp.int32,(T,128),1)<2*HALF
    dq_all=[];dk_all=[];dv_all=[]
    for c in range(2):
        cols=slice(128*c,128*c+128)
        qs=(q_ref[:,cols].astype(F32)*0.125).astype(BF)
        dm=dm_ref[:,cols]
        dks=[];dvs=[];dq=[None]*(T//ROWS)
        for half in range(2):
            i=2*c+half
            dk=None;dv=None
            for b in reversed(range(T//ROWS)):
                rows=slice(b*ROWS,(b+1)*ROWS); nk=(b+1)*ROWS
                s=dot(kp[i][:nk],qs[rows],1,1)+bias_s[:nk,rows]
                p=jnp.exp(s-lse_ref[0,i:i+1,rows])
                dp=dot(vp[i][:nk],dm[rows],1,1)
                delta=jnp.sum(p*dp,axis=0,keepdims=True)
                ds=(p*(dp-delta)).astype(BF)
                part=dot(ds,kp[i][:nk],0,0)
                dq[b]=part if dq[b] is None else dq[b]+part
                pk=dot(ds,qs[rows]); pv=dot(p.astype(BF),dm[rows])
                if dk is None:
                    dk,dv=pk,pv
                else:
                    dk=jnp.concatenate([dk[:nk]+pk,dk[nk:]],axis=0)
                    dv=jnp.concatenate([dv[:nk]+pv,dv[nk:]],axis=0)
            dks.append(dk);dvs.append(dv)
        dql=jnp.concatenate(dq,axis=0)*0.125
        dq_all.append((dql*cos-rotate(dql)*sin).astype(BF))
        dk_all.append(fold(jnp.where(low,dks[0],dks[1])))
        dv_all.append(fold(jnp.where(low,dvs[0],dvs[1])))
    dkl=jnp.where(low,dk_all[0],dk_all[1])
    dkl=(dkl*cos-rotate(dkl)*sin).astype(BF)
    dvl=jnp.where(low,dv_all[0],dv_all[1]).astype(BF)
    dql=jnp.concatenate(dq_all,axis=1)
    x=x_s[...]
    base=pl.multiple_of(step*512,512)
    put(base,dot(x,dql,0,0).astype(BF))
    put(base+256,dot(x,dkl,0,0).astype(BF))
    put(base+384,dot(x,dvl,0,0).astype(BF))
    da=dot(dql,wq_ref[...],1,1)+dot(dkl,wk_ref[...],1,1)+dot(dvl,wv_ref[...],1,1)
    @pl.when(step==0)
    def _():
        da_s[...]=da
    @pl.when(step>0)
    def _():
        da_s[...]+=da
    @pl.when(step==pl.num_programs(0)-1)
    def _():
        inputs=h_ref[...].astype(F32)
        inv=lax.rsqrt(jnp.mean(inputs*inputs,axis=-1,keepdims=True)+norm_eps)
        dattn=da_s[...]
        scaled=dattn*gain_row(misc_ref,gain_at)
        grad_gain=jnp.sum(dattn*inputs*inv,axis=0,keepdims=True)
        gin_ref[...]=(dres_ref[...]+inv*scaled-inputs*(inv*inv*inv*jnp.mean(scaled*inputs,axis=-1,keepdims=True))).astype(BF)
        put(out_s.shape[1]-128,jnp.broadcast_to(grad_gain,(128,D)).T.astype(BF))
        n=pos_ref.shape[0]
        span=D//n
        def copy(j,ref,at):
            rows=pl.ds(pl.multiple_of(at*span,span),span)
            return pltpu.make_async_copy(out_s.at[j*span:(j+1)*span,:],ref.at[rows,:],sem.at[j])
        for go in (True,False):
            for j in range(n):
                for ref,first in ((own_ref,0),(other_ref,n//2)):
                    @pl.when((pos_ref[j]>=first)&(pos_ref[j]<first+n//2))
                    def _(j=j,ref=ref,first=first):
                        c=copy(j,ref,pos_ref[j]-first)
                        if go:
                            c.start()
                        else:
                            c.wait()

def attend_back(pos,gain_at,h,w,cos,sin,segc,segr,q,k,v,dmix,lse,dres,og):
    T,D=h.shape
    kvw=k.shape[1]
    steps=lse.shape[0]
    full=lambda g,_:(0,0)
    kb=D//128; vb=kb+kvw//128
    wide=og.shape[1]
    width=D+2*kvw+wide+128
    return pl.pallas_call(functools.partial(attend_back_kernel,gain_at),
        grid_spec=pltpu.PrefetchScalarGridSpec(num_scalar_prefetch=1,grid=(steps,),
        in_specs=[pl.BlockSpec((T,D),full),pl.BlockSpec((D,128),lambda g,_:(0,MISC)),
                  pl.BlockSpec((D,256),lambda g,_:(0,g)),pl.BlockSpec((D,128),lambda g,_:(0,kb+g)),pl.BlockSpec((D,128),lambda g,_:(0,vb+g)),
                  pl.BlockSpec((T,128),full),pl.BlockSpec((T,128),full),pl.BlockSpec((T,1),full),pl.BlockSpec((1,T),full),
                  pl.BlockSpec((T,256),lambda g,_:(0,g)),pl.BlockSpec((T,128),lambda g,_:(0,g)),pl.BlockSpec((T,128),lambda g,_:(0,g)),
                  pl.BlockSpec((T,256),lambda g,_:(0,g)),pl.BlockSpec((1,8,T),lambda g,_:(g,0,0)),pl.BlockSpec((T,D),full),pl.BlockSpec((D,wide),full)],
        out_specs=[pl.BlockSpec(memory_space=pl.ANY)]*2+[pl.BlockSpec((T,D),full)],
        scratch_shapes=[pltpu.VMEM((T,D),BF),pltpu.VMEM((T,T),F32),pltpu.VMEM((T,D),F32),pltpu.VMEM((D,width),BF),pltpu.SemaphoreType.DMA((pos.shape[0],))]),
        out_shape=[jax.ShapeDtypeStruct((D//2,width),BF)]*2+[jax.ShapeDtypeStruct((T,D),BF)],
        compiler_params=pltpu.CompilerParams(vmem_limit_bytes=60<<20),
        cost_estimate=COST,
        name="attend_back")(pos,h,w,w,w,w,cos,sin,segc,segr,q,k,v,dmix,lse,dres,og)

def rope_tables(segment_row):
    index = jnp.arange(segment_row.shape[0], dtype=jnp.int32)
    earlier = (segment_row[:, None] == segment_row[None, :]) & (index[None, :] < index[:, None])
    position = jnp.sum(earlier.astype(jnp.int32), axis=-1).astype(F32)
    frequency = rope_base ** (-jnp.arange(HALF, dtype=F32) / HALF)
    angles = position[:, None] * frequency[None, :]
    cosine = jnp.cos(angles)
    sine = jnp.sin(angles)
    return (
        jnp.concatenate([cosine] * 4, axis=1),
        jnp.concatenate([-sine, sine, -sine, sine], axis=1),
    )


def pad_columns(values):
    return jnp.pad(values, ((0, 0), (0, -values.shape[1] % 128)))


def body(
    hidden,
    segment_ids,
    routes,
    norm_attn,
    w_query,
    key_weight,
    value_weight,
    w_out,
    norm_moe,
    w_router,
    w_gate,
    w_up,
    w_down,
    cotangent,
):
    tokens, width = hidden.shape
    own_rows = w_query.shape[0]
    owned = w_gate.shape[0]
    peers = lax.axis_size("expert")
    me = lax.axis_index("expert")
    chips = peers // 2
    chip_order = (me // 2 - jnp.arange(chips, dtype=jnp.int32)) % chips
    core_order = (me % 2) ^ jnp.arange(2, dtype=jnp.int32)
    order = (chip_order[:, None] * 2 + core_order[None, :]).reshape(-1)
    slot_of = jnp.argsort(order.reshape(chips, 2).T.reshape(-1))
    dp_count = lax.axis_size("dp")
    dp_order = lax.axis_index("dp") ^ jnp.arange(dp_count, dtype=jnp.int32)
    places = (
        (chip_order[None, None, :] * 2 + core_order[None, :, None]) * dp_count
        + dp_order[:, None, None]
    ).reshape(-1)
    first_pack = pad_columns(
        jnp.concatenate(
            [
                w_query,
                key_weight,
                value_weight,
                norm_attn[:, None],
                norm_moe[:, None],
            ],
            axis=1,
        )
    )
    second_pack = pad_columns(jnp.concatenate([w_out, w_router], axis=1))
    cotangent_steps = [cotangent]
    routes_shifts = all_shifts(routes.astype(BF).reshape(-1, 128))
    both_shifts = all_shifts(own_slice(jnp.concatenate([first_pack, second_pack], axis=1)))
    both_shifts, routes_shifts, cotangent_steps = tie(both_shifts, routes_shifts, cotangent_steps)
    stacks = jnp.stack(both_shifts)
    first_width = first_pack.shape[1]
    stack_one = stacks[:, :, :first_width]
    stack_two = stacks[:, :, first_width:]
    slices_one = [stack_one] + [swap_dp(stack_one, r) for r in range(1, dp_count)]
    cotangent_steps.append(shift_chips(cotangent_steps[0], 1))
    routes_all = []
    for s in routes_shifts:
        routes_all += [s, swap_pair(s)]
    routes_all = jnp.stack(routes_all).astype(jnp.int32).reshape(peers, tokens, TOP)
    expert_ids = jnp.arange(EXPERTS, dtype=jnp.int32)
    member_all = jnp.any(routes_all[:, None, :, :] == expert_ids[:, None, None], axis=3)
    first_expert = me * owned
    member_own = lax.dynamic_slice_in_dim(member_all, first_expert, owned, 1)
    index = jnp.arange(tokens, dtype=jnp.int32)
    before = (index[:, None] < index[None, :]).astype(BF)
    rank = jnp.einsum(
        "sjt,tu->sju", member_own.astype(BF), before, preferred_element_type=F32
    ).astype(jnp.int32)
    rank = jnp.where(member_own, rank, -1)
    first_slot = jnp.arange(owned, dtype=jnp.int32)[:, None] * CAP
    keys = jnp.swapaxes(jnp.where(member_own, rank + first_slot, -1), 1, 2)
    rank_rows = jnp.swapaxes(rank, 0, 1)[:, :, None, :]
    member_all = member_all.astype(F32)
    member_line = jnp.any(routes[None, :, :] == expert_ids[:, None, None], axis=2).astype(F32)
    segment_row = segment_ids[0]
    cosine, sine = rope_tables(segment_row)
    segment_column = segment_row[:, None]
    segment_line = segment_row[None, :]
    tables = [rank_rows, keys, member_all, member_line, cosine, sine, slot_of]
    tables, slices_one, stack_two = tie(tables, slices_one, stack_two)
    rank_rows, keys, member_all, member_line, cosine, sine, slot_of = tables
    pieces_one = []
    for s in slices_one:
        pieces_one += [s, swap_pair(s)]
    pieces_one, stack_two, cotangent_steps = tie(pieces_one, stack_two, cotangent_steps)
    for k in range(2, chips - 1):
        cotangent_steps.append(shift_chips(cotangent_steps[k - 1], 1))
    if chips > 2:
        cotangent_steps.append(shift_chips(cotangent_steps[0], chips - 1))
    attn_weights = assemble(places, pieces_one)
    attn_weights, stack_two = tie(attn_weights, stack_two)
    slices_two = [stack_two] + [swap_dp(stack_two, r) for r in range(1, dp_count)]
    kv_heads = key_weight.shape[1] // (2 * HALF)
    query, key, value, mixed, lse = attend(
        0, hidden, attn_weights, cosine, sine, segment_column, segment_line, kv_heads
    )
    mixed, slices_two, cotangent_steps = tie(mixed, slices_two, cotangent_steps)
    pieces_two = []
    for s in slices_two:
        pieces_two += [s, swap_pair(s)]
    d_pairs = [swap_pair(c) for c in cotangent_steps[:2]]
    mixed, pieces_two, d_pairs = tie(mixed, pieces_two, d_pairs)
    out_weights = assemble(places, pieces_two)
    residual, moe_in = project(1, mixed, out_weights, hidden, attn_weights)
    x = [moe_in, swap_pair(moe_in)]
    x, moe_in = tie(x, moe_in)
    kept = None
    grad_parts = []
    out_parts = []
    hop = None

    def sum_of(*terms):
        total = terms[0].astype(F32)
        for t in terms[1:]:
            total = total + t.astype(F32)
        return total.astype(BF)

    for k in range(chips):
        following = shift_chips(x[0], 1) if k + 1 < chips else None
        later = swap_pair(cotangent_steps[k + 2]) if k + 2 < chips else None
        if k == 3:
            hop = shift_chips(sum_of(*grad_parts[1]), 1)
        outs = list(
            expert_step(
                k,
                first_expert[None],
                x,
                (cotangent_steps[k], d_pairs[k]),
                out_weights,
                member_all,
                rank_rows,
                keys,
                w_gate,
                w_up,
                w_down,
                kept,
            )
        )
        kept = outs[4:]
        outs = outs[:4]
        outs, kept, following, hop, later, grad_parts, out_parts = tie(
            outs, kept, following, hop, later, grad_parts, out_parts
        )
        d_pairs.append(later)
        if following is not None:
            x = [following, swap_pair(following)]
        grad_parts = grad_parts + [(outs[0], swap_pair(outs[1]))]
        out_parts = out_parts + [(outs[2], outs[3])]
    dp_me = lax.axis_index("dp")
    low = dp_me % 2
    high = dp_me // 2
    count = (owned + 1) // 2
    plans = [(0, count, 1, 2, low, high)]
    if owned > count:
        plans.append((count, owned - count, 2, 1, high, low))
    first_hop = 2 if hop is None else 3
    total = sum_of(*grad_parts[first_hop - 1], *([] if hop is None else [hop]))
    total, kept = tie(total, kept)
    moved = shift_chips(total, 1)
    halves = []
    sends = []
    for first_of, many, one, two, bit_one, bit_two in plans:
        send, keep = weight_grads(bit_one[None], first_of, many, kept)
        halves.append((first_of, one, two, bit_one, bit_two, keep))
        sends.append(send)
    moved, sends = tie(moved, sends)
    gots = [swap_dp(send, h[1]) for h, send in zip(halves, sends)]
    for k in range(first_hop, chips):
        moved = shift_chips(sum_of(*grad_parts[k], moved), 1)
    moe_grad = sum_of(*grad_parts[0], moved)
    out_sum = (out_parts[1][0].astype(F32) + swap_pair(out_parts[1][1]).astype(F32)).astype(BF)
    moe_grad, out_sum = tie(moe_grad, out_sum)
    grad_residual, mixed_gradient, out_grads = branch(
        1, moe_grad, residual, moe_in, mixed, cotangent, out_weights, attn_weights, member_line
    )
    out_sum = shift_chips(out_sum, 1)
    own_half, other_half, grad_input = attend_back(
        slot_of,
        0,
        hidden,
        attn_weights,
        cosine,
        sine,
        segment_column,
        segment_line,
        query,
        key,
        value,
        mixed_gradient,
        lse,
        grad_residual,
        out_grads,
    )
    own_half, other_half, out_sum, gots, out_parts = tie(
        own_half, other_half, out_sum, gots, out_parts
    )

    seconds = []
    keeps = []
    for (first_of, one, two, bit_one, bit_two, keep), got in zip(halves, gots):
        send, keep = halve(bit_two[None], keep, got)
        seconds.append(send)
        keeps.append(keep)
    parts = [own_half, swap_pair(other_half)]
    seconds, keeps, parts, out_parts = tie(seconds, keeps, parts, out_parts)
    parts = [
        (
            parts[0][k * own_rows : (k + 1) * own_rows].astype(F32)
            + parts[1][k * own_rows : (k + 1) * own_rows].astype(F32)
        ).astype(BF)
        for k in range(chips)
    ]
    gots = [swap_dp(send, h[2]) for h, send in zip(halves, seconds)]
    running = shift_chips(parts[1], 1)
    out_parts = [(a.astype(F32) + swap_pair(b).astype(F32)).astype(BF) for a, b in out_parts]
    gots, running, out_parts = tie(gots, running, out_parts)
    mine = [(k.astype(F32) + g.astype(F32)).astype(BF) for k, g in zip(keeps, gots)]
    running = (parts[2].astype(F32) + running.astype(F32)).astype(BF)
    mine, running, out_sum = tie(mine, running, out_sum)
    others = [swap_dp(m, h[2]) for h, m in zip(halves, mine)]
    running = shift_chips(running, 1)
    others, running, mine = tie(others, running, mine)
    thirds = [swap_dp(m, h[1]) for h, m in zip(halves, mine)]
    for k in [*range(3, chips), 0]:
        running = (parts[k].astype(F32) + running.astype(F32)).astype(BF)
        if k:
            running = shift_chips(running, 1)
    part, others, mine, out_sum = tie(running, others, mine, out_sum)
    sub = own_rows // dp_count

    def rows_of(r):
        return (dp_me ^ r) * sub

    sent = [lax.dynamic_slice_in_dim(part, rows_of(r), sub, 0) for r in range(dp_count)]
    received = [sent[0]] + [swap_dp(sent[r], r) for r in range(1, dp_count)]
    if chips > 2:
        out_sum = shift_chips((out_parts[2].astype(F32) + out_sum.astype(F32)).astype(BF), 1)
    received, thirds, others = tie(received, thirds, others)
    fourths = [swap_dp(o, h[1]) for h, o in zip(halves, others)]
    total = received[0].astype(F32)
    for piece in received[1:]:
        total = total + piece.astype(F32)
    total = total.astype(BF)
    pieces = [swap_dp(total, r) if r else total for r in range(dp_count)]
    for o in out_parts[3:]:
        out_sum = shift_chips((o.astype(F32) + out_sum.astype(F32)).astype(BF), 1)
    result = (residual + out_parts[0].astype(F32) + out_sum.astype(F32)).astype(BF)
    bits = jnp.stack([jnp.stack(h[3:5]) for h in halves for _ in range(h[5].shape[0])])
    big = place(bits, list(zip(mine, others, thirds)))
    big, fourths, result = tie(big, fourths, result)
    big = place(bits, [(f,) for f in fourths], big)
    big, pieces = tie(big, pieces)
    share = place_share(
        jnp.stack([rows_of(r) for r in range(dp_count)]), pieces, width, key_weight.shape[1]
    )
    return (
        result,
        grad_input,
        share[6][0],
        share[0],
        share[1],
        share[2],
        share[3],
        share[5][0],
        share[4],
        big[0],
        big[1],
        big[2],
    )


def solution(mesh):
    in_specs = (
        P(("dp", "expert"), None),
        P(("dp", "expert"), None),
        P(("dp", "expert"), None),
        P("expert"),
        P("expert", None),
        P("expert", None),
        P("expert", None),
        P("expert", None),
        P("expert"),
        P("expert", None),
        P("expert", None, None),
        P("expert", None, None),
        P("expert", None, None),
        P(("dp", "expert"), None),
    )
    out_specs = (
        P(("dp", "expert"), None),
        P(("dp", "expert"), None),
        P("expert"),
        P("expert", None),
        P("expert", None),
        P("expert", None),
        P("expert", None),
        P("expert"),
        P("expert", None),
        P("expert", None, None),
        P("expert", None, None),
        P("expert", None, None),
    )
    return jax.shard_map(body, mesh=mesh, in_specs=in_specs, out_specs=out_specs, check_vma=False)
```

```python
import functools

import jax
import jax.numpy as jnp
from jax import lax
from jax.experimental import pallas as pl
from jax.experimental.pallas import tpu as pltpu
from jax.sharding import PartitionSpec as P

EXPERTS = 32
TOP = 8
CAP = 192
HALF = 32
ROWS = 256
MISC = 16
F32 = jnp.float32
BF = jnp.bfloat16
COST = pl.CostEstimate(flops=1 << 20, bytes_accessed=1 << 20, transcendentals=0)
norm_eps = 1e-06
rope_base = 10000.0


def dot(a,b,ca=1,cb=0):
    return lax.dot_general(a,b,(((ca,),(cb,)),((),())),preferred_element_type=F32)

def step_kernel(aliased, *refs):
    (first_ref, x0_ref, x1_ref, d0_ref, d1_ref, r_ref, m_ref, rank_ref, key_ref,
     wg_ref, wu_ref, wd_ref) = refs[:12]
    (g0_ref, g1_ref, o0_ref, o1_ref, xs_ref, ge_ref, hs_ref, dgs_ref, dus_ref,
     t_s, gate_s, rg_s, ro_s, dot_s) = refs[12 + aliased:]
    owned = gate_s.shape[0]
    E = m_ref.shape[1]
    T = x0_ref.shape[0]
    e = pl.program_id(0)
    x_refs = (x0_ref, x1_ref)
    d_refs = (d0_ref, d1_ref)

    @pl.when(e == 0)
    def _():
        for q in range(2):
            t_s[...] = dot(x_refs[q][...], r_ref[...]).T
            mem = m_ref[q] > 0.5
            kept = jnp.where(mem, t_s[:E, :], -1e30)
            ex = jnp.where(mem, jnp.exp(kept - jnp.max(kept, axis=0, keepdims=True)), 0.0)
            t_s[:E, :] = ex / jnp.sum(ex, axis=0, keepdims=True)
            for j in range(owned):
                gate_s[j, q] = t_s[pl.ds(first_ref[0] + j, 1), :]

    slot = lax.broadcasted_iota(jnp.int32, (CAP, T), 0)
    gs = []
    hits = []
    ds = []
    for q in range(2):
        rows = slice(q * CAP, (q + 1) * CAP)
        hit = slot == rank_ref[0, q]
        S = jnp.where(hit, 1.0, 0.0).astype(BF)
        xs_ref[0, rows, :] = dot(S, x_refs[q][...]).astype(BF)
        d = dot(S, d_refs[q][...])
        g = jnp.sum(jnp.where(hit, gate_s[e, q], 0.0), axis=1, keepdims=True)
        ge_ref[0, rows, :] = (g * d).astype(BF)
        gs.append(g)
        hits.append(hit)
        ds.append(d.astype(BF))
    x = xs_ref[0]
    gl = dot(x, wg_ref[0])
    ul = dot(x, wu_ref[0])
    sg = jax.nn.sigmoid(gl)
    act = gl * sg
    h = (act * ul).astype(BF)
    hs_ref[0] = h
    eo = dot(h, wd_ref[0]).astype(BF)
    for q in range(2):
        part = eo[q * CAP : (q + 1) * CAP].astype(F32)
        ro_s[q, pl.ds(pl.multiple_of(e * CAP, CAP), CAP), :] = (gs[q] * part).astype(BF)
        sd = jnp.sum(part * ds[q].astype(F32), axis=1, keepdims=True)
        dot_s[e, q] = jnp.sum(jnp.where(hits[q], sd, 0.0), axis=0, keepdims=True)
    dh = dot(ge_ref[0], wd_ref[0], 1, 1)
    dgl = (dh * ul * sg * (1.0 + gl * (1.0 - sg))).astype(BF)
    dul = (dh * act).astype(BF)
    dgs_ref[0] = dgl
    dus_ref[0] = dul
    dr = (dot(dgl, wg_ref[0], 1, 1) + dot(dul, wu_ref[0], 1, 1)).astype(BF)
    for q in range(2):
        rg_s[q, pl.ds(pl.multiple_of(e * CAP, CAP), CAP), :] = dr[q * CAP : (q + 1) * CAP]

    @pl.when(e == owned - 1)
    def _():
        lane = lax.broadcasted_iota(jnp.int32, (T, owned * CAP), 1)
        for q, g_ref, o_ref in ((0, g0_ref, o0_ref), (1, g1_ref, o1_ref)):
            keys = key_ref[q]
            hit = lane == keys[:, 0:1]
            for j in range(1, owned):
                hit = hit | (lane == keys[:, j : j + 1])
            S = jnp.where(hit, 1.0, 0.0).astype(BF)
            g_ref[:T, :] = dot(S, rg_s[q]).astype(BF)
            half = E // 2
            row = lax.broadcasted_iota(jnp.int32, (half, 2 * T), 0)
            column = lax.broadcasted_iota(jnp.int32, (half, 2 * T), 1)
            dots = jnp.zeros((half, 2 * T), F32)
            for j in range(owned):
                number = first_ref[0] + j
                here = (row == number % half) & (column // T == number // half)
                twice = jnp.concatenate([dot_s[j, q], dot_s[j, q]], axis=1)
                dots = jnp.where(here, twice, dots)
            high = dots.astype(BF)
            g_ref[T : T + half, :] = high
            g_ref[T + half :, :] = (dots - high.astype(F32)).astype(BF)
            o_ref[...] = dot(S, ro_s[q]).astype(BF)


def expert_step(k, first, x, d, router, member, rank, keys, wg, wu, wd, kept):
    owned, peers, _, T = rank.shape
    D, F = wg.shape[1:]
    E = member.shape[1]
    M = 2 * CAP
    rows = peers * CAP
    full = lambda e, f: (0, 0)
    shapes = [
        jax.ShapeDtypeStruct((owned, rows, D), BF),
        jax.ShapeDtypeStruct((owned, rows, D), BF),
    ] + [jax.ShapeDtypeStruct((owned, rows, F), BF)] * 3
    token = jax.ShapeDtypeStruct((T, D), BF)
    longer = jax.ShapeDtypeStruct((T + E, D), BF)
    assert 2 * T == D
    aliased = 0 if kept is None else len(shapes)
    return pl.pallas_call(
        functools.partial(step_kernel, aliased),
        grid_spec=pltpu.PrefetchScalarGridSpec(
            num_scalar_prefetch=1,
            grid=(owned,),
            in_specs=[pl.BlockSpec((T, D), full)] * 4
            + [
                pl.BlockSpec((D, 128), lambda e, f: (0, D // 128)),
                pl.BlockSpec((2, E, T), lambda e, f: (k, 0, 0)),
                pl.BlockSpec((1, 2, 1, T), lambda e, f: (e, k, 0, 0)),
                pl.BlockSpec((2, T, owned), lambda e, f: (k, 0, 0)),
                pl.BlockSpec((1, D, F), lambda e, f: (e, 0, 0)),
                pl.BlockSpec((1, D, F), lambda e, f: (e, 0, 0)),
                pl.BlockSpec((1, F, D), lambda e, f: (e, 0, 0)),
            ]
            + [pl.BlockSpec(memory_space=pl.ANY)] * aliased,
            out_specs=[pl.BlockSpec((T + E, D), full)] * 2
            + [pl.BlockSpec((T, D), full)] * 2
            + [pl.BlockSpec((1, M, s.shape[2]), lambda e, f: (e, k, 0)) for s in shapes],
            scratch_shapes=[
                pltpu.VMEM((128, T), F32),
                pltpu.VMEM((owned, 2, 1, T), F32),
                pltpu.VMEM((2, owned * CAP, D), BF),
                pltpu.VMEM((2, owned * CAP, D), BF),
                pltpu.VMEM((owned, 2, 1, T), F32),
            ],
        ),
        out_shape=[longer] * 2 + [token] * 2 + shapes,
        input_output_aliases={12 + i: 4 + i for i in range(aliased)},
        compiler_params=pltpu.CompilerParams(vmem_limit_bytes=60 << 20),
        cost_estimate=COST,
        name="expert_step",
    )(first, *x, *d, router, member, rank, keys, wg, wu, wd, *(kept or ()))


def weight_kernel(parts, bit_ref, xs_ref, ge_ref, hs_ref, dgs_ref, dus_ref, send_ref, keep_ref, *acc):
    at = pl.program_id(1)
    half = xs_ref.shape[2] // 2
    for n, o_ref in enumerate((send_ref, keep_ref)):
        bit = 1 - bit_ref[0] if n == 0 else bit_ref[0]
        off = pl.multiple_of(bit * half, half)
        x = xs_ref[0, :, pl.ds(off, half)]
        totals = (
            dot(x, dgs_ref[0], 0, 0),
            dot(x, dus_ref[0], 0, 0),
            dot(hs_ref[0], ge_ref[0, :, pl.ds(off, half)], 0, 0),
        )
        for i, total in enumerate(totals):
            if parts > 1:
                s = acc[0].at[3 * n + i]
                total = jnp.where(at == 0, 0.0, s[...]) + total
                s[...] = total
            o_ref[0, i] = total.astype(BF)


def weight_grads(bit, first, count, kept):
    rows, D = kept[0].shape[1:]
    F = kept[2].shape[2]
    half = D // 2
    assert half == F
    block = min(rows, 8 * CAP)
    parts = rows // block
    out = jax.ShapeDtypeStruct((count, 3, half, F), BF)
    return pl.pallas_call(
        functools.partial(weight_kernel, parts),
        grid_spec=pltpu.PrefetchScalarGridSpec(
            num_scalar_prefetch=1,
            grid=(count, parts),
            in_specs=[
                pl.BlockSpec((1, block, s.shape[2]), lambda e, i, b: (first + e, i, 0)) for s in kept
            ],
            out_specs=[pl.BlockSpec((1, 3, half, F), lambda e, i, b: (e, 0, 0, 0))] * 2,
            scratch_shapes=[pltpu.VMEM((6, half, F), F32)] if parts > 1 else [],
        ),
        out_shape=[out, out],
        compiler_params=pltpu.CompilerParams(vmem_limit_bytes=60 << 20),
        cost_estimate=COST,
        name="weight_grads",
    )(bit, *kept)


def halve_kernel(bit_ref, keep_ref, got_ref, send_ref, kept_ref):
    half = send_ref.shape[2]
    for n, o_ref in enumerate((send_ref, kept_ref)):
        bit = 1 - bit_ref[0] if n == 0 else bit_ref[0]
        rows = pl.ds(pl.multiple_of(bit * half, half), half)
        for i in range(keep_ref.shape[1]):
            o_ref[0, i] = (
                keep_ref[0, i, rows, :].astype(F32) + got_ref[0, i, rows, :].astype(F32)
            ).astype(BF)


def halve(bit, keep, got):
    count, mats, rows, F = keep.shape
    full = pl.BlockSpec((1, mats, rows, F), lambda e, b: (e, 0, 0, 0))
    part = pl.BlockSpec((1, mats, rows // 2, F), lambda e, b: (e, 0, 0, 0))
    out = jax.ShapeDtypeStruct((count, mats, rows // 2, F), BF)
    return pl.pallas_call(
        halve_kernel,
        grid_spec=pltpu.PrefetchScalarGridSpec(
            num_scalar_prefetch=1, grid=(count,), in_specs=[full, full], out_specs=[part, part]
        ),
        out_shape=[out, out],
        cost_estimate=COST,
        name="halve",
    )(bit, keep, got)


def place_early_kernel(counts, bits_ref, *refs):
    ins, (gg_ref, gu_ref, gd_ref) = refs[:-3], refs[-3:]
    e = pl.program_id(0)
    begin = 0
    for n, many in enumerate(counts):

        @pl.when((e >= begin) & (e < begin + many))
        def _(n=n):
            for i in range(3):
                q_ref = ins[3 * n + i]
                rows, half = q_ref.shape[2:]
                one = bits_ref[e, 0] if i < 2 else 1 - bits_ref[e, 0]
                two = bits_ref[e, 1] if i % 2 == 0 else 1 - bits_ref[e, 1]
                at = pl.ds(pl.multiple_of((2 * one + two) * rows, rows), rows)
                gg_ref[0, at, :] = q_ref[0, 0].astype(F32)
                gu_ref[0, at, :] = q_ref[0, 1].astype(F32)
                at = pl.ds(pl.multiple_of(two * rows, rows), rows)
                columns = pl.ds(pl.multiple_of(one * half, half), half)
                gd_ref[0, at, columns] = q_ref[0, 2].astype(F32)

        begin += many


def place_late_kernel(counts, bits_ref, *refs):
    n = len(counts)
    ins, outs = refs[:n], refs[n + 3 :]
    e = pl.program_id(0)
    begin = 0
    for q_ref, many in zip(ins, counts):

        @pl.when((e >= begin) & (e < begin + many))
        def _(q_ref=q_ref):
            for i, o_ref in enumerate(outs):
                o_ref[0] = q_ref[0, i].astype(F32)

        begin += many


def place(bits, quarters, held=None):
    counts = [q[0].shape[0] for q in quarters]
    owned = sum(counts)
    _, _, rows, F = quarters[0][0].shape
    D = 4 * rows
    specs = []
    begin = 0
    for many, group in zip(counts, quarters):
        block = lambda e, b, begin=begin, many=many: (jnp.clip(e - begin, 0, many - 1), 0, 0, 0)
        specs += [pl.BlockSpec((1, 3, rows, F), block)] * len(group)
        begin += many
    shapes = [(D, F), (D, F), (F, D)]
    if held is None:
        kernel = place_early_kernel
        outs = [pl.BlockSpec((1,) + s, lambda e, b: (e, 0, 0)) for s in shapes]
        aliases = {}
    else:
        kernel = place_late_kernel
        tall = pl.BlockSpec((1, rows, F), lambda e, b: (e, 3 - 2 * b[e, 0] - b[e, 1], 0))
        wide = pl.BlockSpec((1, rows, F), lambda e, b: (e, 1 - b[e, 1], 1 - b[e, 0]))
        outs = [tall, tall, wide]
        aliases = {1 + len(specs) + i: i for i in range(3)}
        specs = specs + [pl.BlockSpec(memory_space=pl.ANY)] * 3
    return pl.pallas_call(
        functools.partial(kernel, counts),
        grid_spec=pltpu.PrefetchScalarGridSpec(
            num_scalar_prefetch=1, grid=(owned,), in_specs=specs, out_specs=outs
        ),
        out_shape=[jax.ShapeDtypeStruct((owned,) + s, F32) for s in shapes],
        input_output_aliases=aliases,
        compiler_params=pltpu.CompilerParams(vmem_limit_bytes=60 << 20),
        cost_estimate=COST,
        name="place_early" if held is None else "place_late",
    )(bits, *[q for group in quarters for q in group], *(held or ()))


def assemble_kernel(p_ref,*refs):
    ins=refs[:-1]; o_ref=refs[-1]
    for n,r in enumerate(ins):
        chips,sub,_=r.shape
        for k in range(chips):
            row=pl.multiple_of(p_ref[n*chips+k]*sub,sub)
            o_ref[pl.ds(row,sub),:]=r[k]

def assemble(places,pieces):
    n=len(pieces); chips,sub,W=pieces[0].shape
    return pl.pallas_call(assemble_kernel,
        grid_spec=pltpu.PrefetchScalarGridSpec(num_scalar_prefetch=1,grid=(1,),
          in_specs=[pl.BlockSpec(memory_space=pltpu.VMEM)]*n,
          out_specs=pl.BlockSpec((n*chips*sub,W),lambda i,p:(0,0))),
        out_shape=jax.ShapeDtypeStruct((n*chips*sub,W),BF),cost_estimate=COST,
        compiler_params=pltpu.CompilerParams(vmem_limit_bytes=40<<20),
        name="assemble")(places,*pieces)

def ring_steps(v):
    n=lax.axis_size("expert")
    ring=[(i,(i+2)%n) for i in range(n)]
    blocks=[v]
    for _ in range(n//2-1):
        blocks.append(lax.ppermute(blocks[-1],"expert",ring))
    return blocks

def swap_pair(v):
    return lax.ppermute(v,"expert",[(i,i^1) for i in range(lax.axis_size("expert"))])

def swap_dp(v,r):
    return lax.ppermute(v,"dp",[(i,i^r) for i in range(lax.axis_size("dp"))])

def shift_chips(v,k):
    n=lax.axis_size("expert")
    return lax.ppermute(v,"expert",[(i,(i+2*k)%n) for i in range(n)])

def ring_gather(v):
    blocks=[]
    for b in ring_steps(v):
        blocks+=[b,swap_pair(b)]
    return blocks

def all_shifts(v):
    return [v]+[shift_chips(v,k) for k in range(1,lax.axis_size("expert")//2)]

def share_kernel(count, rows_ref, *refs):
    q_ref, k_ref, v_ref, o_ref, r_ref, m_ref, a_ref, s_ref, g_ref = refs[count:]
    D = q_ref.shape[1]
    groups = D // 256
    for r, piece in enumerate(refs[:count]):
        sub = piece.shape[0]
        rows = pl.ds(pl.multiple_of(rows_ref[r], sub), sub)
        for g in range(groups):
            at = 512 * g
            q_ref[rows, 256 * g : 256 * g + 256] = piece[:, at : at + 256].astype(F32)
            k_ref[rows, 128 * g : 128 * g + 128] = piece[:, at + 256 : at + 384].astype(F32)
            v_ref[rows, 128 * g : 128 * g + 128] = piece[:, at + 384 : at + 512].astype(F32)
        at = 512 * groups
        o_ref[rows, :] = piece[:, at : at + D].astype(F32)
        s_ref[rows, :] = piece[:, at + D : at + D + 128].astype(F32)
        g_ref[rows, :] = piece[:, at + D + 128 : at + D + 256].astype(F32)
    E = r_ref.shape[1]
    r_ref[...] = s_ref[:, :E]
    m_ref[...] = s_ref[...].T[E : E + 1, :]
    a_ref[...] = g_ref[...].T[:1, :]


def place_share(rows, pieces, D, kv):
    sub, W = pieces[0].shape
    n = len(pieces)
    assert W == 2 * D + 2 * kv + 256 and D // 256 == kv // 128
    shapes = [(n * sub, w) for w in (D, kv, kv, D, EXPERTS)] + [(1, n * sub)] * 2
    return pl.pallas_call(
        functools.partial(share_kernel, n),
        grid_spec=pltpu.PrefetchScalarGridSpec(
            num_scalar_prefetch=1,
            grid=(1,),
            in_specs=[pl.BlockSpec((sub, W), lambda i, r: (0, 0))] * n,
            out_specs=[pl.BlockSpec(s, lambda i, r: (0, 0)) for s in shapes],
            scratch_shapes=[pltpu.VMEM((n * sub, 128), F32)] * 2,
        ),
        out_shape=[jax.ShapeDtypeStruct(s, F32) for s in shapes],
        cost_estimate=COST,
        name="place_share",
    )(rows, *pieces)


def own_slice(pack):
    dp=lax.axis_size("dp")
    sub=pack.shape[0]//dp
    return lax.dynamic_slice_in_dim(pack,lax.axis_index("dp")*sub,sub,0)

def tie(*values):
    return lax.optimization_barrier(values)

def rotate(v):
    lane=lax.broadcasted_iota(jnp.int32,v.shape,1)
    width=v.shape[1]
    return jnp.where(lane%(2*HALF)<HALF,pltpu.roll(v,width-HALF,1),pltpu.roll(v,HALF,1))

def spread(v):
    lane=lax.broadcasted_iota(jnp.int32,v.shape,1)
    low=lane<2*HALF
    other=pltpu.roll(v,2*HALF,1)
    zero=jnp.zeros_like(v)
    return [jnp.where(low,v,zero).astype(BF),jnp.where(low,zero,other).astype(BF),
            jnp.where(low,other,zero).astype(BF),jnp.where(low,zero,v).astype(BF)]

def gain_row(misc_ref,which):
    return misc_ref[...].astype(F32).T[which:which+1,:]

def attend_kernel(gain_at,h_ref,misc_ref,wq_ref,wk_ref,wv_ref,cos_ref,sin_ref,segc_ref,segr_ref,
                  q_ref,k_ref,v_ref,mix_ref,lse_ref,x_s,bias_s):
    T=h_ref.shape[0]
    @pl.when(pl.program_id(0)==0)
    def _():
        inputs=h_ref[...].astype(F32)
        inv=lax.rsqrt(jnp.mean(inputs*inputs,axis=-1,keepdims=True)+norm_eps)
        x_s[...]=(inputs*inv*gain_row(misc_ref,gain_at)).astype(BF)
        r=lax.broadcasted_iota(jnp.int32,(T,T),0); c=lax.broadcasted_iota(jnp.int32,(T,T),1)
        bias_s[...]=jnp.where((segc_ref[...]==segr_ref[...])&(c<=r),0.0,-1e30)
    x=x_s[...]
    cos=cos_ref[...]; sin=sin_ref[...]
    ql=dot(x,wq_ref[...])
    qs=[]
    for c in range(2):
        part=ql[:,128*c:128*c+128]
        part=part*cos+rotate(part)*sin
        q_ref[:,128*c:128*c+128]=part.astype(BF)
        qs.append((part.astype(BF).astype(F32)*0.125).astype(BF))
    kl=dot(x,wk_ref[...])
    kl=(kl*cos+rotate(kl)*sin).astype(BF)
    k_ref[...]=kl
    vl=dot(x,wv_ref[...]).astype(BF)
    v_ref[...]=vl
    kp=spread(kl.astype(F32)); vp=spread(vl.astype(F32))
    lane=lax.broadcasted_iota(jnp.int32,(ROWS,128),1)
    for b in range(T//ROWS):
        rows=slice(b*ROWS,(b+1)*ROWS); nk=(b+1)*ROWS
        lse=jnp.zeros((ROWS,128),F32)
        for c in range(2):
            o=None
            for half in range(2):
                i=2*c+half
                s=dot(qs[c][rows],kp[i][:nk],1,1)+bias_s[rows,:nk]
                m=jnp.max(s,axis=1,keepdims=True)
                e=jnp.exp(s-m)
                l=jnp.sum(e,axis=1,keepdims=True)
                p=(e*(1.0/l)).astype(BF)
                part=dot(p,vp[i][:nk])
                o=part if o is None else o+part
                lse=jnp.where(lane==i,m+jnp.log(l),lse)
            mix_ref[rows,128*c:128*c+128]=o.astype(BF)
        lse_ref[0,:,rows]=lse.T[:8,:]

def attend(gain_at,h,w,cos,sin,segc,segr,kv_heads):
    T,D=h.shape
    steps=kv_heads//2
    full=lambda g:(0,0)
    qb=D//256; kb=D//128; vb=kb+kv_heads//2; mb=vb+kv_heads//2
    return pl.pallas_call(functools.partial(attend_kernel,gain_at),grid=(steps,),
        in_specs=[pl.BlockSpec((T,D),full),pl.BlockSpec((D,128),lambda g:(0,mb)),
                  pl.BlockSpec((D,256),lambda g:(0,g)),pl.BlockSpec((D,128),lambda g:(0,kb+g)),pl.BlockSpec((D,128),lambda g:(0,vb+g)),
                  pl.BlockSpec((T,128),full),pl.BlockSpec((T,128),full),pl.BlockSpec((T,1),full),pl.BlockSpec((1,T),full)],
        out_specs=[pl.BlockSpec((T,256),lambda g:(0,g)),pl.BlockSpec((T,128),lambda g:(0,g)),pl.BlockSpec((T,128),lambda g:(0,g)),
                   pl.BlockSpec((T,256),lambda g:(0,g)),pl.BlockSpec((1,8,T),lambda g:(g,0,0))],
        out_shape=[jax.ShapeDtypeStruct((T,D),BF),jax.ShapeDtypeStruct((T,64*kv_heads),BF),jax.ShapeDtypeStruct((T,64*kv_heads),BF),
                   jax.ShapeDtypeStruct((T,D),BF),jax.ShapeDtypeStruct((steps,8,T),F32)],
        scratch_shapes=[pltpu.VMEM((T,D),BF),pltpu.VMEM((T,T),F32)],
        cost_estimate=COST,
        name="attend")(h,w,w,w,w,cos,sin,segc,segr)


def project_kernel(gain_at,m_ref,w_ref,h_ref,misc_ref,res_ref,moe_ref):
    res=h_ref[...].astype(F32)+dot(m_ref[...],w_ref[...])
    res_ref[...]=res
    inv=lax.rsqrt(jnp.mean(res*res,axis=-1,keepdims=True)+norm_eps)
    moe_ref[...]=(res*inv*gain_row(misc_ref,gain_at)).astype(BF)

def project(gain_at,mixed,w2,h,w1):
    T,D=h.shape
    R=256
    return pl.pallas_call(functools.partial(project_kernel,gain_at),grid=(T//R,),
        in_specs=[pl.BlockSpec((R,D),lambda i:(i,0)),pl.BlockSpec((D,D),lambda i:(0,0)),pl.BlockSpec((R,D),lambda i:(i,0)),
                  pl.BlockSpec((D,128),lambda i:(0,MISC))],
        out_specs=[pl.BlockSpec((R,D),lambda i:(i,0)),pl.BlockSpec((R,D),lambda i:(i,0))],
        out_shape=[jax.ShapeDtypeStruct((T,D),F32),jax.ShapeDtypeStruct((T,D),BF)],
        cost_estimate=COST,
        name="project")(mixed,w2,h,w1)

def branch_kernel(gain_at,mg_ref,res_ref,moe_ref,mix_ref,cot_ref,wo_ref,r_ref,misc_ref,mem_ref,
                  dres_ref,dmix_ref,out_ref,t_s):
    T,D=res_ref.shape
    E=mem_ref.shape[0]
    t_s[...]=dot(moe_ref[...],r_ref[...]).T
    mem=mem_ref[...]>0.5
    kept=jnp.where(mem,t_s[:E,:],-1e30)
    e=jnp.where(mem,jnp.exp(kept-jnp.max(kept,axis=0,keepdims=True)),0.0)
    g=e/jnp.sum(e,axis=0,keepdims=True)
    half=E//2
    sums=mg_ref[T:T+half,:].astype(F32)+mg_ref[T+half:,:].astype(F32)
    td=jnp.concatenate([sums[:,:T],sums[:,T:]],axis=0)
    t_s[...]=jnp.zeros_like(t_s)
    t_s[:E,:]=g*(td-jnp.sum(g*td,axis=0,keepdims=True))
    gl=t_s[...].T.astype(BF)
    dmoe=dot(gl,r_ref[...],1,1)+mg_ref[:T,:].astype(F32)
    res=res_ref[...]
    inv=lax.rsqrt(jnp.mean(res*res,axis=-1,keepdims=True)+norm_eps)
    gain=gain_row(misc_ref,gain_at)
    scaled=dmoe*gain
    grad_gain=jnp.sum(dmoe*res*inv,axis=0,keepdims=True)
    dres=cot_ref[...].astype(F32)+inv*scaled-res*(inv*inv*inv*jnp.mean(scaled*res,axis=-1,keepdims=True))
    dres_ref[...]=dres
    br=dres.astype(BF)
    dmix_ref[...]=dot(br,wo_ref[...],1,1).astype(BF)
    out_ref[:,:D]=dot(mix_ref[...],br,0,0).astype(BF)
    lane=lax.broadcasted_iota(jnp.int32,(D,128),1)
    column=jnp.broadcast_to(grad_gain,(128,D)).T
    out_ref[:,D:]=jnp.where(lane==E,column,dot(moe_ref[...],gl,0,0)).astype(BF)

def branch(gain_at,mg,res,moe_in,mixed,cot,w2,w1,mem_t):
    T,D=res.shape
    E=mem_t.shape[0]
    full=lambda i:(0,0)
    return pl.pallas_call(functools.partial(branch_kernel,gain_at),grid=(1,),
        in_specs=[pl.BlockSpec((T+E,D),full)]+[pl.BlockSpec((T,D),full)]*4+[pl.BlockSpec((D,D),full),pl.BlockSpec((D,128),lambda i:(0,D//128)),
                  pl.BlockSpec((D,128),lambda i:(0,MISC)),pl.BlockSpec((E,T),full)],
        out_specs=[pl.BlockSpec((T,D),full),pl.BlockSpec((T,D),full),pl.BlockSpec((D,D+128),full)],
        out_shape=[jax.ShapeDtypeStruct((T,D),F32),jax.ShapeDtypeStruct((T,D),BF),jax.ShapeDtypeStruct((D,D+128),BF)],
        scratch_shapes=[pltpu.VMEM((128,T),F32)],
        compiler_params=pltpu.CompilerParams(vmem_limit_bytes=60<<20),
        cost_estimate=COST,
        name="branch")(mg,res,moe_in,mixed,cot,w2,w2,w1,mem_t)

def fold(v):
    return v+pltpu.roll(v,2*HALF,1)

def attend_back_kernel(gain_at,pos_ref,h_ref,misc_ref,wq_ref,wk_ref,wv_ref,cos_ref,sin_ref,segc_ref,segr_ref,
                       q_ref,k_ref,v_ref,dm_ref,lse_ref,dres_ref,og_ref,
                       own_ref,other_ref,gin_ref,x_s,bias_s,da_s,out_s,sem):
    T,D=h_ref.shape
    step=pl.program_id(0)
    def put(column,value):
        out_s[:,pl.ds(column,value.shape[1])]=value
    @pl.when(step==0)
    def _():
        inputs=h_ref[...].astype(F32)
        inv=lax.rsqrt(jnp.mean(inputs*inputs,axis=-1,keepdims=True)+norm_eps)
        x_s[...]=(inputs*inv*gain_row(misc_ref,gain_at)).astype(BF)
        r=lax.broadcasted_iota(jnp.int32,(T,T),0); c=lax.broadcasted_iota(jnp.int32,(T,T),1)
        bias_s[...]=jnp.where((segc_ref[...]==segr_ref[...])&(r<=c),0.0,-1e30)
        wide=og_ref.shape[1]
        put(out_s.shape[1]-128-wide,og_ref[...])
    cos=cos_ref[...]; sin=sin_ref[...]
    kp=spread(k_ref[...].astype(F32)); vp=spread(v_ref[...].astype(F32))
    low=lax.broadcasted_iota(jnp.int32,(T,128),1)<2*HALF
    dq_all=[];dk_all=[];dv_all=[]
    for c in range(2):
        cols=slice(128*c,128*c+128)
        qs=(q_ref[:,cols].astype(F32)*0.125).astype(BF)
        dm=dm_ref[:,cols]
        dks=[];dvs=[];dq=[None]*(T//ROWS)
        for half in range(2):
            i=2*c+half
            dk=None;dv=None
            for b in reversed(range(T//ROWS)):
                rows=slice(b*ROWS,(b+1)*ROWS); nk=(b+1)*ROWS
                s=dot(kp[i][:nk],qs[rows],1,1)+bias_s[:nk,rows]
                p=jnp.exp(s-lse_ref[0,i:i+1,rows])
                dp=dot(vp[i][:nk],dm[rows],1,1)
                delta=jnp.sum(p*dp,axis=0,keepdims=True)
                ds=(p*(dp-delta)).astype(BF)
                part=dot(ds,kp[i][:nk],0,0)
                dq[b]=part if dq[b] is None else dq[b]+part
                pk=dot(ds,qs[rows]); pv=dot(p.astype(BF),dm[rows])
                if dk is None:
                    dk,dv=pk,pv
                else:
                    dk=jnp.concatenate([dk[:nk]+pk,dk[nk:]],axis=0)
                    dv=jnp.concatenate([dv[:nk]+pv,dv[nk:]],axis=0)
            dks.append(dk);dvs.append(dv)
        dql=jnp.concatenate(dq,axis=0)*0.125
        dq_all.append((dql*cos-rotate(dql)*sin).astype(BF))
        dk_all.append(fold(jnp.where(low,dks[0],dks[1])))
        dv_all.append(fold(jnp.where(low,dvs[0],dvs[1])))
    dkl=jnp.where(low,dk_all[0],dk_all[1])
    dkl=(dkl*cos-rotate(dkl)*sin).astype(BF)
    dvl=jnp.where(low,dv_all[0],dv_all[1]).astype(BF)
    dql=jnp.concatenate(dq_all,axis=1)
    x=x_s[...]
    base=pl.multiple_of(step*512,512)
    put(base,dot(x,dql,0,0).astype(BF))
    put(base+256,dot(x,dkl,0,0).astype(BF))
    put(base+384,dot(x,dvl,0,0).astype(BF))
    da=dot(dql,wq_ref[...],1,1)+dot(dkl,wk_ref[...],1,1)+dot(dvl,wv_ref[...],1,1)
    @pl.when(step==0)
    def _():
        da_s[...]=da
    @pl.when(step>0)
    def _():
        da_s[...]+=da
    @pl.when(step==pl.num_programs(0)-1)
    def _():
        inputs=h_ref[...].astype(F32)
        inv=lax.rsqrt(jnp.mean(inputs*inputs,axis=-1,keepdims=True)+norm_eps)
        dattn=da_s[...]
        scaled=dattn*gain_row(misc_ref,gain_at)
        grad_gain=jnp.sum(dattn*inputs*inv,axis=0,keepdims=True)
        gin_ref[...]=(dres_ref[...]+inv*scaled-inputs*(inv*inv*inv*jnp.mean(scaled*inputs,axis=-1,keepdims=True))).astype(BF)
        put(out_s.shape[1]-128,jnp.broadcast_to(grad_gain,(128,D)).T.astype(BF))
        n=pos_ref.shape[0]
        span=D//n
        def copy(j,ref,at):
            rows=pl.ds(pl.multiple_of(at*span,span),span)
            return pltpu.make_async_copy(out_s.at[j*span:(j+1)*span,:],ref.at[rows,:],sem.at[j])
        for go in (True,False):
            for j in range(n):
                for ref,first in ((own_ref,0),(other_ref,n//2)):
                    @pl.when((pos_ref[j]>=first)&(pos_ref[j]<first+n//2))
                    def _(j=j,ref=ref,first=first):
                        c=copy(j,ref,pos_ref[j]-first)
                        if go:
                            c.start()
                        else:
                            c.wait()

def attend_back(pos,gain_at,h,w,cos,sin,segc,segr,q,k,v,dmix,lse,dres,og):
    T,D=h.shape
    kvw=k.shape[1]
    steps=lse.shape[0]
    full=lambda g,_:(0,0)
    kb=D//128; vb=kb+kvw//128
    wide=og.shape[1]
    width=D+2*kvw+wide+128
    return pl.pallas_call(functools.partial(attend_back_kernel,gain_at),
        grid_spec=pltpu.PrefetchScalarGridSpec(num_scalar_prefetch=1,grid=(steps,),
        in_specs=[pl.BlockSpec((T,D),full),pl.BlockSpec((D,128),lambda g,_:(0,MISC)),
                  pl.BlockSpec((D,256),lambda g,_:(0,g)),pl.BlockSpec((D,128),lambda g,_:(0,kb+g)),pl.BlockSpec((D,128),lambda g,_:(0,vb+g)),
                  pl.BlockSpec((T,128),full),pl.BlockSpec((T,128),full),pl.BlockSpec((T,1),full),pl.BlockSpec((1,T),full),
                  pl.BlockSpec((T,256),lambda g,_:(0,g)),pl.BlockSpec((T,128),lambda g,_:(0,g)),pl.BlockSpec((T,128),lambda g,_:(0,g)),
                  pl.BlockSpec((T,256),lambda g,_:(0,g)),pl.BlockSpec((1,8,T),lambda g,_:(g,0,0)),pl.BlockSpec((T,D),full),pl.BlockSpec((D,wide),full)],
        out_specs=[pl.BlockSpec(memory_space=pl.ANY)]*2+[pl.BlockSpec((T,D),full)],
        scratch_shapes=[pltpu.VMEM((T,D),BF),pltpu.VMEM((T,T),F32),pltpu.VMEM((T,D),F32),pltpu.VMEM((D,width),BF),pltpu.SemaphoreType.DMA((pos.shape[0],))]),
        out_shape=[jax.ShapeDtypeStruct((D//2,width),BF)]*2+[jax.ShapeDtypeStruct((T,D),BF)],
        compiler_params=pltpu.CompilerParams(vmem_limit_bytes=60<<20),
        cost_estimate=COST,
        name="attend_back")(pos,h,w,w,w,w,cos,sin,segc,segr,q,k,v,dmix,lse,dres,og)

def rope_tables(segment_row):
    index = jnp.arange(segment_row.shape[0], dtype=jnp.int32)
    earlier = (segment_row[:, None] == segment_row[None, :]) & (index[None, :] < index[:, None])
    position = jnp.sum(earlier.astype(jnp.int32), axis=-1).astype(F32)
    frequency = rope_base ** (-jnp.arange(HALF, dtype=F32) / HALF)
    angles = position[:, None] * frequency[None, :]
    cosine = jnp.cos(angles)
    sine = jnp.sin(angles)
    return (
        jnp.concatenate([cosine] * 4, axis=1),
        jnp.concatenate([-sine, sine, -sine, sine], axis=1),
    )


def pad_columns(values):
    return jnp.pad(values, ((0, 0), (0, -values.shape[1] % 128)))


def body(
    hidden,
    segment_ids,
    routes,
    norm_attn,
    w_query,
    key_weight,
    value_weight,
    w_out,
    norm_moe,
    w_router,
    w_gate,
    w_up,
    w_down,
    cotangent,
):
    tokens, width = hidden.shape
    own_rows = w_query.shape[0]
    owned = w_gate.shape[0]
    peers = lax.axis_size("expert")
    me = lax.axis_index("expert")
    chips = peers // 2
    chip_order = (me // 2 - jnp.arange(chips, dtype=jnp.int32)) % chips
    core_order = (me % 2) ^ jnp.arange(2, dtype=jnp.int32)
    order = (chip_order[:, None] * 2 + core_order[None, :]).reshape(-1)
    slot_of = jnp.argsort(order.reshape(chips, 2).T.reshape(-1))
    dp_count = lax.axis_size("dp")
    dp_order = lax.axis_index("dp") ^ jnp.arange(dp_count, dtype=jnp.int32)
    places = (
        (chip_order[None, None, :] * 2 + core_order[None, :, None]) * dp_count
        + dp_order[:, None, None]
    ).reshape(-1)
    first_pack = pad_columns(
        jnp.concatenate(
            [
                w_query,
                key_weight,
                value_weight,
                norm_attn[:, None],
                norm_moe[:, None],
            ],
            axis=1,
        )
    )
    second_pack = pad_columns(jnp.concatenate([w_out, w_router], axis=1))
    cotangent_steps = [cotangent]
    routes_shifts = all_shifts(routes.astype(BF).reshape(-1, 128))
    both_shifts = all_shifts(own_slice(jnp.concatenate([first_pack, second_pack], axis=1)))
    both_shifts, routes_shifts, cotangent_steps = tie(both_shifts, routes_shifts, cotangent_steps)
    stacks = jnp.stack(both_shifts)
    first_width = first_pack.shape[1]
    stack_one = stacks[:, :, :first_width]
    stack_two = stacks[:, :, first_width:]
    slices_one = [stack_one] + [swap_dp(stack_one, r) for r in range(1, dp_count)]
    cotangent_steps.append(shift_chips(cotangent_steps[0], 1))
    last_step = [shift_chips(cotangent_steps[0], chips - 1)] if chips > 2 else []
    routes_all = []
    for s in routes_shifts:
        routes_all += [s, swap_pair(s)]
    routes_all = jnp.stack(routes_all).astype(jnp.int32).reshape(peers, tokens, TOP)
    expert_ids = jnp.arange(EXPERTS, dtype=jnp.int32)
    member_all = jnp.any(routes_all[:, None, :, :] == expert_ids[:, None, None], axis=3)
    first_expert = me * owned
    member_own = lax.dynamic_slice_in_dim(member_all, first_expert, owned, 1)
    index = jnp.arange(tokens, dtype=jnp.int32)
    before = (index[:, None] < index[None, :]).astype(BF)
    rank = jnp.einsum(
        "sjt,tu->sju", member_own.astype(BF), before, preferred_element_type=F32
    ).astype(jnp.int32)
    rank = jnp.where(member_own, rank, -1)
    first_slot = jnp.arange(owned, dtype=jnp.int32)[:, None] * CAP
    keys = jnp.swapaxes(jnp.where(member_own, rank + first_slot, -1), 1, 2)
    rank_rows = jnp.swapaxes(rank, 0, 1)[:, :, None, :]
    member_all = member_all.astype(F32)
    member_line = jnp.any(routes[None, :, :] == expert_ids[:, None, None], axis=2).astype(F32)
    segment_row = segment_ids[0]
    cosine, sine = rope_tables(segment_row)
    segment_column = segment_row[:, None]
    segment_line = segment_row[None, :]
    tables = [rank_rows, keys, member_all, member_line, cosine, sine, slot_of]
    tables, slices_one, stack_two = tie(tables, slices_one, stack_two)
    rank_rows, keys, member_all, member_line, cosine, sine, slot_of = tables
    pieces_one = []
    for s in slices_one:
        pieces_one += [s, swap_pair(s)]
    pieces_one, stack_two, cotangent_steps = tie(pieces_one, stack_two, cotangent_steps)
    for k in range(2, chips - 1):
        cotangent_steps.append(shift_chips(cotangent_steps[k - 1], 1))
    attn_weights = assemble(places, pieces_one)
    attn_weights, stack_two, last_step = tie(attn_weights, stack_two, last_step)
    cotangent_steps += last_step
    slices_two = [stack_two] + [swap_dp(stack_two, r) for r in range(1, dp_count)]
    kv_heads = key_weight.shape[1] // (2 * HALF)
    query, key, value, mixed, lse = attend(
        0, hidden, attn_weights, cosine, sine, segment_column, segment_line, kv_heads
    )
    mixed, slices_two, cotangent_steps = tie(mixed, slices_two, cotangent_steps)
    pieces_two = []
    for s in slices_two:
        pieces_two += [s, swap_pair(s)]
    d_pairs = [swap_pair(c) for c in cotangent_steps[:2]]
    mixed, pieces_two, d_pairs = tie(mixed, pieces_two, d_pairs)
    out_weights = assemble(places, pieces_two)
    residual, moe_in = project(1, mixed, out_weights, hidden, attn_weights)
    x = [moe_in, swap_pair(moe_in)]
    x, moe_in = tie(x, moe_in)
    kept = None
    grad_parts = []
    out_parts = []
    hop = None

    def sum_of(*terms):
        total = terms[0].astype(F32)
        for t in terms[1:]:
            total = total + t.astype(F32)
        return total.astype(BF)

    for k in range(chips):
        following = shift_chips(x[0], 1) if k + 1 < chips else None
        later = swap_pair(cotangent_steps[k + 2]) if k + 2 < chips else None
        if k == 3:
            hop = shift_chips(sum_of(*grad_parts[1]), 1)
        outs = list(
            expert_step(
                k,
                first_expert[None],
                x,
                (cotangent_steps[k], d_pairs[k]),
                out_weights,
                member_all,
                rank_rows,
                keys,
                w_gate,
                w_up,
                w_down,
                kept,
            )
        )
        kept = outs[4:]
        outs = outs[:4]
        outs, kept, following, hop, later, grad_parts, out_parts = tie(
            outs, kept, following, hop, later, grad_parts, out_parts
        )
        d_pairs.append(later)
        if following is not None:
            x = [following, swap_pair(following)]
        grad_parts = grad_parts + [(outs[0], swap_pair(outs[1]))]
        out_parts = out_parts + [(outs[2], outs[3])]
    dp_me = lax.axis_index("dp")
    low = dp_me % 2
    high = dp_me // 2
    count = (owned + 1) // 2
    plans = [(0, count, 1, 2, low, high)]
    if owned > count:
        plans.append((count, owned - count, 2, 1, high, low))
    first_hop = 2 if hop is None else 3
    total = sum_of(*grad_parts[first_hop - 1], *([] if hop is None else [hop]))
    total, kept = tie(total, kept)
    moved = shift_chips(total, 1)
    halves = []
    sends = []
    for first_of, many, one, two, bit_one, bit_two in plans:
        send, keep = weight_grads(bit_one[None], first_of, many, kept)
        halves.append((first_of, one, two, bit_one, bit_two, keep))
        sends.append(send)
    moved, sends = tie(moved, sends)
    gots = [swap_dp(send, h[1]) for h, send in zip(halves, sends)]
    for k in range(first_hop, chips):
        moved = shift_chips(sum_of(*grad_parts[k], moved), 1)
    moe_grad = sum_of(*grad_parts[0], moved)
    out_sum = (out_parts[1][0].astype(F32) + swap_pair(out_parts[1][1]).astype(F32)).astype(BF)
    moe_grad, out_sum = tie(moe_grad, out_sum)
    grad_residual, mixed_gradient, out_grads = branch(
        1, moe_grad, residual, moe_in, mixed, cotangent, out_weights, attn_weights, member_line
    )
    out_sum = shift_chips(out_sum, 1)
    own_half, other_half, grad_input = attend_back(
        slot_of,
        0,
        hidden,
        attn_weights,
        cosine,
        sine,
        segment_column,
        segment_line,
        query,
        key,
        value,
        mixed_gradient,
        lse,
        grad_residual,
        out_grads,
    )
    own_half, other_half, out_sum, gots, out_parts = tie(
        own_half, other_half, out_sum, gots, out_parts
    )

    seconds = []
    keeps = []
    for (first_of, one, two, bit_one, bit_two, keep), got in zip(halves, gots):
        send, keep = halve(bit_two[None], keep, got)
        seconds.append(send)
        keeps.append(keep)
    parts = [own_half, swap_pair(other_half)]
    seconds, keeps, parts, out_parts = tie(seconds, keeps, parts, out_parts)
    parts = [
        (
            parts[0][k * own_rows : (k + 1) * own_rows].astype(F32)
            + parts[1][k * own_rows : (k + 1) * own_rows].astype(F32)
        ).astype(BF)
        for k in range(chips)
    ]
    gots = [swap_dp(send, h[2]) for h, send in zip(halves, seconds)]
    running = shift_chips(parts[1], 1)
    out_parts = [(a.astype(F32) + swap_pair(b).astype(F32)).astype(BF) for a, b in out_parts]
    gots, running, out_parts = tie(gots, running, out_parts)
    mine = [(k.astype(F32) + g.astype(F32)).astype(BF) for k, g in zip(keeps, gots)]
    running = (parts[2].astype(F32) + running.astype(F32)).astype(BF)
    mine, running, out_sum = tie(mine, running, out_sum)
    others = [swap_dp(m, h[2]) for h, m in zip(halves, mine)]
    running = shift_chips(running, 1)
    others, running, mine = tie(others, running, mine)
    thirds = [swap_dp(m, h[1]) for h, m in zip(halves, mine)]
    for k in [*range(3, chips), 0]:
        running = (parts[k].astype(F32) + running.astype(F32)).astype(BF)
        if k:
            running = shift_chips(running, 1)
    part, others, mine, out_sum = tie(running, others, mine, out_sum)
    sub = own_rows // dp_count

    def rows_of(r):
        return (dp_me ^ r) * sub

    sent = [lax.dynamic_slice_in_dim(part, rows_of(r), sub, 0) for r in range(dp_count)]
    received = [sent[0]] + [swap_dp(sent[r], r) for r in range(1, dp_count)]
    if chips > 2:
        out_sum = shift_chips((out_parts[2].astype(F32) + out_sum.astype(F32)).astype(BF), 1)
    received, thirds, others = tie(received, thirds, others)
    fourths = [swap_dp(o, h[1]) for h, o in zip(halves, others)]
    total = received[0].astype(F32)
    for piece in received[1:]:
        total = total + piece.astype(F32)
    total = total.astype(BF)
    pieces = [swap_dp(total, r) if r else total for r in range(dp_count)]
    for o in out_parts[3:]:
        out_sum = shift_chips((o.astype(F32) + out_sum.astype(F32)).astype(BF), 1)
    result = (residual + out_parts[0].astype(F32) + out_sum.astype(F32)).astype(BF)
    bits = jnp.stack([jnp.stack(h[3:5]) for h in halves for _ in range(h[5].shape[0])])
    big = place(bits, list(zip(mine, others, thirds)))
    big, fourths, result = tie(big, fourths, result)
    big = place(bits, [(f,) for f in fourths], big)
    big, pieces = tie(big, pieces)
    share = place_share(
        jnp.stack([rows_of(r) for r in range(dp_count)]), pieces, width, key_weight.shape[1]
    )
    return (
        result,
        grad_input,
        share[6][0],
        share[0],
        share[1],
        share[2],
        share[3],
        share[5][0],
        share[4],
        big[0],
        big[1],
        big[2],
    )


def solution(mesh):
    in_specs = (
        P(("dp", "expert"), None),
        P(("dp", "expert"), None),
        P(("dp", "expert"), None),
        P("expert"),
        P("expert", None),
        P("expert", None),
        P("expert", None),
        P("expert", None),
        P("expert"),
        P("expert", None),
        P("expert", None, None),
        P("expert", None, None),
        P("expert", None, None),
        P(("dp", "expert"), None),
    )
    out_specs = (
        P(("dp", "expert"), None),
        P(("dp", "expert"), None),
        P("expert"),
        P("expert", None),
        P("expert", None),
        P("expert", None),
        P("expert", None),
        P("expert"),
        P("expert", None),
        P("expert", None, None),
        P("expert", None, None),
        P("expert", None, None),
    )
    return jax.shard_map(body, mesh=mesh, in_specs=in_specs, out_specs=out_specs, check_vma=False)
```

```python
import functools

import jax
import jax.numpy as jnp
from jax import lax
from jax.experimental import pallas as pl
from jax.experimental.pallas import tpu as pltpu
from jax.sharding import PartitionSpec as P

EXPERTS = 32
TOP = 8
CAP = 192
HALF = 32
ROWS = 256
MISC = 16
F32 = jnp.float32
BF = jnp.bfloat16
COST = pl.CostEstimate(flops=1 << 20, bytes_accessed=1 << 20, transcendentals=0)
norm_eps = 1e-06
rope_base = 10000.0


def dot(a,b,ca=1,cb=0):
    return lax.dot_general(a,b,(((ca,),(cb,)),((),())),preferred_element_type=F32)

def step_kernel(aliased, *refs):
    (first_ref, x0_ref, x1_ref, d0_ref, d1_ref, r_ref, m_ref, rank_ref, key_ref,
     wg_ref, wu_ref, wd_ref) = refs[:12]
    (g0_ref, g1_ref, o0_ref, o1_ref, xs_ref, ge_ref, hs_ref, dgs_ref, dus_ref,
     t_s, gate_s, rg_s, ro_s, dot_s) = refs[12 + aliased:]
    owned = gate_s.shape[0]
    E = m_ref.shape[1]
    T = x0_ref.shape[0]
    e = pl.program_id(0)
    x_refs = (x0_ref, x1_ref)
    d_refs = (d0_ref, d1_ref)

    @pl.when(e == 0)
    def _():
        for q in range(2):
            t_s[...] = dot(x_refs[q][...], r_ref[...]).T
            mem = m_ref[q] > 0.5
            kept = jnp.where(mem, t_s[:E, :], -1e30)
            ex = jnp.where(mem, jnp.exp(kept - jnp.max(kept, axis=0, keepdims=True)), 0.0)
            t_s[:E, :] = ex / jnp.sum(ex, axis=0, keepdims=True)
            for j in range(owned):
                gate_s[j, q] = t_s[pl.ds(first_ref[0] + j, 1), :]

    slot = lax.broadcasted_iota(jnp.int32, (CAP, T), 0)
    gs = []
    hits = []
    ds = []
    for q in range(2):
        rows = slice(q * CAP, (q + 1) * CAP)
        hit = slot == rank_ref[0, q]
        S = jnp.where(hit, 1.0, 0.0).astype(BF)
        xs_ref[0, rows, :] = dot(S, x_refs[q][...]).astype(BF)
        d = dot(S, d_refs[q][...])
        g = jnp.sum(jnp.where(hit, gate_s[e, q], 0.0), axis=1, keepdims=True)
        ge_ref[0, rows, :] = (g * d).astype(BF)
        gs.append(g)
        hits.append(hit)
        ds.append(d.astype(BF))
    x = xs_ref[0]
    gl = dot(x, wg_ref[0])
    ul = dot(x, wu_ref[0])
    sg = jax.nn.sigmoid(gl)
    act = gl * sg
    h = (act * ul).astype(BF)
    hs_ref[0] = h
    eo = dot(h, wd_ref[0]).astype(BF)
    for q in range(2):
        part = eo[q * CAP : (q + 1) * CAP].astype(F32)
        ro_s[q, pl.ds(pl.multiple_of(e * CAP, CAP), CAP), :] = (gs[q] * part).astype(BF)
        sd = jnp.sum(part * ds[q].astype(F32), axis=1, keepdims=True)
        dot_s[e, q] = jnp.sum(jnp.where(hits[q], sd, 0.0), axis=0, keepdims=True)
    dh = dot(ge_ref[0], wd_ref[0], 1, 1)
    dgl = (dh * ul * sg * (1.0 + gl * (1.0 - sg))).astype(BF)
    dul = (dh * act).astype(BF)
    dgs_ref[0] = dgl
    dus_ref[0] = dul
    dr = (dot(dgl, wg_ref[0], 1, 1) + dot(dul, wu_ref[0], 1, 1)).astype(BF)
    for q in range(2):
        rg_s[q, pl.ds(pl.multiple_of(e * CAP, CAP), CAP), :] = dr[q * CAP : (q + 1) * CAP]

    @pl.when(e == owned - 1)
    def _():
        lane = lax.broadcasted_iota(jnp.int32, (T, owned * CAP), 1)
        for q, g_ref, o_ref in ((0, g0_ref, o0_ref), (1, g1_ref, o1_ref)):
            keys = key_ref[q]
            hit = lane == keys[:, 0:1]
            for j in range(1, owned):
                hit = hit | (lane == keys[:, j : j + 1])
            S = jnp.where(hit, 1.0, 0.0).astype(BF)
            g_ref[:T, :] = dot(S, rg_s[q]).astype(BF)
            half = E // 2
            row = lax.broadcasted_iota(jnp.int32, (half, 2 * T), 0)
            column = lax.broadcasted_iota(jnp.int32, (half, 2 * T), 1)
            dots = jnp.zeros((half, 2 * T), F32)
            for j in range(owned):
                number = first_ref[0] + j
                here = (row == number % half) & (column // T == number // half)
                twice = jnp.concatenate([dot_s[j, q], dot_s[j, q]], axis=1)
                dots = jnp.where(here, twice, dots)
            high = dots.astype(BF)
            g_ref[T : T + half, :] = high
            g_ref[T + half :, :] = (dots - high.astype(F32)).astype(BF)
            o_ref[...] = dot(S, ro_s[q]).astype(BF)


def expert_step(k, first, x, d, router, member, rank, keys, wg, wu, wd, kept):
    owned, peers, _, T = rank.shape
    D, F = wg.shape[1:]
    E = member.shape[1]
    M = 2 * CAP
    rows = peers * CAP
    full = lambda e, f: (0, 0)
    shapes = [
        jax.ShapeDtypeStruct((owned, rows, D), BF),
        jax.ShapeDtypeStruct((owned, rows, D), BF),
    ] + [jax.ShapeDtypeStruct((owned, rows, F), BF)] * 3
    token = jax.ShapeDtypeStruct((T, D), BF)
    longer = jax.ShapeDtypeStruct((T + E, D), BF)
    assert 2 * T == D
    aliased = 0 if kept is None else len(shapes)
    return pl.pallas_call(
        functools.partial(step_kernel, aliased),
        grid_spec=pltpu.PrefetchScalarGridSpec(
            num_scalar_prefetch=1,
            grid=(owned,),
            in_specs=[pl.BlockSpec((T, D), full)] * 4
            + [
                pl.BlockSpec((D, 128), lambda e, f: (0, D // 128)),
                pl.BlockSpec((2, E, T), lambda e, f: (k, 0, 0)),
                pl.BlockSpec((1, 2, 1, T), lambda e, f: (e, k, 0, 0)),
                pl.BlockSpec((2, T, owned), lambda e, f: (k, 0, 0)),
                pl.BlockSpec((1, D, F), lambda e, f: (e, 0, 0)),
                pl.BlockSpec((1, D, F), lambda e, f: (e, 0, 0)),
                pl.BlockSpec((1, F, D), lambda e, f: (e, 0, 0)),
            ]
            + [pl.BlockSpec(memory_space=pl.ANY)] * aliased,
            out_specs=[pl.BlockSpec((T + E, D), full)] * 2
            + [pl.BlockSpec((T, D), full)] * 2
            + [pl.BlockSpec((1, M, s.shape[2]), lambda e, f: (e, k, 0)) for s in shapes],
            scratch_shapes=[
                pltpu.VMEM((128, T), F32),
                pltpu.VMEM((owned, 2, 1, T), F32),
                pltpu.VMEM((2, owned * CAP, D), BF),
                pltpu.VMEM((2, owned * CAP, D), BF),
                pltpu.VMEM((owned, 2, 1, T), F32),
            ],
        ),
        out_shape=[longer] * 2 + [token] * 2 + shapes,
        input_output_aliases={12 + i: 4 + i for i in range(aliased)},
        compiler_params=pltpu.CompilerParams(vmem_limit_bytes=60 << 20),
        cost_estimate=COST,
        name="expert_step",
    )(first, *x, *d, router, member, rank, keys, wg, wu, wd, *(kept or ()))


def weight_kernel(parts, bit_ref, xs_ref, ge_ref, hs_ref, dgs_ref, dus_ref, send_ref, keep_ref, *acc):
    at = pl.program_id(1)
    half = xs_ref.shape[2] // 2
    for n, o_ref in enumerate((send_ref, keep_ref)):
        bit = 1 - bit_ref[0] if n == 0 else bit_ref[0]
        off = pl.multiple_of(bit * half, half)
        x = xs_ref[0, :, pl.ds(off, half)]
        totals = (
            dot(x, dgs_ref[0], 0, 0),
            dot(x, dus_ref[0], 0, 0),
            dot(hs_ref[0], ge_ref[0, :, pl.ds(off, half)], 0, 0),
        )
        for i, total in enumerate(totals):
            if parts > 1:
                s = acc[0].at[3 * n + i]
                total = jnp.where(at == 0, 0.0, s[...]) + total
                s[...] = total
            o_ref[0, i] = total.astype(BF)


def weight_grads(bit, first, count, kept):
    rows, D = kept[0].shape[1:]
    F = kept[2].shape[2]
    half = D // 2
    assert half == F
    block = min(rows, 8 * CAP)
    parts = rows // block
    out = jax.ShapeDtypeStruct((count, 3, half, F), BF)
    return pl.pallas_call(
        functools.partial(weight_kernel, parts),
        grid_spec=pltpu.PrefetchScalarGridSpec(
            num_scalar_prefetch=1,
            grid=(count, parts),
            in_specs=[
                pl.BlockSpec((1, block, s.shape[2]), lambda e, i, b: (first + e, i, 0)) for s in kept
            ],
            out_specs=[pl.BlockSpec((1, 3, half, F), lambda e, i, b: (e, 0, 0, 0))] * 2,
            scratch_shapes=[pltpu.VMEM((6, half, F), F32)] if parts > 1 else [],
        ),
        out_shape=[out, out],
        compiler_params=pltpu.CompilerParams(vmem_limit_bytes=60 << 20),
        cost_estimate=COST,
        name="weight_grads",
    )(bit, *kept)


def halve_kernel(bit_ref, keep_ref, got_ref, send_ref, kept_ref):
    half = send_ref.shape[2]
    for n, o_ref in enumerate((send_ref, kept_ref)):
        bit = 1 - bit_ref[0] if n == 0 else bit_ref[0]
        rows = pl.ds(pl.multiple_of(bit * half, half), half)
        for i in range(keep_ref.shape[1]):
            o_ref[0, i] = (
                keep_ref[0, i, rows, :].astype(F32) + got_ref[0, i, rows, :].astype(F32)
            ).astype(BF)


def halve(bit, keep, got):
    count, mats, rows, F = keep.shape
    full = pl.BlockSpec((1, mats, rows, F), lambda e, b: (e, 0, 0, 0))
    part = pl.BlockSpec((1, mats, rows // 2, F), lambda e, b: (e, 0, 0, 0))
    out = jax.ShapeDtypeStruct((count, mats, rows // 2, F), BF)
    return pl.pallas_call(
        halve_kernel,
        grid_spec=pltpu.PrefetchScalarGridSpec(
            num_scalar_prefetch=1, grid=(count,), in_specs=[full, full], out_specs=[part, part]
        ),
        out_shape=[out, out],
        cost_estimate=COST,
        name="halve",
    )(bit, keep, got)


def place_early_kernel(counts, bits_ref, *refs):
    ins, (gg_ref, gu_ref, gd_ref) = refs[:-3], refs[-3:]
    e = pl.program_id(0)
    begin = 0
    for n, many in enumerate(counts):

        @pl.when((e >= begin) & (e < begin + many))
        def _(n=n):
            for i in range(3):
                q_ref = ins[3 * n + i]
                rows, half = q_ref.shape[2:]
                one = bits_ref[e, 0] if i < 2 else 1 - bits_ref[e, 0]
                two = bits_ref[e, 1] if i % 2 == 0 else 1 - bits_ref[e, 1]
                at = pl.ds(pl.multiple_of((2 * one + two) * rows, rows), rows)
                gg_ref[0, at, :] = q_ref[0, 0].astype(F32)
                gu_ref[0, at, :] = q_ref[0, 1].astype(F32)
                at = pl.ds(pl.multiple_of(two * rows, rows), rows)
                columns = pl.ds(pl.multiple_of(one * half, half), half)
                gd_ref[0, at, columns] = q_ref[0, 2].astype(F32)

        begin += many


def place_late_kernel(counts, bits_ref, *refs):
    n = len(counts)
    ins, outs = refs[:n], refs[n + 3 :]
    e = pl.program_id(0)
    begin = 0
    for q_ref, many in zip(ins, counts):

        @pl.when((e >= begin) & (e < begin + many))
        def _(q_ref=q_ref):
            for i, o_ref in enumerate(outs):
                o_ref[0] = q_ref[0, i].astype(F32)

        begin += many


def place(bits, quarters, held=None):
    counts = [q[0].shape[0] for q in quarters]
    owned = sum(counts)
    _, _, rows, F = quarters[0][0].shape
    D = 4 * rows
    specs = []
    begin = 0
    for many, group in zip(counts, quarters):
        block = lambda e, b, begin=begin, many=many: (jnp.clip(e - begin, 0, many - 1), 0, 0, 0)
        specs += [pl.BlockSpec((1, 3, rows, F), block)] * len(group)
        begin += many
    shapes = [(D, F), (D, F), (F, D)]
    if held is None:
        kernel = place_early_kernel
        outs = [pl.BlockSpec((1,) + s, lambda e, b: (e, 0, 0)) for s in shapes]
        aliases = {}
    else:
        kernel = place_late_kernel
        tall = pl.BlockSpec((1, rows, F), lambda e, b: (e, 3 - 2 * b[e, 0] - b[e, 1], 0))
        wide = pl.BlockSpec((1, rows, F), lambda e, b: (e, 1 - b[e, 1], 1 - b[e, 0]))
        outs = [tall, tall, wide]
        aliases = {1 + len(specs) + i: i for i in range(3)}
        specs = specs + [pl.BlockSpec(memory_space=pl.ANY)] * 3
    return pl.pallas_call(
        functools.partial(kernel, counts),
        grid_spec=pltpu.PrefetchScalarGridSpec(
            num_scalar_prefetch=1, grid=(owned,), in_specs=specs, out_specs=outs
        ),
        out_shape=[jax.ShapeDtypeStruct((owned,) + s, F32) for s in shapes],
        input_output_aliases=aliases,
        compiler_params=pltpu.CompilerParams(vmem_limit_bytes=60 << 20),
        cost_estimate=COST,
        name="place_early" if held is None else "place_late",
    )(bits, *[q for group in quarters for q in group], *(held or ()))


def assemble_kernel(p_ref,*refs):
    ins=refs[:-1]; o_ref=refs[-1]
    for n,r in enumerate(ins):
        chips,sub,_=r.shape
        for k in range(chips):
            row=pl.multiple_of(p_ref[n*chips+k]*sub,sub)
            o_ref[pl.ds(row,sub),:]=r[k]

def assemble(places,pieces):
    n=len(pieces); chips,sub,W=pieces[0].shape
    return pl.pallas_call(assemble_kernel,
        grid_spec=pltpu.PrefetchScalarGridSpec(num_scalar_prefetch=1,grid=(1,),
          in_specs=[pl.BlockSpec(memory_space=pltpu.VMEM)]*n,
          out_specs=pl.BlockSpec((n*chips*sub,W),lambda i,p:(0,0))),
        out_shape=jax.ShapeDtypeStruct((n*chips*sub,W),BF),cost_estimate=COST,
        compiler_params=pltpu.CompilerParams(vmem_limit_bytes=40<<20),
        name="assemble")(places,*pieces)

def ring_steps(v):
    n=lax.axis_size("expert")
    ring=[(i,(i+2)%n) for i in range(n)]
    blocks=[v]
    for _ in range(n//2-1):
        blocks.append(lax.ppermute(blocks[-1],"expert",ring))
    return blocks

def swap_pair(v):
    return lax.ppermute(v,"expert",[(i,i^1) for i in range(lax.axis_size("expert"))])

def swap_dp(v,r):
    return lax.ppermute(v,"dp",[(i,i^r) for i in range(lax.axis_size("dp"))])

def shift_chips(v,k):
    n=lax.axis_size("expert")
    return lax.ppermute(v,"expert",[(i,(i+2*k)%n) for i in range(n)])

def ring_gather(v):
    blocks=[]
    for b in ring_steps(v):
        blocks+=[b,swap_pair(b)]
    return blocks

def all_shifts(v):
    return [v]+[shift_chips(v,k) for k in range(1,lax.axis_size("expert")//2)]

def share_kernel(count, rows_ref, *refs):
    q_ref, k_ref, v_ref, o_ref, r_ref, m_ref, a_ref, s_ref, g_ref = refs[count:]
    D = q_ref.shape[1]
    groups = D // 256
    for r, piece in enumerate(refs[:count]):
        sub = piece.shape[0]
        rows = pl.ds(pl.multiple_of(rows_ref[r], sub), sub)
        for g in range(groups):
            at = 512 * g
            q_ref[rows, 256 * g : 256 * g + 256] = piece[:, at : at + 256].astype(F32)
            k_ref[rows, 128 * g : 128 * g + 128] = piece[:, at + 256 : at + 384].astype(F32)
            v_ref[rows, 128 * g : 128 * g + 128] = piece[:, at + 384 : at + 512].astype(F32)
        at = 512 * groups
        o_ref[rows, :] = piece[:, at : at + D].astype(F32)
        s_ref[rows, :] = piece[:, at + D : at + D + 128].astype(F32)
        g_ref[rows, :] = piece[:, at + D + 128 : at + D + 256].astype(F32)
    E = r_ref.shape[1]
    r_ref[...] = s_ref[:, :E]
    m_ref[...] = s_ref[...].T[E : E + 1, :]
    a_ref[...] = g_ref[...].T[:1, :]


def place_share(rows, pieces, D, kv):
    sub, W = pieces[0].shape
    n = len(pieces)
    assert W == 2 * D + 2 * kv + 256 and D // 256 == kv // 128
    shapes = [(n * sub, w) for w in (D, kv, kv, D, EXPERTS)] + [(1, n * sub)] * 2
    return pl.pallas_call(
        functools.partial(share_kernel, n),
        grid_spec=pltpu.PrefetchScalarGridSpec(
            num_scalar_prefetch=1,
            grid=(1,),
            in_specs=[pl.BlockSpec((sub, W), lambda i, r: (0, 0))] * n,
            out_specs=[pl.BlockSpec(s, lambda i, r: (0, 0)) for s in shapes],
            scratch_shapes=[pltpu.VMEM((n * sub, 128), F32)] * 2,
        ),
        out_shape=[jax.ShapeDtypeStruct(s, F32) for s in shapes],
        cost_estimate=COST,
        name="place_share",
    )(rows, *pieces)


def own_slice(pack):
    dp=lax.axis_size("dp")
    sub=pack.shape[0]//dp
    return lax.dynamic_slice_in_dim(pack,lax.axis_index("dp")*sub,sub,0)

def tie(*values):
    return lax.optimization_barrier(values)

def rotate(v):
    lane=lax.broadcasted_iota(jnp.int32,v.shape,1)
    width=v.shape[1]
    return jnp.where(lane%(2*HALF)<HALF,pltpu.roll(v,width-HALF,1),pltpu.roll(v,HALF,1))

def spread(v):
    lane=lax.broadcasted_iota(jnp.int32,v.shape,1)
    low=lane<2*HALF
    other=pltpu.roll(v,2*HALF,1)
    zero=jnp.zeros_like(v)
    return [jnp.where(low,v,zero).astype(BF),jnp.where(low,zero,other).astype(BF),
            jnp.where(low,other,zero).astype(BF),jnp.where(low,zero,v).astype(BF)]

def gain_row(misc_ref,which):
    return misc_ref[...].astype(F32).T[which:which+1,:]

def attend_kernel(gain_at,h_ref,misc_ref,wq_ref,wk_ref,wv_ref,cos_ref,sin_ref,segc_ref,segr_ref,
                  q_ref,k_ref,v_ref,mix_ref,lse_ref,x_s,bias_s):
    T=h_ref.shape[0]
    @pl.when(pl.program_id(0)==0)
    def _():
        inputs=h_ref[...].astype(F32)
        inv=lax.rsqrt(jnp.mean(inputs*inputs,axis=-1,keepdims=True)+norm_eps)
        x_s[...]=(inputs*inv*gain_row(misc_ref,gain_at)).astype(BF)
        r=lax.broadcasted_iota(jnp.int32,(T,T),0); c=lax.broadcasted_iota(jnp.int32,(T,T),1)
        bias_s[...]=jnp.where((segc_ref[...]==segr_ref[...])&(c<=r),0.0,-1e30)
    x=x_s[...]
    cos=cos_ref[...]; sin=sin_ref[...]
    ql=dot(x,wq_ref[...])
    qs=[]
    for c in range(2):
        part=ql[:,128*c:128*c+128]
        part=part*cos+rotate(part)*sin
        q_ref[:,128*c:128*c+128]=part.astype(BF)
        qs.append((part.astype(BF).astype(F32)*0.125).astype(BF))
    kl=dot(x,wk_ref[...])
    kl=(kl*cos+rotate(kl)*sin).astype(BF)
    k_ref[...]=kl
    vl=dot(x,wv_ref[...]).astype(BF)
    v_ref[...]=vl
    kp=spread(kl.astype(F32)); vp=spread(vl.astype(F32))
    lane=lax.broadcasted_iota(jnp.int32,(ROWS,128),1)
    for b in range(T//ROWS):
        rows=slice(b*ROWS,(b+1)*ROWS); nk=(b+1)*ROWS
        lse=jnp.zeros((ROWS,128),F32)
        for c in range(2):
            o=None
            for half in range(2):
                i=2*c+half
                s=dot(qs[c][rows],kp[i][:nk],1,1)+bias_s[rows,:nk]
                m=jnp.max(s,axis=1,keepdims=True)
                e=jnp.exp(s-m)
                l=jnp.sum(e,axis=1,keepdims=True)
                p=(e*(1.0/l)).astype(BF)
                part=dot(p,vp[i][:nk])
                o=part if o is None else o+part
                lse=jnp.where(lane==i,m+jnp.log(l),lse)
            mix_ref[rows,128*c:128*c+128]=o.astype(BF)
        lse_ref[0,:,rows]=lse.T[:8,:]

def attend(gain_at,h,w,cos,sin,segc,segr,kv_heads):
    T,D=h.shape
    steps=kv_heads//2
    full=lambda g:(0,0)
    qb=D//256; kb=D//128; vb=kb+kv_heads//2; mb=vb+kv_heads//2
    return pl.pallas_call(functools.partial(attend_kernel,gain_at),grid=(steps,),
        in_specs=[pl.BlockSpec((T,D),full),pl.BlockSpec((D,128),lambda g:(0,mb)),
                  pl.BlockSpec((D,256),lambda g:(0,g)),pl.BlockSpec((D,128),lambda g:(0,kb+g)),pl.BlockSpec((D,128),lambda g:(0,vb+g)),
                  pl.BlockSpec((T,128),full),pl.BlockSpec((T,128),full),pl.BlockSpec((T,1),full),pl.BlockSpec((1,T),full)],
        out_specs=[pl.BlockSpec((T,256),lambda g:(0,g)),pl.BlockSpec((T,128),lambda g:(0,g)),pl.BlockSpec((T,128),lambda g:(0,g)),
                   pl.BlockSpec((T,256),lambda g:(0,g)),pl.BlockSpec((1,8,T),lambda g:(g,0,0))],
        out_shape=[jax.ShapeDtypeStruct((T,D),BF),jax.ShapeDtypeStruct((T,64*kv_heads),BF),jax.ShapeDtypeStruct((T,64*kv_heads),BF),
                   jax.ShapeDtypeStruct((T,D),BF),jax.ShapeDtypeStruct((steps,8,T),F32)],
        scratch_shapes=[pltpu.VMEM((T,D),BF),pltpu.VMEM((T,T),F32)],
        cost_estimate=COST,
        name="attend")(h,w,w,w,w,cos,sin,segc,segr)


def project_kernel(gain_at,m_ref,w_ref,h_ref,misc_ref,res_ref,moe_ref):
    res=h_ref[...].astype(F32)+dot(m_ref[...],w_ref[...])
    res_ref[...]=res
    inv=lax.rsqrt(jnp.mean(res*res,axis=-1,keepdims=True)+norm_eps)
    moe_ref[...]=(res*inv*gain_row(misc_ref,gain_at)).astype(BF)

def project(gain_at,mixed,w2,h,w1):
    T,D=h.shape
    R=256
    return pl.pallas_call(functools.partial(project_kernel,gain_at),grid=(T//R,),
        in_specs=[pl.BlockSpec((R,D),lambda i:(i,0)),pl.BlockSpec((D,D),lambda i:(0,0)),pl.BlockSpec((R,D),lambda i:(i,0)),
                  pl.BlockSpec((D,128),lambda i:(0,MISC))],
        out_specs=[pl.BlockSpec((R,D),lambda i:(i,0)),pl.BlockSpec((R,D),lambda i:(i,0))],
        out_shape=[jax.ShapeDtypeStruct((T,D),F32),jax.ShapeDtypeStruct((T,D),BF)],
        cost_estimate=COST,
        name="project")(mixed,w2,h,w1)

def branch_kernel(gain_at,mg_ref,res_ref,moe_ref,mix_ref,cot_ref,wo_ref,r_ref,misc_ref,mem_ref,
                  dres_ref,dmix_ref,out_ref,t_s):
    T,D=res_ref.shape
    E=mem_ref.shape[0]
    t_s[...]=dot(moe_ref[...],r_ref[...]).T
    mem=mem_ref[...]>0.5
    kept=jnp.where(mem,t_s[:E,:],-1e30)
    e=jnp.where(mem,jnp.exp(kept-jnp.max(kept,axis=0,keepdims=True)),0.0)
    g=e/jnp.sum(e,axis=0,keepdims=True)
    half=E//2
    sums=mg_ref[T:T+half,:].astype(F32)+mg_ref[T+half:,:].astype(F32)
    td=jnp.concatenate([sums[:,:T],sums[:,T:]],axis=0)
    t_s[...]=jnp.zeros_like(t_s)
    t_s[:E,:]=g*(td-jnp.sum(g*td,axis=0,keepdims=True))
    gl=t_s[...].T.astype(BF)
    dmoe=dot(gl,r_ref[...],1,1)+mg_ref[:T,:].astype(F32)
    res=res_ref[...]
    inv=lax.rsqrt(jnp.mean(res*res,axis=-1,keepdims=True)+norm_eps)
    gain=gain_row(misc_ref,gain_at)
    scaled=dmoe*gain
    grad_gain=jnp.sum(dmoe*res*inv,axis=0,keepdims=True)
    dres=cot_ref[...].astype(F32)+inv*scaled-res*(inv*inv*inv*jnp.mean(scaled*res,axis=-1,keepdims=True))
    dres_ref[...]=dres
    br=dres.astype(BF)
    dmix_ref[...]=dot(br,wo_ref[...],1,1).astype(BF)
    out_ref[:,:D]=dot(mix_ref[...],br,0,0).astype(BF)
    lane=lax.broadcasted_iota(jnp.int32,(D,128),1)
    column=jnp.broadcast_to(grad_gain,(128,D)).T
    out_ref[:,D:]=jnp.where(lane==E,column,dot(moe_ref[...],gl,0,0)).astype(BF)

def branch(gain_at,mg,res,moe_in,mixed,cot,w2,w1,mem_t):
    T,D=res.shape
    E=mem_t.shape[0]
    full=lambda i:(0,0)
    return pl.pallas_call(functools.partial(branch_kernel,gain_at),grid=(1,),
        in_specs=[pl.BlockSpec((T+E,D),full)]+[pl.BlockSpec((T,D),full)]*4+[pl.BlockSpec((D,D),full),pl.BlockSpec((D,128),lambda i:(0,D//128)),
                  pl.BlockSpec((D,128),lambda i:(0,MISC)),pl.BlockSpec((E,T),full)],
        out_specs=[pl.BlockSpec((T,D),full),pl.BlockSpec((T,D),full),pl.BlockSpec((D,D+128),full)],
        out_shape=[jax.ShapeDtypeStruct((T,D),F32),jax.ShapeDtypeStruct((T,D),BF),jax.ShapeDtypeStruct((D,D+128),BF)],
        scratch_shapes=[pltpu.VMEM((128,T),F32)],
        compiler_params=pltpu.CompilerParams(vmem_limit_bytes=60<<20),
        cost_estimate=COST,
        name="branch")(mg,res,moe_in,mixed,cot,w2,w2,w1,mem_t)

def fold(v):
    return v+pltpu.roll(v,2*HALF,1)

def attend_back_kernel(gain_at,pos_ref,h_ref,misc_ref,wq_ref,wk_ref,wv_ref,cos_ref,sin_ref,segc_ref,segr_ref,
                       q_ref,k_ref,v_ref,dm_ref,lse_ref,dres_ref,og_ref,
                       own_ref,other_ref,gin_ref,x_s,bias_s,da_s,out_s,sem):
    T,D=h_ref.shape
    step=pl.program_id(0)
    def put(column,value):
        out_s[:,pl.ds(column,value.shape[1])]=value
    @pl.when(step==0)
    def _():
        inputs=h_ref[...].astype(F32)
        inv=lax.rsqrt(jnp.mean(inputs*inputs,axis=-1,keepdims=True)+norm_eps)
        x_s[...]=(inputs*inv*gain_row(misc_ref,gain_at)).astype(BF)
        r=lax.broadcasted_iota(jnp.int32,(T,T),0); c=lax.broadcasted_iota(jnp.int32,(T,T),1)
        bias_s[...]=jnp.where((segc_ref[...]==segr_ref[...])&(r<=c),0.0,-1e30)
        wide=og_ref.shape[1]
        put(out_s.shape[1]-128-wide,og_ref[...])
    cos=cos_ref[...]; sin=sin_ref[...]
    kp=spread(k_ref[...].astype(F32)); vp=spread(v_ref[...].astype(F32))
    low=lax.broadcasted_iota(jnp.int32,(T,128),1)<2*HALF
    dq_all=[];dk_all=[];dv_all=[]
    for c in range(2):
        cols=slice(128*c,128*c+128)
        qs=(q_ref[:,cols].astype(F32)*0.125).astype(BF)
        dm=dm_ref[:,cols]
        dks=[];dvs=[];dq=[None]*(T//ROWS)
        for half in range(2):
            i=2*c+half
            dk=None;dv=None
            for b in reversed(range(T//ROWS)):
                rows=slice(b*ROWS,(b+1)*ROWS); nk=(b+1)*ROWS
                s=dot(kp[i][:nk],qs[rows],1,1)+bias_s[:nk,rows]
                p=jnp.exp(s-lse_ref[0,i:i+1,rows])
                dp=dot(vp[i][:nk],dm[rows],1,1)
                delta=jnp.sum(p*dp,axis=0,keepdims=True)
                ds=(p*(dp-delta)).astype(BF)
                part=dot(ds,kp[i][:nk],0,0)
                dq[b]=part if dq[b] is None else dq[b]+part
                pk=dot(ds,qs[rows]); pv=dot(p.astype(BF),dm[rows])
                if dk is None:
                    dk,dv=pk,pv
                else:
                    dk=jnp.concatenate([dk[:nk]+pk,dk[nk:]],axis=0)
                    dv=jnp.concatenate([dv[:nk]+pv,dv[nk:]],axis=0)
            dks.append(dk);dvs.append(dv)
        dql=jnp.concatenate(dq,axis=0)*0.125
        dq_all.append((dql*cos-rotate(dql)*sin).astype(BF))
        dk_all.append(fold(jnp.where(low,dks[0],dks[1])))
        dv_all.append(fold(jnp.where(low,dvs[0],dvs[1])))
    dkl=jnp.where(low,dk_all[0],dk_all[1])
    dkl=(dkl*cos-rotate(dkl)*sin).astype(BF)
    dvl=jnp.where(low,dv_all[0],dv_all[1]).astype(BF)
    dql=jnp.concatenate(dq_all,axis=1)
    x=x_s[...]
    base=pl.multiple_of(step*512,512)
    put(base,dot(x,dql,0,0).astype(BF))
    put(base+256,dot(x,dkl,0,0).astype(BF))
    put(base+384,dot(x,dvl,0,0).astype(BF))
    da=dot(dql,wq_ref[...],1,1)+dot(dkl,wk_ref[...],1,1)+dot(dvl,wv_ref[...],1,1)
    @pl.when(step==0)
    def _():
        da_s[...]=da
    @pl.when(step>0)
    def _():
        da_s[...]+=da
    @pl.when(step==pl.num_programs(0)-1)
    def _():
        inputs=h_ref[...].astype(F32)
        inv=lax.rsqrt(jnp.mean(inputs*inputs,axis=-1,keepdims=True)+norm_eps)
        dattn=da_s[...]
        scaled=dattn*gain_row(misc_ref,gain_at)
        grad_gain=jnp.sum(dattn*inputs*inv,axis=0,keepdims=True)
        gin_ref[...]=(dres_ref[...]+inv*scaled-inputs*(inv*inv*inv*jnp.mean(scaled*inputs,axis=-1,keepdims=True))).astype(BF)
        put(out_s.shape[1]-128,jnp.broadcast_to(grad_gain,(128,D)).T.astype(BF))
        n=pos_ref.shape[0]
        span=D//n
        def copy(j,ref,at):
            rows=pl.ds(pl.multiple_of(at*span,span),span)
            return pltpu.make_async_copy(out_s.at[j*span:(j+1)*span,:],ref.at[rows,:],sem.at[j])
        for go in (True,False):
            for j in range(n):
                for ref,first in ((own_ref,0),(other_ref,n//2)):
                    @pl.when((pos_ref[j]>=first)&(pos_ref[j]<first+n//2))
                    def _(j=j,ref=ref,first=first):
                        c=copy(j,ref,pos_ref[j]-first)
                        if go:
                            c.start()
                        else:
                            c.wait()

def attend_back(pos,gain_at,h,w,cos,sin,segc,segr,q,k,v,dmix,lse,dres,og):
    T,D=h.shape
    kvw=k.shape[1]
    steps=lse.shape[0]
    full=lambda g,_:(0,0)
    kb=D//128; vb=kb+kvw//128
    wide=og.shape[1]
    width=D+2*kvw+wide+128
    return pl.pallas_call(functools.partial(attend_back_kernel,gain_at),
        grid_spec=pltpu.PrefetchScalarGridSpec(num_scalar_prefetch=1,grid=(steps,),
        in_specs=[pl.BlockSpec((T,D),full),pl.BlockSpec((D,128),lambda g,_:(0,MISC)),
                  pl.BlockSpec((D,256),lambda g,_:(0,g)),pl.BlockSpec((D,128),lambda g,_:(0,kb+g)),pl.BlockSpec((D,128),lambda g,_:(0,vb+g)),
                  pl.BlockSpec((T,128),full),pl.BlockSpec((T,128),full),pl.BlockSpec((T,1),full),pl.BlockSpec((1,T),full),
                  pl.BlockSpec((T,256),lambda g,_:(0,g)),pl.BlockSpec((T,128),lambda g,_:(0,g)),pl.BlockSpec((T,128),lambda g,_:(0,g)),
                  pl.BlockSpec((T,256),lambda g,_:(0,g)),pl.BlockSpec((1,8,T),lambda g,_:(g,0,0)),pl.BlockSpec((T,D),full),pl.BlockSpec((D,wide),full)],
        out_specs=[pl.BlockSpec(memory_space=pl.ANY)]*2+[pl.BlockSpec((T,D),full)],
        scratch_shapes=[pltpu.VMEM((T,D),BF),pltpu.VMEM((T,T),F32),pltpu.VMEM((T,D),F32),pltpu.VMEM((D,width),BF),pltpu.SemaphoreType.DMA((pos.shape[0],))]),
        out_shape=[jax.ShapeDtypeStruct((D//2,width),BF)]*2+[jax.ShapeDtypeStruct((T,D),BF)],
        compiler_params=pltpu.CompilerParams(vmem_limit_bytes=60<<20),
        cost_estimate=COST,
        name="attend_back")(pos,h,w,w,w,w,cos,sin,segc,segr,q,k,v,dmix,lse,dres,og)

def rope_tables(segment_row):
    index = jnp.arange(segment_row.shape[0], dtype=jnp.int32)
    earlier = (segment_row[:, None] == segment_row[None, :]) & (index[None, :] < index[:, None])
    position = jnp.sum(earlier.astype(jnp.int32), axis=-1).astype(F32)
    frequency = rope_base ** (-jnp.arange(HALF, dtype=F32) / HALF)
    angles = position[:, None] * frequency[None, :]
    cosine = jnp.cos(angles)
    sine = jnp.sin(angles)
    return (
        jnp.concatenate([cosine] * 4, axis=1),
        jnp.concatenate([-sine, sine, -sine, sine], axis=1),
    )


def pad_columns(values):
    return jnp.pad(values, ((0, 0), (0, -values.shape[1] % 128)))


def body(
    hidden,
    segment_ids,
    routes,
    norm_attn,
    w_query,
    key_weight,
    value_weight,
    w_out,
    norm_moe,
    w_router,
    w_gate,
    w_up,
    w_down,
    cotangent,
):
    tokens, width = hidden.shape
    own_rows = w_query.shape[0]
    owned = w_gate.shape[0]
    peers = lax.axis_size("expert")
    me = lax.axis_index("expert")
    chips = peers // 2
    chip_order = (me // 2 - jnp.arange(chips, dtype=jnp.int32)) % chips
    core_order = (me % 2) ^ jnp.arange(2, dtype=jnp.int32)
    order = (chip_order[:, None] * 2 + core_order[None, :]).reshape(-1)
    slot_of = jnp.argsort(order.reshape(chips, 2).T.reshape(-1))
    dp_count = lax.axis_size("dp")
    dp_order = lax.axis_index("dp") ^ jnp.arange(dp_count, dtype=jnp.int32)
    places = (
        (chip_order[None, None, :] * 2 + core_order[None, :, None]) * dp_count
        + dp_order[:, None, None]
    ).reshape(-1)
    first_pack = pad_columns(
        jnp.concatenate(
            [
                w_query,
                key_weight,
                value_weight,
                norm_attn[:, None],
                norm_moe[:, None],
            ],
            axis=1,
        )
    )
    second_pack = pad_columns(jnp.concatenate([w_out, w_router], axis=1))
    cotangent_steps = [cotangent]
    routes_shifts = all_shifts(routes.astype(BF).reshape(-1, 128))
    both_shifts = all_shifts(own_slice(jnp.concatenate([first_pack, second_pack], axis=1)))
    both_shifts, routes_shifts, cotangent_steps = tie(both_shifts, routes_shifts, cotangent_steps)
    stacks = jnp.stack(both_shifts)
    first_width = first_pack.shape[1]
    stack_one = stacks[:, :, :first_width]
    stack_two = stacks[:, :, first_width:]
    slices_one = [stack_one] + [swap_dp(stack_one, r) for r in range(1, dp_count)]
    cotangent_steps.append(shift_chips(cotangent_steps[0], 1))
    last_step = [shift_chips(cotangent_steps[0], chips - 1)] if chips > 2 else []
    routes_all = []
    for s in routes_shifts:
        routes_all += [s, swap_pair(s)]
    routes_all = jnp.stack(routes_all).astype(jnp.int32).reshape(peers, tokens, TOP)
    expert_ids = jnp.arange(EXPERTS, dtype=jnp.int32)
    member_all = jnp.any(routes_all[:, None, :, :] == expert_ids[:, None, None], axis=3)
    first_expert = me * owned
    member_own = lax.dynamic_slice_in_dim(member_all, first_expert, owned, 1)
    index = jnp.arange(tokens, dtype=jnp.int32)
    before = (index[:, None] < index[None, :]).astype(BF)
    rank = jnp.einsum(
        "sjt,tu->sju", member_own.astype(BF), before, preferred_element_type=F32
    ).astype(jnp.int32)
    rank = jnp.where(member_own, rank, -1)
    first_slot = jnp.arange(owned, dtype=jnp.int32)[:, None] * CAP
    keys = jnp.swapaxes(jnp.where(member_own, rank + first_slot, -1), 1, 2)
    rank_rows = jnp.swapaxes(rank, 0, 1)[:, :, None, :]
    member_all = member_all.astype(F32)
    member_line = jnp.any(routes[None, :, :] == expert_ids[:, None, None], axis=2).astype(F32)
    segment_row = segment_ids[0]
    cosine, sine = rope_tables(segment_row)
    segment_column = segment_row[:, None]
    segment_line = segment_row[None, :]
    tables = [rank_rows, keys, member_all, member_line, cosine, sine, slot_of]
    tables, slices_one, stack_two = tie(tables, slices_one, stack_two)
    rank_rows, keys, member_all, member_line, cosine, sine, slot_of = tables
    pieces_one = []
    for s in slices_one:
        pieces_one += [s, swap_pair(s)]
    pieces_one, stack_two, cotangent_steps = tie(pieces_one, stack_two, cotangent_steps)
    for k in range(2, chips - 1):
        cotangent_steps.append(shift_chips(cotangent_steps[k - 1], 1))
    attn_weights = assemble(places, pieces_one)
    attn_weights, stack_two, last_step = tie(attn_weights, stack_two, last_step)
    cotangent_steps += last_step
    slices_two = [stack_two] + [swap_dp(stack_two, r) for r in range(1, dp_count)]
    kv_heads = key_weight.shape[1] // (2 * HALF)
    query, key, value, mixed, lse = attend(
        0, hidden, attn_weights, cosine, sine, segment_column, segment_line, kv_heads
    )
    mixed, slices_two, cotangent_steps = tie(mixed, slices_two, cotangent_steps)
    pieces_two = []
    for s in slices_two:
        pieces_two += [s, swap_pair(s)]
    d_pairs = [swap_pair(c) for c in cotangent_steps[:2]]
    mixed, pieces_two, d_pairs = tie(mixed, pieces_two, d_pairs)
    out_weights = assemble(places, pieces_two)
    residual, moe_in = project(1, mixed, out_weights, hidden, attn_weights)
    x = [moe_in, swap_pair(moe_in)]
    x, moe_in = tie(x, moe_in)
    kept = None
    grad_parts = []
    out_parts = []
    hop = None

    def sum_of(*terms):
        total = terms[0].astype(F32)
        for t in terms[1:]:
            total = total + t.astype(F32)
        return total.astype(BF)

    for k in range(chips):
        following = shift_chips(x[0], 1) if k + 1 < chips else None
        later = swap_pair(cotangent_steps[k + 2]) if k + 2 < chips else None
        if k == 3:
            hop = shift_chips(sum_of(*grad_parts[1]), 1)
        outs = list(
            expert_step(
                k,
                first_expert[None],
                x,
                (cotangent_steps[k], d_pairs[k]),
                out_weights,
                member_all,
                rank_rows,
                keys,
                w_gate,
                w_up,
                w_down,
                kept,
            )
        )
        kept = outs[4:]
        outs = outs[:4]
        outs, kept, following, hop, later, grad_parts, out_parts = tie(
            outs, kept, following, hop, later, grad_parts, out_parts
        )
        d_pairs.append(later)
        if following is not None:
            x = [following, swap_pair(following)]
        grad_parts = grad_parts + [(outs[0], swap_pair(outs[1]))]
        out_parts = out_parts + [(outs[2], outs[3])]
    dp_me = lax.axis_index("dp")
    low = dp_me % 2
    high = dp_me // 2
    count = (owned + 1) // 2
    plans = [(0, count, 1, 2, low, high)]
    if owned > count:
        plans.append((count, owned - count, 2, 1, high, low))
    first_hop = 2 if hop is None else 3
    total = sum_of(*grad_parts[first_hop - 1], *([] if hop is None else [hop]))
    total, kept = tie(total, kept)
    moved = shift_chips(total, 1)
    halves = []
    sends = []
    for first_of, many, one, two, bit_one, bit_two in plans:
        send, keep = weight_grads(bit_one[None], first_of, many, kept)
        halves.append((first_of, one, two, bit_one, bit_two, keep))
        sends.append(send)
    moved, sends = tie(moved, sends)
    if first_hop < chips:
        total, sends = tie(sum_of(*grad_parts[first_hop], moved), sends)
        moved = shift_chips(total, 1)
    gots = [swap_dp(send, h[1]) for h, send in zip(halves, sends)]
    for k in range(first_hop + 1, chips):
        moved = shift_chips(sum_of(*grad_parts[k], moved), 1)
    moe_grad = sum_of(*grad_parts[0], moved)
    out_sum = (out_parts[1][0].astype(F32) + swap_pair(out_parts[1][1]).astype(F32)).astype(BF)
    moe_grad, out_sum = tie(moe_grad, out_sum)
    grad_residual, mixed_gradient, out_grads = branch(
        1, moe_grad, residual, moe_in, mixed, cotangent, out_weights, attn_weights, member_line
    )
    out_sum = shift_chips(out_sum, 1)
    own_half, other_half, grad_input = attend_back(
        slot_of,
        0,
        hidden,
        attn_weights,
        cosine,
        sine,
        segment_column,
        segment_line,
        query,
        key,
        value,
        mixed_gradient,
        lse,
        grad_residual,
        out_grads,
    )
    own_half, other_half, out_sum, gots, out_parts = tie(
        own_half, other_half, out_sum, gots, out_parts
    )

    seconds = []
    keeps = []
    for (first_of, one, two, bit_one, bit_two, keep), got in zip(halves, gots):
        send, keep = halve(bit_two[None], keep, got)
        seconds.append(send)
        keeps.append(keep)
    parts = [own_half, swap_pair(other_half)]
    seconds, keeps, parts, out_parts = tie(seconds, keeps, parts, out_parts)
    parts = [
        (
            parts[0][k * own_rows : (k + 1) * own_rows].astype(F32)
            + parts[1][k * own_rows : (k + 1) * own_rows].astype(F32)
        ).astype(BF)
        for k in range(chips)
    ]
    gots = [swap_dp(send, h[2]) for h, send in zip(halves, seconds)]
    running = shift_chips(parts[1], 1)
    out_parts = [(a.astype(F32) + swap_pair(b).astype(F32)).astype(BF) for a, b in out_parts]
    gots, running, out_parts = tie(gots, running, out_parts)
    mine = [(k.astype(F32) + g.astype(F32)).astype(BF) for k, g in zip(keeps, gots)]
    running = (parts[2].astype(F32) + running.astype(F32)).astype(BF)
    mine, running, out_sum = tie(mine, running, out_sum)
    others = [swap_dp(m, h[2]) for h, m in zip(halves, mine)]
    running = shift_chips(running, 1)
    others, running, mine = tie(others, running, mine)
    thirds = [swap_dp(m, h[1]) for h, m in zip(halves, mine)]
    for k in [*range(3, chips), 0]:
        running = (parts[k].astype(F32) + running.astype(F32)).astype(BF)
        if k:
            running = shift_chips(running, 1)
    part, others, mine, out_sum = tie(running, others, mine, out_sum)
    sub = own_rows // dp_count

    def rows_of(r):
        return (dp_me ^ r) * sub

    sent = [lax.dynamic_slice_in_dim(part, rows_of(r), sub, 0) for r in range(dp_count)]
    received = [sent[0]] + [swap_dp(sent[r], r) for r in range(1, dp_count)]
    if chips > 2:
        out_sum = shift_chips((out_parts[2].astype(F32) + out_sum.astype(F32)).astype(BF), 1)
    received, thirds, others = tie(received, thirds, others)
    fourths = [swap_dp(o, h[1]) for h, o in zip(halves, others)]
    total = received[0].astype(F32)
    for piece in received[1:]:
        total = total + piece.astype(F32)
    total = total.astype(BF)
    pieces = [swap_dp(total, r) if r else total for r in range(dp_count)]
    for o in out_parts[3:]:
        out_sum = shift_chips((o.astype(F32) + out_sum.astype(F32)).astype(BF), 1)
    result = (residual + out_parts[0].astype(F32) + out_sum.astype(F32)).astype(BF)
    bits = jnp.stack([jnp.stack(h[3:5]) for h in halves for _ in range(h[5].shape[0])])
    big = place(bits, list(zip(mine, others, thirds)))
    big, fourths, result = tie(big, fourths, result)
    big = place(bits, [(f,) for f in fourths], big)
    big, pieces = tie(big, pieces)
    share = place_share(
        jnp.stack([rows_of(r) for r in range(dp_count)]), pieces, width, key_weight.shape[1]
    )
    return (
        result,
        grad_input,
        share[6][0],
        share[0],
        share[1],
        share[2],
        share[3],
        share[5][0],
        share[4],
        big[0],
        big[1],
        big[2],
    )


def solution(mesh):
    in_specs = (
        P(("dp", "expert"), None),
        P(("dp", "expert"), None),
        P(("dp", "expert"), None),
        P("expert"),
        P("expert", None),
        P("expert", None),
        P("expert", None),
        P("expert", None),
        P("expert"),
        P("expert", None),
        P("expert", None, None),
        P("expert", None, None),
        P("expert", None, None),
        P(("dp", "expert"), None),
    )
    out_specs = (
        P(("dp", "expert"), None),
        P(("dp", "expert"), None),
        P("expert"),
        P("expert", None),
        P("expert", None),
        P("expert", None),
        P("expert", None),
        P("expert"),
        P("expert", None),
        P("expert", None, None),
        P("expert", None, None),
        P("expert", None, None),
    )
    return jax.shard_map(body, mesh=mesh, in_specs=in_specs, out_specs=out_specs, check_vma=False)
```
